128 devices in a mesh: seq: 16 (over z, x), head: 8 (over y, core).
Axes of the slice: x: 4, y: 4, z: 4, core: 2. Of those that a mesh axis runs over, the one named last changes fastest.
Arguments:
- hidden_in: bfloat16 [65536, 1024], P('seq'), may hold values from -6 to 6
- norm_gain: bfloat16 [1024], replicated, may hold values from 0.099609375 to 1.8984375
- gate_weight: bfloat16 [1024, 2048], P(None, 'head'), may hold values from -0.1875 to 0.1875
- value_weight: bfloat16 [1024, 2048], P(None, 'head'), may hold values from -0.375 to 0.375
- state_weight: bfloat16 [1024, 256], replicated, may hold values from -0.1875 to 0.1875
- step_weight: bfloat16 [1024, 32], P(None, 'head'), may hold values from -0.1875 to 0.1875
- step_bias: float32 [32], P('head'), may hold values from -1 to 1
- decay_log: float32 [32], P('head'), may hold values from -16 to -3
- skip_gain: float32 [32], P('head'), may hold values from 0.5 to 1.5
- conv_value: bfloat16 [4, 2048], P(None, 'head'), may hold values from -3 to 3
- conv_state: bfloat16 [4, 256], replicated, may hold values from -3 to 3
- output_gain: bfloat16 [2048], P('head'), may hold values from 0.099609375 to 1.8984375
- output_weight: bfloat16 [2048, 1024], P('head'), may hold values from -0.125 to 0.125
- piece_lengths: int32 [16], replicated, may hold values from 1 to 32768, 65536 in all
Outputs:
- block_out: bfloat16 [65536, 1024], P(('seq', 'head'))
The draws below stay inside these ranges and needn't reach their ends.
Inputs may be any that keep to these rules, and one draw needn't show every extreme that they name: `piece_lengths`: the lengths sum to 65536; the pieces lie end to end from position 0.
All inputs are finite; a program needn't handle non-finite values.
Results may differ from the reference program's by a relative error of at most 0.018.
Values may be sent and summed in bfloat16 or wider, within the bound.
A program may use at most 128 MiB of HBM per device.

```python
import math
import jax
import jax.numpy as jnp
import numpy as np
from jax import lax

D = 1024
HEADS = 32
HEAD_DIM = 64
STATE = 128
CONV = 4
BLOCK = 256
PIECES = 16
INNER = 2048
TOKENS = 65536


def draw_decay_log(key, part):
    slow_key = jax.random.fold_in(key, 11)
    fast_key = jax.random.fold_in(key, 12)
    pick_key = jax.random.fold_in(key, 13)
    slow_rates = jax.random.uniform(slow_key, (HEADS,), jnp.float32, math.log(0.2), math.log(1.5)) - math.log(TOKENS)
    fast_rates = jax.random.uniform(fast_key, (HEADS,), jnp.float32, math.log(0.02), math.log(0.04))
    fast_share = 0.5
    picked = jax.random.uniform(pick_key, (HEADS,), jnp.float32) < fast_share
    return jnp.where(picked, fast_rates, slow_rates).astype(jnp.float32)


def draw_value_weight(key, part):
    noise = jax.random.truncated_normal(key, -4.0, 4.0, (D, INNER), jnp.float32) / math.sqrt(D)
    column_ramp = 1.0 + jnp.arange(INNER, dtype=jnp.float32) / (INNER - 1)
    return (noise * column_ramp[None, :]).astype(jnp.bfloat16)


def block_levels(own_key, dims, split, smallest, largest):
    level, own = 1.0, jax.random.fold_in(own_key, 6)
    for axis_at, shards_of in split:
        steps = jnp.exp(jax.random.uniform(jax.random.fold_in(own, axis_at), (shards_of,), jnp.float32, smallest / len(split), largest / len(split)))
        level = level * jnp.repeat(steps, dims[axis_at] // shards_of).reshape([-1 if axis == axis_at else 1 for axis in range(len(dims))])
    return level


def profile(number_of, total, bound, slope):
    weights = [(1 << 20) // math.isqrt(grade ** slope) + 1 for grade in range(2, number_of + 1)]
    surplus, holding = total - bound - (number_of - 1), [1] * (number_of - 1)
    while surplus > 0:
        free = [i for i in range(number_of - 1) if holding[i] < bound]
        mass, remaining = sum([weights[i] for i in free]), surplus
        for i in free:
            more = min(bound - holding[i], max(1, remaining * weights[i] // mass), surplus)
            holding[i] = holding[i] + more
            surplus = surplus - more
    return np.array([bound] + holding)


def ragged(stream_key, number_of, total, bound, skew):
    if number_of == 2:
        one = jax.random.randint(stream_key, (), max(1, total - bound), min(bound, total - 1) + 1)
        return jnp.stack([one, total - one])
    tallies = jnp.asarray(profile(number_of, total, bound, skew), jnp.int32)
    couples = (number_of - 1) // 2
    giver, sink = tallies[1:1 + 2 * couples:2], tallies[2:2 + 2 * couples:2]
    slack = jnp.minimum(giver - 1, bound - sink)
    shifted = jax.random.randint(jax.random.fold_in(stream_key, 1), (couples,), 0, 1 << 20) % (slack + 1)
    tallies = tallies.at[1:1 + 2 * couples:2].set(giver - shifted).at[2:2 + 2 * couples:2].set(sink + shifted)
    return tallies[jax.random.permutation(jax.random.fold_in(stream_key, 2), number_of)]


def gaussian(stream_key, dims, scale, bound, pieces=(), kind=jnp.bfloat16):
    level = block_levels(stream_key, dims, pieces, -0.22, 0.18) if pieces else 1.0
    drawn = jax.random.normal(stream_key, dims, jnp.float32) * scale * level
    return jnp.minimum(jnp.maximum(drawn, -bound), bound).astype(kind)


def setup_inputs(seed: int = 0) -> dict:
    keys = jax.random.split(jax.random.key(seed), 15)
    return {
        "hidden_in": gaussian(keys[0], (TOKENS, D), 1.0, 6.0, ((0, 16),)),
        "norm_gain": jnp.clip(1.0 + 0.18 * jax.random.normal(keys[1], (D,), jnp.float32), 0.099609375, 1.8984375).astype(jnp.bfloat16),
        "gate_weight": gaussian(keys[2], (D, INNER), D ** -0.5, 0.1875, ((1, 8),)),
        "value_weight": draw_value_weight(jax.random.fold_in(keys[14], 71), 0),
        "state_weight": gaussian(keys[4], (D, 2 * STATE), D ** -0.5, 0.1875),
        "step_weight": gaussian(keys[5], (D, HEADS), D ** -0.5, 0.1875, ((1, 8),)),
        "step_bias": jnp.clip(jax.random.uniform(keys[6], (HEADS,), jnp.float32, -1.0, 1.0) * block_levels(keys[6], (HEADS,), ((0, 8),), -0.4, 0.0), -1.0, 1.0),
        "decay_log": draw_decay_log(jax.random.fold_in(keys[14], 71), 0),
        "skip_gain": jnp.clip(0.5 + 1.0 * jax.random.uniform(keys[8], (HEADS,), jnp.float32) ** block_levels(keys[8], (HEADS,), ((0, 8),), -0.2, 0.2), 0.5, 1.5),
        "conv_value": gaussian(keys[9], (CONV, INNER), CONV ** -0.5, 3.0, ((1, 8),)),
        "conv_state": gaussian(keys[10], (CONV, 2 * STATE), CONV ** -0.5, 3.0),
        "output_gain": jnp.clip(1.0 + 0.18 * jax.random.normal(keys[11], (INNER,), jnp.float32), 0.099609375, 1.8984375).astype(jnp.bfloat16),
        "output_weight": gaussian(keys[12], (INNER, D), INNER ** -0.5, 0.125, ((0, 8),)),
        "piece_lengths": ragged(keys[13], PIECES, TOKENS, TOKENS // 2, 2).astype(jnp.int32),
    }


exact_mode = lax.Precision.HIGHEST
epsilon = 1e-05

def rms_scale(values):
    return lax.rsqrt(lax.optimization_barrier(jnp.mean(values * values, axis=-1, keepdims=True)) + epsilon)

def piece_index(positions, piece_lengths):
    starts = jnp.cumsum(piece_lengths).astype(jnp.int32) - piece_lengths
    counted = lax.optimization_barrier(jnp.sum((starts[None, :] <= positions[:, None]).astype(jnp.int32), axis=1)).astype(jnp.int32)
    return counted - 1

def convolve(padded, padded_ids, kernel, length, reverse):
    tap_count = kernel.shape[0]
    centre_ids = padded_ids[tap_count - 1:tap_count - 1 + length]
    running = jnp.zeros((length, padded.shape[1]), jnp.float32)
    for offset in range(tap_count):
        start_row = 2 * (tap_count - 1) - offset if reverse else offset
        window = padded[start_row:start_row + length].astype(jnp.float32)
        same_piece = (padded_ids[start_row:start_row + length] == centre_ids)[:, None]
        running = running + jnp.where(same_piece, window * kernel[offset].astype(jnp.float32)[None, :], 0.0)
    return jax.nn.silu(running).astype(jnp.bfloat16)

def scan_direction(values, write_rows, read_rows, step_sizes, piece_ids, decay_log, skip_gain):
    length = values.shape[0]
    blocks = length // BLOCK
    head_total = step_sizes.shape[1]
    decay_rate = -jnp.exp(decay_log)
    row_iota = lax.broadcasted_iota(jnp.int32, (BLOCK, BLOCK), 0)
    col_iota = lax.broadcasted_iota(jnp.int32, (BLOCK, BLOCK), 1)
    lower_mask = row_iota >= col_iota

    def advance(carry, block_in):
        carried_state, prior_piece = carry
        block_values, block_write, block_read, block_steps, block_ids = block_in
        log_steps = block_steps * decay_rate[None, :]
        cumulative = jnp.cumsum(log_steps, axis=0)
        same_piece = lower_mask & (block_ids[:, None] == block_ids[None, :])
        log_gap = cumulative[:, None, :] - cumulative[None, :, :]
        decay_table = jnp.where(same_piece[:, :, None], jnp.exp(jnp.minimum(log_gap, 0.0)), 0.0)
        intersection = jnp.dot(block_read, block_write.T, preferred_element_type=jnp.float32)
        weight = (intersection[:, :, None] * decay_table * block_steps[None, :, :]).astype(jnp.bfloat16)
        values_wide = block_values.astype(jnp.float32).reshape(BLOCK, head_total, HEAD_DIM)
        local_mix = jnp.einsum('ijh,jhp->ihp', weight.astype(jnp.float32), values_wide)
        opening = jnp.where((block_ids == prior_piece)[:, None], jnp.exp(cumulative), 0.0)
        from_state = jnp.einsum('in,hpn->ihp', block_read.astype(jnp.float32), carried_state, precision=exact_mode)
        result = local_mix + from_state * opening[:, :, None] + skip_gain[None, :, None] * values_wide
        tail_weight = jnp.where((block_ids == block_ids[-1])[:, None], jnp.exp(cumulative[-1][None, :] - cumulative), 0.0) * block_steps
        fresh_state = jnp.einsum('jhp,jn->hpn', values_wide * tail_weight[:, :, None], block_write.astype(jnp.float32), precision=exact_mode)
        passing = jnp.where(block_ids[-1] == prior_piece, jnp.exp(cumulative[-1]), 0.0)
        next_state = passing[:, None, None] * carried_state + fresh_state
        return ((next_state, block_ids[-1]), result.reshape(BLOCK, head_total * HEAD_DIM).astype(jnp.bfloat16))
    initial = (jnp.zeros((head_total, HEAD_DIM, STATE), jnp.float32), jnp.array(-1, jnp.int32))
    blocks_in = (values.reshape(blocks, BLOCK, -1), write_rows.reshape(blocks, BLOCK, STATE), read_rows.reshape(blocks, BLOCK, STATE), step_sizes.reshape(blocks, BLOCK, head_total), piece_ids.reshape(blocks, BLOCK))
    final_carry, outputs = lax.scan(advance, initial, blocks_in)
    return outputs.reshape(length, -1)

def reference(hidden_in, norm_gain, gate_weight, value_weight, state_weight, step_weight, step_bias, decay_log, skip_gain, conv_value, conv_state, output_gain, output_weight, piece_lengths):
    wide_in = hidden_in.astype(jnp.float32)
    normed = (wide_in * rms_scale(wide_in) * norm_gain.astype(jnp.float32)[None, :]).astype(jnp.bfloat16)
    gate_rows = jnp.dot(normed, gate_weight, preferred_element_type=jnp.float32).astype(jnp.bfloat16)
    mixing_input = jnp.concatenate([jnp.dot(normed, value_weight, preferred_element_type=jnp.float32), jnp.dot(normed, state_weight, preferred_element_type=jnp.float32)], axis=1).astype(jnp.bfloat16)
    step_sizes = jax.nn.softplus(jnp.dot(normed, step_weight, preferred_element_type=jnp.float32) + step_bias[None, :])
    length = hidden_in.shape[0]
    positions = jnp.arange(length, dtype=jnp.int32)
    piece_ids = piece_index(positions, piece_lengths)
    kernel = jnp.concatenate([conv_value, conv_state], axis=1)
    margin = CONV - 1
    padded = jnp.pad(mixing_input, ((margin, margin), (0, 0)))
    padded_ids = jnp.pad(piece_ids, (margin, margin), constant_values=-2)
    forward_in = convolve(padded, padded_ids, kernel, length, False)
    backward_in = convolve(padded, padded_ids, kernel, length, True)
    inner_total = value_weight.shape[1]
    forward_out = scan_direction(forward_in[:, :inner_total], forward_in[:, inner_total:inner_total + STATE], forward_in[:, inner_total + STATE:], step_sizes, piece_ids, decay_log, skip_gain)
    flipped = jnp.flip(backward_in, 0)
    backward_out = jnp.flip(scan_direction(flipped[:, :inner_total], flipped[:, inner_total:inner_total + STATE], flipped[:, inner_total + STATE:], jnp.flip(step_sizes, 0), jnp.flip(piece_ids, 0), decay_log, skip_gain), 0)
    gate_wide = jax.nn.silu(gate_rows.astype(jnp.float32))
    gated_forward = forward_out.astype(jnp.float32) * gate_wide
    gated_backward = backward_out.astype(jnp.float32) * gate_wide
    combined = ((gated_forward * rms_scale(gated_forward) + gated_backward * rms_scale(gated_backward)) * output_gain.astype(jnp.float32)[None, :]).astype(jnp.bfloat16)
    return (wide_in + jnp.dot(combined, output_weight, preferred_element_type=jnp.float32)).astype(jnp.bfloat16)
```

```python
import functools
import math

import jax
import jax.numpy as jnp
from jax import lax
from jax.experimental import pallas as pl
from jax.experimental.pallas import tpu as pltpu
from jax.sharding import PartitionSpec as P

HEAD_DIM = 64
STATE = 128
CONV = 4
CHUNK = 128
PIECES = 16
HALO = 8
RESET = 256.0
LOG2E = math.log2(math.e)

f32 = jnp.float32
bf16 = jnp.bfloat16
epsilon = 1e-05
MESH = pl.DeviceIdType.MESH
NN = (((1,), (0,)), ((), ()))
NT = (((1,), (1,)), ((), ()))
TN = (((0,), (0,)), ((), ()))


def mm(a, b, dims=NN, precision=None):
    return lax.dot_general(a, b, dims, precision=precision, preferred_element_type=f32)


def silu(x):
    half = 0.5 * x
    return half * jnp.tanh(half) + half


def normalized(h, gain):
    wide = h.astype(f32)
    scale = lax.rsqrt(jnp.mean(wide * wide, axis=1, keepdims=True) + epsilon)
    return (wide * scale * gain.astype(f32)).astype(bf16)


def whole(shape):
    zeros = (0,) * len(shape)
    return pl.BlockSpec(shape, lambda *_: zeros)


SMEM_SPEC = pl.BlockSpec(memory_space=pltpu.SMEM)
ANY_SPEC = pl.BlockSpec(memory_space=pl.ANY)


def params(**kw):
    return pltpu.CompilerParams(vmem_limit_bytes=60 * 1024 * 1024, **kw)


def project_kernel(h_ref, gain_ref, gw_ref, vw_ref, sw_ref, tw_ref, gate_ref, mix_ref, raw_ref):
    inner = vw_ref.shape[1]
    n = normalized(h_ref[...], gain_ref[...])
    gate_ref[...] = mm(n, gw_ref[...]).astype(bf16)
    mix_ref[:, :inner] = mm(n, vw_ref[...]).astype(bf16)
    mix_ref[:, inner:] = mm(n, sw_ref[...]).astype(bf16)
    raw = mm(tw_ref[...], n, NT)
    for q in range(raw.shape[1] // CHUNK):
        raw_ref[q] = raw[:, q * CHUNK : (q + 1) * CHUNK]


def project(hidden, gain, gw, vw, sw, tw):
    tokens, width = hidden.shape
    inner = vw.shape[1]
    mixed = inner + sw.shape[1]
    rows = 512
    return pl.pallas_call(
        project_kernel,
        grid=(tokens // rows,),
        in_specs=[
            pl.BlockSpec((rows, width), lambda i: (i, 0)),
            whole(gain.shape),
            whole(gw.shape),
            whole(vw.shape),
            whole(sw.shape),
            whole(tw.shape),
        ],
        out_specs=[
            pl.BlockSpec((rows, inner), lambda i: (i, 0)),
            pl.BlockSpec((rows, mixed), lambda i: (i, 0)),
            pl.BlockSpec((rows // CHUNK, 8, CHUNK), lambda i: (i, 0, 0)),
        ],
        out_shape=[
            jax.ShapeDtypeStruct((tokens, inner), bf16),
            jax.ShapeDtypeStruct((tokens, mixed), bf16),
            jax.ShapeDtypeStruct((tokens // CHUNK, 8, CHUNK), f32),
        ],
        compiler_params=params(),
        cost_estimate=pl.CostEstimate(
            flops=2 * tokens * width * 1024, bytes_accessed=20 << 20, transcendentals=0
        ),
        name="project",
    )(hidden, gain, gw, vw, sw, tw)


def head_lanes(columns):
    low = lax.broadcasted_iota(jnp.int32, (columns[0].shape[0], 2 * HEAD_DIM), 1) < HEAD_DIM
    pairs = [
        jnp.where(low, columns[2 * p], columns[2 * p + 1]) for p in range(len(columns) // 2)
    ]
    return jnp.concatenate(pairs, axis=1)


def decays(first_row, raw, lens_ref, bias_ref, rate_ref):
    chunks = raw.shape[0]
    shape = (chunks, 8, CHUNK)
    sub = lax.broadcasted_iota(jnp.int32, shape, 1)
    upper = sub < 4
    head = jnp.where(upper, sub, sub - 4)
    pos = (
        first_row
        + lax.broadcasted_iota(jnp.int32, shape, 0) * CHUNK
        + lax.broadcasted_iota(jnp.int32, shape, 2)
    )
    start = jnp.zeros(shape, jnp.int32)
    stop = jnp.full(shape, 1 << 30, jnp.int32)
    edge = jnp.int32(0)
    for k in range(PIECES):
        start = jnp.where(pos >= edge, edge, start)
        edge = edge + lens_ref[k]
        stop = jnp.minimum(stop, jnp.where(edge > pos, edge, 1 << 30))
    since = pos - start
    until = stop - 1 - pos
    bias = jnp.zeros(shape, f32)
    rate = jnp.zeros(shape, f32)
    for h in range(4):
        bias = jnp.where(head == h, bias_ref[h], bias)
        rate = jnp.where(head == h, rate_ref[h], rate)
    rate = jnp.exp(rate) * (-LOG2E)
    z = raw + bias
    step = jnp.maximum(z, 0.0) + jnp.log1p(jnp.exp(-jnp.abs(z)))
    log = step * rate
    reset = jnp.where(since == 0, -RESET, 0.0)
    ones = (
        lax.broadcasted_iota(jnp.int32, (CHUNK, CHUNK), 0)
        <= lax.broadcasted_iota(jnp.int32, (CHUNK, CHUNK), 1)
    ).astype(f32)
    cum = mm(
        (log + reset).reshape(chunks * 8, CHUNK), ones, precision=lax.Precision.HIGHEST
    ).reshape(shape)
    excl = cum - log
    total = cum[:, :, CHUNK - 1 :]
    log_step = jnp.log2(step)
    row = jnp.where(upper, cum - log_step, excl + log_step)
    g1 = jnp.where(upper, cum, excl)
    g2 = jnp.where(upper, jnp.exp2(cum), jnp.exp2(total - cum) * step)
    g3 = jnp.where(upper, jnp.exp2(total - excl), jnp.exp2(excl) * step)
    g4 = jnp.where(upper, since, until).astype(f32)
    return row, g1, g2, g3, g4


def states_kernel(
    axis,
    mix_ref,
    before_ref,
    after_ref,
    halo_ref,
    gain_ref,
    vw_ref,
    sw_ref,
    raw_ref,
    lens_ref,
    bias_ref,
    rate_ref,
    cv_ref,
    cs_ref,
    conv_ref,
    fresh_ref,
    cols_ref,
    row_ref,
    end_ref,
    total_ref,
    ext,
    halo,
    run,
    reach,
):
    c = pl.program_id(0)
    count = pl.num_programs(0)
    inner = vw_ref.shape[1]
    mixed = mix_ref.shape[1]

    @pl.when(c == 0)
    def _():
        n = normalized(halo_ref[...], gain_ref[...])
        halo[:, :inner] = mm(n, vw_ref[...]).astype(bf16).astype(f32)
        halo[:, inner:] = mm(n, sw_ref[...]).astype(bf16).astype(f32)
        first_row = lax.axis_index(axis) * (count * CHUNK)
        row, g1, g2, g3, g4 = decays(first_row, raw_ref[...], lens_ref, bias_ref, rate_ref)
        row_ref[...] = row
        cols_ref[:, 0:8, :] = g1
        cols_ref[:, 8:16, :] = g2
        cols_ref[:, 16:24, :] = g3
        cols_ref[:, 24:32, :] = g4
        run[...] = jnp.zeros_like(run)
        reach[...] = jnp.zeros_like(reach)

    ext[HALO : HALO + CHUNK, :] = mix_ref[...].astype(f32)

    @pl.when(c == 0)
    def _():
        ext[0:HALO, :] = halo[0:HALO, :]

    @pl.when(c > 0)
    def _():
        ext[0:HALO, :] = before_ref[...].astype(f32)[HALO:, :]

    @pl.when(c == count - 1)
    def _():
        ext[HALO + CHUNK :, :] = halo[HALO:, :]

    @pl.when(c < count - 1)
    def _():
        ext[HALO + CHUNK :, :] = after_ref[...].astype(f32)[:HALO, :]

    cols = cols_ref[c]
    turned = jnp.concatenate([cols, jnp.zeros((CHUNK - 32, CHUNK), f32)], axis=0).T
    width = 128
    since = jnp.broadcast_to(turned[:, 24:25], (CHUNK, width))
    until = jnp.broadcast_to(turned[:, 28:29], (CHUNK, width))
    taps = jnp.concatenate([cv_ref[...], cs_ref[...]], axis=1).astype(f32)
    for reverse in (False, True):
        left = until if reverse else since
        for block in range(mixed // width):
            lanes = slice(block * width, (block + 1) * width)
            total = ext[HALO : HALO + CHUNK, lanes] * taps[CONV - 1 : CONV, lanes]
            for distance in range(1, CONV):
                at = HALO + distance if reverse else HALO - distance
                term = ext[at : at + CHUNK, lanes] * taps[CONV - 1 - distance : CONV - distance, lanes]
                total = total + jnp.where(left >= distance, term, 0.0)
            base = mixed if reverse else 0
            conv_ref[:, base + block * width : base + (block + 1) * width] = silu(total).astype(bf16)

    tails = (
        head_lanes([turned[:, 12 + h : 13 + h] for h in range(4)]),
        head_lanes([turned[:, 20 + h : 21 + h] for h in range(4)]),
    )
    passing = head_lanes([cols[h : h + 1, CHUNK - 1 :] for h in range(4)])
    for d in range(2):
        x = conv_ref[:, d * mixed : d * mixed + inner].astype(f32)
        write = conv_ref[:, d * mixed + inner : d * mixed + inner + STATE]
        scaled = (x * tails[d]).astype(bf16)
        fresh = mm(write, scaled, TN)
        fresh_ref[0, d] = fresh.astype(bf16)
        if d == 0:
            run[0] = run[0] * jnp.exp2(passing) + fresh
        else:
            run[1] = run[1] + jnp.exp2(reach[0:1, :]) * fresh
    reach[...] = reach[...] + passing

    @pl.when(c == count - 1)
    def _():
        end_ref[...] = run[...].astype(bf16)
        total_ref[...] = reach[...]


def states(axis, mix, halo, gain, vw, sw, raw, lens, bias, rate, cv, cs):
    tokens, mixed = mix.shape
    chunks = tokens // CHUNK
    inner = vw.shape[1]
    per = CHUNK // 16
    last = tokens // 16 - 1
    return pl.pallas_call(
        functools.partial(states_kernel, axis),
        grid=(chunks,),
        in_specs=[
            pl.BlockSpec((CHUNK, mixed), lambda c: (c, 0)),
            pl.BlockSpec((16, mixed), lambda c: (jnp.maximum(c * per - 1, 0), 0)),
            pl.BlockSpec((16, mixed), lambda c: (jnp.minimum(c * per + per, last), 0)),
            whole(halo.shape),
            whole(gain.shape),
            whole(vw.shape),
            whole(sw.shape),
            whole(raw.shape),
            SMEM_SPEC,
            SMEM_SPEC,
            SMEM_SPEC,
            whole(cv.shape),
            whole(cs.shape),
        ],
        out_specs=[
            pl.BlockSpec((CHUNK, 2 * mixed), lambda c: (c, 0)),
            pl.BlockSpec((1, 2, STATE, inner), lambda c: (c, 0, 0, 0)),
            whole((chunks, 32, CHUNK)),
            whole((chunks, 8, CHUNK)),
            whole((2, STATE, inner)),
            whole((8, inner)),
        ],
        out_shape=[
            jax.ShapeDtypeStruct((tokens, 2 * mixed), bf16),
            jax.ShapeDtypeStruct((chunks, 2, STATE, inner), bf16),
            jax.ShapeDtypeStruct((chunks, 32, CHUNK), f32),
            jax.ShapeDtypeStruct((chunks, 8, CHUNK), f32),
            jax.ShapeDtypeStruct((2, STATE, inner), bf16),
            jax.ShapeDtypeStruct((8, inner), f32),
        ],
        scratch_shapes=[
            pltpu.VMEM((CHUNK + 2 * HALO, mixed), f32),
            pltpu.VMEM((2 * HALO, mixed), f32),
            pltpu.VMEM((2, STATE, inner), f32),
            pltpu.VMEM((8, inner), f32),
        ],
        compiler_params=params(),
        name="states",
    )(mix, mix, mix, halo, gain, vw, sw, raw, lens, bias, rate, cv, cs)


def remote(src, dst, send, recv, **where):
    return pltpu.make_async_remote_copy(
        src_ref=src,
        dst_ref=dst,
        send_sem=send,
        recv_sem=recv,
        device_id=where,
        device_id_type=MESH,
    )


def greet(axes_and_peers):
    barrier = pltpu.get_barrier_semaphore()
    for where in axes_and_peers:
        pl.semaphore_signal(barrier, inc=1, device_id=where, device_id_type=MESH)
    pl.semaphore_wait(barrier, len(axes_and_peers))


def head_peer(me, chips, dy, dc):
    y, core = me // 2, me % 2
    return ((y + dy) % chips) * 2 + (core + dc) % 2


def exchange_kernel(
    seq_count,
    head_count,
    end_ref,
    total_ref,
    w_ref,
    in_ref,
    all_ref,
    ends,
    totals,
    end_send,
    end_recv,
    total_send,
    total_recv,
    w_send,
    w_recv,
):
    me = lax.axis_index("seq")
    head = lax.axis_index("head")
    chips = head_count // 2
    half = w_ref.shape[0] // 2
    up = head_peer(head, chips, 1, 0)
    down = head_peer(head, chips, chips - 1, 0)
    partner = head_peer(head, chips, 0, 1)
    greet(
        [{"seq": (me + k) % seq_count} for k in range(1, seq_count)]
        + [{"head": up}, {"head": down}, {"head": partner}]
    )
    started = []

    def start(copy):
        copy.start()
        started.append(copy)
        return copy

    near = start(remote(w_ref, all_ref.at[2], w_send.at[0], w_recv.at[0], head=up))
    far = start(remote(w_ref, all_ref.at[6], w_send.at[1], w_recv.at[1], head=down))
    beside = start(remote(w_ref, all_ref.at[1], w_send.at[2], w_recv.at[2], head=partner))
    for k in range(1, seq_count):
        target = (me + k) % seq_count
        backward = (me + k) // seq_count
        start(remote(end_ref.at[backward], ends.at[k], end_send.at[k], end_recv.at[k], seq=target))
        start(remote(total_ref, totals.at[k], total_send.at[k], total_recv.at[k], seq=target))

    near.wait_recv()
    top, bottom = pl.ds(0, half), pl.ds(half, half)
    t1 = start(remote(all_ref.at[2, top], all_ref.at[4, top], w_send.at[3], w_recv.at[3], head=up))
    t2 = start(remote(all_ref.at[2], all_ref.at[3], w_send.at[4], w_recv.at[4], head=partner))
    far.wait_recv()
    t3 = start(
        remote(all_ref.at[6, bottom], all_ref.at[4, bottom], w_send.at[5], w_recv.at[5], head=down)
    )
    t4 = start(remote(all_ref.at[6], all_ref.at[7], w_send.at[6], w_recv.at[6], head=partner))

    for k in range(1, seq_count):
        target = (me + k) % seq_count
        remote(end_ref.at[0], ends.at[k], end_send.at[k], end_recv.at[k], seq=target).wait_recv()
        remote(total_ref, totals.at[k], total_send.at[k], total_recv.at[k], seq=target).wait_recv()
    in_ref[...] = jnp.zeros_like(in_ref)
    for k in range(seq_count - 1, 0, -1):

        @pl.when(k <= me)
        def _(k=k):
            in_ref[0] = in_ref[0] * jnp.exp2(totals[k, 0:1, :]) + ends[k].astype(f32)

    for k in range(1, seq_count):

        @pl.when(k > me)
        def _(k=k):
            in_ref[1] = in_ref[1] * jnp.exp2(totals[k, 0:1, :]) + ends[k].astype(f32)

    t1.wait_recv()
    t3.wait_recv()
    t5 = start(remote(all_ref.at[4], all_ref.at[5], w_send.at[7], w_recv.at[7], head=partner))
    for copy in (beside, t2, t4, t5):
        copy.wait_recv()
    for copy in started:
        copy.wait_send()


def exchange(mesh_shape, end, total, w):
    seq_count, head_count = mesh_shape
    return pl.pallas_call(
        functools.partial(exchange_kernel, seq_count, head_count),
        in_specs=[whole(end.shape), whole(total.shape), ANY_SPEC],
        out_specs=[whole(end.shape), ANY_SPEC],
        out_shape=[
            jax.ShapeDtypeStruct(end.shape, f32),
            jax.ShapeDtypeStruct((head_count,) + w.shape, bf16),
        ],
        scratch_shapes=[
            pltpu.VMEM((seq_count,) + end.shape[1:], bf16),
            pltpu.VMEM((seq_count,) + total.shape, f32),
            pltpu.SemaphoreType.DMA((seq_count,)),
            pltpu.SemaphoreType.DMA((seq_count,)),
            pltpu.SemaphoreType.DMA((seq_count,)),
            pltpu.SemaphoreType.DMA((seq_count,)),
            pltpu.SemaphoreType.DMA((8,)),
            pltpu.SemaphoreType.DMA((8,)),
        ],
        compiler_params=params(collective_id=0, has_side_effects=True),
        name="exchange",
    )(end, total, w)


def outputs_kernel(
    conv_ref, gate_ref, cols_ref, row_ref, fresh_ref, in_ref, skip_ref, gf_ref, gb_ref, ss_ref, entry
):
    g = pl.program_id(0)
    chunks = fresh_ref.shape[0]
    inner = gate_ref.shape[1]
    mixed = conv_ref.shape[1] // 2
    group = conv_ref.shape[0] // CHUNK

    @pl.when(g == 0)
    def _():
        def passing(c):
            return jnp.exp2(head_lanes([cols_ref[c, h : h + 1, CHUNK - 1 :] for h in range(4)]))

        def forward(c, state):
            entry[0, c] = state.astype(bf16)
            return state * passing(c) + fresh_ref[c, 0].astype(f32)

        def backward(i, state):
            c = chunks - 1 - i
            entry[1, c] = state.astype(bf16)
            return state * passing(c) + fresh_ref[c, 1].astype(f32)

        lax.fori_loop(0, chunks, forward, in_ref[0])
        lax.fori_loop(0, chunks, backward, in_ref[1])

    i = lax.broadcasted_iota(jnp.int32, (CHUNK, CHUNK), 0)
    j = lax.broadcasted_iota(jnp.int32, (CHUNK, CHUNK), 1)
    lower = i >= j
    upper = i <= j
    low = j < HEAD_DIM
    skip = head_lanes([jnp.full((1, 1), skip_ref[h], f32) for h in range(4)])
    sub = lax.broadcasted_iota(jnp.int32, (8, CHUNK), 0)
    ones = jnp.ones((8, inner), bf16)
    sums = jnp.zeros((8, CHUNK), f32)
    for q in range(group):
        c = g * group + q
        rows = slice(q * CHUNK, (q + 1) * CHUNK)
        cols = cols_ref[c]
        turned = jnp.concatenate([cols, jnp.zeros((CHUNK - 32, CHUNK), f32)], axis=0).T
        row = row_ref[c]
        pair = []
        for d, keep in ((0, lower), (1, upper)):
            base = d * mixed + inner
            write = conv_ref[rows, base : base + STATE]
            read = conv_ref[rows, base + STATE : base + 2 * STATE]
            pair.append(jnp.where(keep, mm(read, write, NT), 0.0))
        weights = ([], [])
        for h in range(4):
            arg = jnp.where(
                lower,
                turned[:, h : h + 1] - row[h : h + 1, :],
                row[4 + h : 5 + h, :] - turned[:, 4 + h : 5 + h],
            )
            table = jnp.exp2(arg)
            for d in range(2):
                weights[d].append((pair[d] * table).astype(bf16))
        gate = silu(gate_ref[rows, :].astype(f32))
        opening = (8, 16)
        for d, out_ref in ((0, gf_ref), (1, gb_ref)):
            x = conv_ref[rows, d * mixed : d * mixed + inner]
            read = conv_ref[rows, d * mixed + inner + STATE : (d + 1) * mixed]
            local = []
            for p in range(2):
                half = x[:, p * CHUNK : (p + 1) * CHUNK]
                zero = jnp.zeros_like(half)
                stacked = jnp.concatenate(
                    [jnp.where(low, half, zero), jnp.where(low, zero, half)], axis=0
                )
                both = jnp.concatenate(weights[d][2 * p : 2 * p + 2], axis=1)
                local.append(mm(both, stacked))
            carried = mm(read, entry[d, c])
            open_at = opening[d]
            scale = head_lanes([turned[:, open_at + h : open_at + h + 1] for h in range(4)])
            out = jnp.concatenate(local, axis=1) + carried * scale + skip * x.astype(f32)
            gated = out * gate
            out_ref[rows, :] = gated.astype(bf16)
            square = mm(ones, (gated * gated).astype(bf16), NT)
            sums = jnp.where(sub == 2 * q + d, square, sums)
    ss_ref[...] = sums


def outputs(conv, gate, cols, row, fresh, incoming, skip):
    tokens, inner = gate.shape
    chunks = tokens // CHUNK
    rows = 4 * CHUNK
    return pl.pallas_call(
        outputs_kernel,
        grid=(tokens // rows,),
        in_specs=[
            pl.BlockSpec((rows, conv.shape[1]), lambda g: (g, 0)),
            pl.BlockSpec((rows, inner), lambda g: (g, 0)),
            whole(cols.shape),
            whole(row.shape),
            whole(fresh.shape),
            whole(incoming.shape),
            SMEM_SPEC,
        ],
        out_specs=[
            pl.BlockSpec((rows, inner), lambda g: (g, 0)),
            pl.BlockSpec((rows, inner), lambda g: (g, 0)),
            pl.BlockSpec((8, CHUNK), lambda g: (g, 0)),
        ],
        out_shape=[
            jax.ShapeDtypeStruct((tokens, inner), bf16),
            jax.ShapeDtypeStruct((tokens, inner), bf16),
            jax.ShapeDtypeStruct((2 * chunks, CHUNK), f32),
        ],
        scratch_shapes=[pltpu.VMEM((2, chunks, STATE, inner), bf16)],
        compiler_params=params(),
        name="outputs",
    )(conv, gate, cols, row, fresh, incoming, skip)


def finish_kernel(
    head_count,
    gf_ref,
    gb_ref,
    ss_ref,
    gain_ref,
    hidden_ref,
    w_ref,
    all_ref,
    out_ref,
    sums,
    sending,
    arrived,
    total,
    rest,
    ss_send,
    ss_recv,
    send,
    recv,
    load,
):
    me = lax.axis_index("head")
    chips = head_count // 2
    inner = gain_ref.shape[1]
    rows = out_ref.shape[0]
    lines = ss_ref.shape[0] // head_count
    slots = [(dy, dc) for dy in range(chips) for dc in range(2)]
    peers = [head_peer(me, chips, dy, dc) for dy, dc in slots]
    residual = pltpu.make_async_copy(
        hidden_ref.at[pl.ds(pl.multiple_of(me * rows, rows), rows), :], rest, load
    )
    residual.start()
    greet([{"head": p} for p in peers[1:]])
    started = []
    for k in range(1, head_count):
        copy = remote(ss_ref, sums.at[k], ss_send.at[k], ss_recv.at[k], head=peers[k])
        copy.start()
        started.append(copy)
    for copy in started:
        copy.wait_recv()
    squares = ss_ref[...]
    for k in range(1, head_count):
        squares = squares + sums[k]
    total[...] = lax.rsqrt(squares * (1.0 / (inner * head_count)) + epsilon)
    gain = gain_ref[...].astype(f32)

    def combine(owner, slot):
        scale = total[pl.ds(pl.multiple_of(owner * lines, lines), lines), :]
        scale = jnp.concatenate([scale, jnp.zeros((CHUNK - lines, CHUNK), f32)], axis=0).T
        for q in range(rows // CHUNK):
            at = pl.ds(pl.multiple_of(owner * rows + q * CHUNK, CHUNK), CHUNK)
            both = gf_ref[at, :].astype(f32) * scale[:, 2 * q : 2 * q + 1]
            both = both + gb_ref[at, :].astype(f32) * scale[:, 2 * q + 1 : 2 * q + 2]
            sending[slot, q * CHUNK : (q + 1) * CHUNK, :] = (both * gain).astype(bf16)

    order = sorted(range(1, head_count), key=lambda k: -min(slots[k][0], chips - slots[k][0]))
    copies = []
    for k in order:
        combine(peers[k], k)
        copy = remote(sending.at[k], arrived.at[k], send.at[k], recv.at[k], head=peers[k])
        copy.start()
        copies.append(copy)
    combine(me, 0)
    residual.wait()
    step = 256

    def add(rows_in, weight, first):
        for b in range(out_ref.shape[1] // step):
            lanes = slice(b * step, (b + 1) * step)
            term = mm(rows_in, weight[:, lanes])
            if first:
                rest_wide[:, lanes] = rest[:, lanes].astype(f32) + term
            else:
                rest_wide[:, lanes] = rest_wide[:, lanes] + term

    def body(rest_wide_ref):
        nonlocal rest_wide
        rest_wide = rest_wide_ref
        add(sending[0], w_ref[...], True)
        for copy, k in reversed(list(zip(copies, order))):
            copy.wait_recv()
            add(arrived[k], all_ref[k], False)
        out_ref[...] = rest_wide_ref[...].astype(bf16)

    rest_wide = None
    pl.run_scoped(body, pltpu.VMEM(out_ref.shape, f32))
    for copy in started + copies:
        copy.wait_send()


def finish(head_count, gf, gb, ss, gain, hidden, w, w_all):
    tokens, inner = gf.shape
    rows = tokens // head_count
    width = hidden.shape[1]
    return pl.pallas_call(
        functools.partial(finish_kernel, head_count),
        in_specs=[
            whole(gf.shape),
            whole(gb.shape),
            whole(ss.shape),
            whole(gain.shape),
            ANY_SPEC,
            whole(w.shape),
            whole(w_all.shape),
        ],
        out_specs=whole((rows, width)),
        out_shape=jax.ShapeDtypeStruct((rows, width), bf16),
        scratch_shapes=[
            pltpu.VMEM((head_count,) + ss.shape, f32),
            pltpu.VMEM((head_count, rows, inner), bf16),
            pltpu.VMEM((head_count, rows, inner), bf16),
            pltpu.VMEM(ss.shape, f32),
            pltpu.VMEM((rows, width), bf16),
            pltpu.SemaphoreType.DMA((head_count,)),
            pltpu.SemaphoreType.DMA((head_count,)),
            pltpu.SemaphoreType.DMA((head_count,)),
            pltpu.SemaphoreType.DMA((head_count,)),
            pltpu.SemaphoreType.DMA,
        ],
        compiler_params=params(collective_id=1, has_side_effects=True),
        name="finish",
    )(gf, gb, ss, gain, hidden, w, w_all)


def local(
    hidden_in,
    norm_gain,
    gate_weight,
    value_weight,
    state_weight,
    step_weight,
    step_bias,
    decay_log,
    skip_gain,
    conv_value,
    conv_state,
    output_gain,
    output_weight,
    piece_lengths,
):
    seq_count, head_count = lax.axis_size("seq"), lax.axis_size("head")
    up = [(i, i + 1) for i in range(seq_count - 1)]
    down = [(j, i) for i, j in up]
    before = lax.ppermute(hidden_in[-HALO:], "seq", up)
    after = lax.ppermute(hidden_in[:HALO], "seq", down)
    gain = norm_gain.reshape(1, -1)
    turned = step_weight.T
    gate, mix, raw = project(
        hidden_in, gain, gate_weight, value_weight, state_weight, jnp.concatenate([turned, turned])
    )
    halo = jnp.concatenate([before, after])
    conv, fresh, cols, row, end, total = states(
        "seq",
        mix,
        halo,
        gain,
        value_weight,
        state_weight,
        raw,
        piece_lengths,
        step_bias,
        decay_log,
        conv_value,
        conv_state,
    )
    incoming, w_all = exchange((seq_count, head_count), end, total, output_weight)
    gf, gb, ss = outputs(conv, gate, cols, row, fresh, incoming, skip_gain)
    return finish(
        head_count, gf, gb, ss, output_gain.reshape(1, -1), hidden_in, output_weight, w_all
    )


def solution(mesh):
    in_specs = (
        P("seq", None),
        P(),
        P(None, "head"),
        P(None, "head"),
        P(),
        P(None, "head"),
        P("head"),
        P("head"),
        P("head"),
        P(None, "head"),
        P(),
        P("head"),
        P("head", None),
        P(),
    )
    out_specs = P(("seq", "head"), None)
    return jax.shard_map(local, mesh=mesh, in_specs=in_specs, out_specs=out_specs, check_vma=False)
```

```python
import functools
import math

import jax
import jax.numpy as jnp
from jax import lax
from jax.experimental import pallas as pl
from jax.experimental.pallas import tpu as pltpu
from jax.sharding import PartitionSpec as P

HEAD_DIM = 64
STATE = 128
CONV = 4
CHUNK = 128
PIECES = 16
HALO = 16
REACH = 8
RESET = 256.0
LOG2E = math.log2(math.e)

f32 = jnp.float32
bf16 = jnp.bfloat16
epsilon = 1e-05
MESH = pl.DeviceIdType.MESH
NN = (((1,), (0,)), ((), ()))
NT = (((1,), (1,)), ((), ()))
TN = (((0,), (0,)), ((), ()))


def mm(a, b, dims=NN, precision=None):
    return lax.dot_general(a, b, dims, precision=precision, preferred_element_type=f32)


def silu(x):
    half = 0.5 * x
    return half * jnp.tanh(half) + half


def normalized(h, gain):
    wide = h.astype(f32)
    scale = lax.rsqrt(jnp.mean(wide * wide, axis=1, keepdims=True) + epsilon)
    return (wide * scale * gain.astype(f32)).astype(bf16)


def whole(shape):
    zeros = (0,) * len(shape)
    return pl.BlockSpec(shape, lambda *_: zeros)


SMEM_SPEC = pl.BlockSpec(memory_space=pltpu.SMEM)
ANY_SPEC = pl.BlockSpec(memory_space=pl.ANY)


def params(**kw):
    return pltpu.CompilerParams(vmem_limit_bytes=60 * 1024 * 1024, **kw)


def remote(src, dst, send, recv, **where):
    return pltpu.make_async_remote_copy(
        src_ref=src,
        dst_ref=dst,
        send_sem=send,
        recv_sem=recv,
        device_id=where,
        device_id_type=MESH,
    )


def greet(axes_and_peers):
    barrier = pltpu.get_barrier_semaphore()
    for where in axes_and_peers:
        pl.semaphore_signal(barrier, inc=1, device_id=where, device_id_type=MESH)
    pl.semaphore_wait(barrier, len(axes_and_peers))


def head_peer(me, chips, dy, dc):
    y, core = me // 2, me % 2
    return ((y + dy) % chips) * 2 + (core + dc) % 2


def project_copies(seq_count, head_count, hidden, w, halo, hop, send, recv):
    me = lax.axis_index("seq")
    head = lax.axis_index("head")
    chips = head_count // 2
    tokens = hidden.shape[0]
    after = (me + 1) % seq_count
    before = (me + seq_count - 1) % seq_count
    first, last = pl.ds(0, HALO), pl.ds(tokens - HALO, HALO)
    low, high = pl.ds(0, HALO), pl.ds(HALO, HALO)
    up = head_peer(head, chips, 1, 0)
    down = head_peer(head, chips, chips - 1, 0)
    partner = head_peer(head, chips, 0, 1)
    return (
        remote(hidden.at[last], halo.at[low], send.at[0], recv.at[0], seq=after),
        remote(hidden.at[first], halo.at[high], send.at[1], recv.at[1], seq=before),
        remote(w, hop.at[0], send.at[2], recv.at[2], head=up),
        remote(w, hop.at[1], send.at[3], recv.at[3], head=down),
        remote(w, hop.at[2], send.at[4], recv.at[4], head=partner),
    ), [{"seq": after}, {"seq": before}, {"head": up}, {"head": down}, {"head": partner}]


def project_kernel(
    mesh_shape,
    h_ref,
    gain_ref,
    gw_ref,
    vw_ref,
    sw_ref,
    tw_ref,
    hidden,
    w,
    gate_ref,
    mix_ref,
    raw_ref,
    halo,
    hop,
    turned,
    send,
    recv,
):
    i = pl.program_id(0)
    copies, peers = project_copies(*mesh_shape, hidden, w, halo, hop, send, recv)
    barrier = pltpu.get_barrier_semaphore()

    @pl.when(i == 0)
    def _():
        for where in peers:
            pl.semaphore_signal(barrier, inc=1, device_id=where, device_id_type=MESH)
        narrow = tw_ref[...].astype(f32)
        depth, few = narrow.shape
        padded = jnp.concatenate(
            [narrow, narrow, jnp.zeros((depth, CHUNK - 2 * few), f32)], axis=1
        )
        turned[...] = padded.T[:8].astype(bf16)

    @pl.when(i == 1)
    def _():
        pl.semaphore_wait(barrier, len(peers))
        for copy in copies:
            copy.start()

    inner = vw_ref.shape[1]
    n = normalized(h_ref[...], gain_ref[...].reshape(1, -1))
    gate_ref[...] = mm(n, gw_ref[...]).astype(bf16)
    mix_ref[:, :inner] = mm(n, vw_ref[...]).astype(bf16)
    mix_ref[:, inner:] = mm(n, sw_ref[...]).astype(bf16)
    raw = mm(turned[...], n, NT)
    for q in range(raw.shape[1] // CHUNK):
        raw_ref[q] = raw[:, q * CHUNK : (q + 1) * CHUNK]

    @pl.when(i == pl.num_programs(0) - 1)
    def _():
        for copy in copies:
            copy.wait()


def project(mesh_shape, hidden, gain, gw, vw, sw, tw, w):
    tokens, width = hidden.shape
    inner = vw.shape[1]
    mixed = inner + sw.shape[1]
    rows = min(512, tokens // 2)
    return pl.pallas_call(
        functools.partial(project_kernel, mesh_shape),
        grid=(tokens // rows,),
        in_specs=[
            pl.BlockSpec((rows, width), lambda i: (i, 0)),
            whole(gain.shape),
            whole(gw.shape),
            whole(vw.shape),
            whole(sw.shape),
            whole(tw.shape),
            ANY_SPEC,
            ANY_SPEC,
        ],
        out_specs=[
            pl.BlockSpec((rows, inner), lambda i: (i, 0)),
            pl.BlockSpec((rows, mixed), lambda i: (i, 0)),
            pl.BlockSpec((rows // CHUNK, 8, CHUNK), lambda i: (i, 0, 0)),
            ANY_SPEC,
            ANY_SPEC,
        ],
        out_shape=[
            jax.ShapeDtypeStruct((tokens, inner), bf16),
            jax.ShapeDtypeStruct((tokens, mixed), bf16),
            jax.ShapeDtypeStruct((tokens // CHUNK, 8, CHUNK), f32),
            jax.ShapeDtypeStruct((2 * HALO, width), bf16),
            jax.ShapeDtypeStruct((3,) + w.shape, bf16),
        ],
        scratch_shapes=[
            pltpu.VMEM((8, width), bf16),
            pltpu.SemaphoreType.DMA((5,)),
            pltpu.SemaphoreType.DMA((5,)),
        ],
        compiler_params=params(collective_id=2, has_side_effects=True),
        name="project",
    )(hidden, gain, gw, vw, sw, tw, hidden, w)


def head_lanes(columns):
    low = lax.broadcasted_iota(jnp.int32, (columns[0].shape[0], 2 * HEAD_DIM), 1) < HEAD_DIM
    pairs = [
        jnp.where(low, columns[2 * p], columns[2 * p + 1]) for p in range(len(columns) // 2)
    ]
    return jnp.concatenate(pairs, axis=1)


def decays(first_row, raw, lens_ref, bias_ref, rate_ref):
    chunks = raw.shape[0]
    shape = (chunks, 8, CHUNK)
    sub = lax.broadcasted_iota(jnp.int32, shape, 1)
    upper = sub < 4
    head = jnp.where(upper, sub, sub - 4)
    pos = (
        first_row
        + lax.broadcasted_iota(jnp.int32, shape, 0) * CHUNK
        + lax.broadcasted_iota(jnp.int32, shape, 2)
    )
    start = jnp.zeros(shape, jnp.int32)
    stop = jnp.full(shape, 1 << 30, jnp.int32)
    edge = jnp.int32(0)
    for k in range(PIECES):
        start = jnp.where(pos >= edge, edge, start)
        edge = edge + lens_ref[k]
        stop = jnp.minimum(stop, jnp.where(edge > pos, edge, 1 << 30))
    since = pos - start
    until = stop - 1 - pos
    bias = jnp.zeros(shape, f32)
    rate = jnp.zeros(shape, f32)
    for h in range(4):
        bias = jnp.where(head == h, bias_ref[h], bias)
        rate = jnp.where(head == h, rate_ref[h], rate)
    rate = jnp.exp(rate) * (-LOG2E)
    z = raw + bias
    step = jnp.maximum(z, 0.0) + jnp.log1p(jnp.exp(-jnp.abs(z)))
    log = step * rate
    reset = jnp.where(since == 0, -RESET, 0.0)
    ones = (
        lax.broadcasted_iota(jnp.int32, (CHUNK, CHUNK), 0)
        <= lax.broadcasted_iota(jnp.int32, (CHUNK, CHUNK), 1)
    ).astype(f32)
    cum = mm(
        (log + reset).reshape(chunks * 8, CHUNK), ones, precision=lax.Precision.HIGHEST
    ).reshape(shape)
    excl = cum - log
    total = cum[:, :, CHUNK - 1 :]
    log_step = jnp.where(step > 0.0, jnp.log2(step), -RESET)
    row = jnp.where(upper, cum - log_step, excl + log_step)
    g1 = jnp.where(upper, cum, excl)
    g2 = jnp.where(upper, jnp.exp2(cum), jnp.exp2(total - cum) * step)
    g3 = jnp.where(upper, jnp.exp2(total - excl), jnp.exp2(excl) * step)
    g4 = jnp.where(upper, since, until).astype(f32)
    return row, g1, g2, g3, g4


def states_kernel(
    axis,
    mix_ref,
    before_ref,
    after_ref,
    halo_ref,
    gain_ref,
    vw_ref,
    sw_ref,
    raw_ref,
    lens_ref,
    bias_ref,
    rate_ref,
    cv_ref,
    cs_ref,
    conv_ref,
    fresh_ref,
    cols_ref,
    row_ref,
    end_ref,
    total_ref,
    prod,
    halo,
    run,
    reach,
    spread,
    near,
):
    c = pl.program_id(0)
    count = pl.num_programs(0)
    inner = vw_ref.shape[1]
    mixed = mix_ref.shape[1]
    blocks = mixed // 128
    first_row = lax.axis_index(axis) * (count * CHUNK)

    @pl.when(c == 0)
    def _():
        n = normalized(halo_ref[...], gain_ref[...].reshape(1, -1))
        halo[:, :inner] = mm(n, vw_ref[...]).astype(bf16).astype(f32)
        halo[:, inner:] = mm(n, sw_ref[...]).astype(bf16).astype(f32)
        row, g1, g2, g3, g4 = decays(first_row, raw_ref[...], lens_ref, bias_ref, rate_ref)
        row_ref[...] = row
        cols_ref[:, 0:8, :] = g1
        cols_ref[:, 8:16, :] = g2
        cols_ref[:, 16:24, :] = g3
        cols_ref[:, 24:32, :] = g4
        run[...] = jnp.zeros_like(run)
        reach[...] = jnp.zeros_like(reach)
        line = lax.broadcasted_iota(jnp.int32, spread.shape, 0) % 32
        lane = lax.broadcasted_iota(jnp.int32, spread.shape, 1)
        wanted = 12 + (lane // inner) * 8 + (lane % inner) // HEAD_DIM
        spread[...] = (line == wanted).astype(f32).astype(bf16)

        def clear(k, carry):
            near[k] = 0
            return carry

        lax.fori_loop(0, near.shape[0], clear, 0)

        def mark(k, edge):
            for shift in (-(CONV - 1), CONV - 2):
                at = (edge + shift - first_row + CHUNK) // CHUNK
                near[jnp.clip(at, 0, near.shape[0] - 1)] = 1
            return edge + lens_ref[jnp.minimum(k, PIECES - 1)]

        lax.fori_loop(0, PIECES + 1, mark, jnp.int32(0))

    taps = jnp.concatenate([cv_ref[...], cs_ref[...]], axis=1).astype(f32)
    here = slice(REACH, REACH + CHUNK)

    def put(rows, values):
        for k in range(CONV - 1):
            for b in range(blocks):
                lanes = slice(b * 128, (b + 1) * 128)
                prod[k, b, rows, :] = values[:, lanes] * taps[k : k + 1, lanes]

    put(here, mix_ref[...].astype(f32))
    ahead, behind = slice(0, REACH), slice(REACH + CHUNK, 2 * REACH + CHUNK)

    @pl.when(c == 0)
    def _():
        put(ahead, halo[HALO - REACH : HALO, :])

    @pl.when(c > 0)
    def _():
        put(ahead, before_ref[...].astype(f32)[16 - REACH :, :])

    @pl.when(c == count - 1)
    def _():
        put(behind, halo[HALO : HALO + REACH, :])

    @pl.when(c < count - 1)
    def _():
        put(behind, after_ref[...].astype(f32)[:REACH, :])

    cols = cols_ref[c]

    def convolve(masked):
        if masked:
            turned = jnp.concatenate([cols, jnp.zeros((CHUNK - 32, CHUNK), f32)], axis=0).T
            sides = [jnp.broadcast_to(turned[:, r : r + 1], (CHUNK, 128)) for r in (24, 28)]
        for b in range(blocks):
            lanes = slice(b * 128, (b + 1) * 128)
            centre = mix_ref[:, lanes].astype(f32) * taps[CONV - 1 : CONV, lanes]
            for d in range(2):
                total = centre
                for distance in range(1, CONV):
                    at = REACH + distance if d else REACH - distance
                    term = prod[CONV - 1 - distance, b, at : at + CHUNK, :]
                    if masked:
                        term = jnp.where(sides[d] >= distance, term, 0.0)
                    total = total + term
                at = d * mixed + b * 128
                conv_ref[:, at : at + 128] = silu(total).astype(bf16)

    edges = near[c + 1]

    @pl.when(edges == 0)
    def _():
        convolve(False)

    @pl.when(edges != 0)
    def _():
        convolve(True)

    high = cols.astype(bf16).astype(f32)
    both = jnp.concatenate([high, cols - high], axis=0).astype(bf16)
    tails = mm(both, spread[...], TN)
    passing = head_lanes([cols[h : h + 1, CHUNK - 1 :] for h in range(4)])
    for d in range(2):
        x = conv_ref[:, d * mixed : d * mixed + inner].astype(f32)
        write = conv_ref[:, d * mixed + inner : d * mixed + inner + STATE]
        scaled = (x * tails[:, d * inner : (d + 1) * inner]).astype(bf16)
        fresh = mm(write, scaled, TN)
        fresh_ref[0, d] = fresh.astype(bf16)
        if d == 0:
            run[0] = run[0] * jnp.exp2(passing) + fresh
        else:
            run[1] = run[1] + jnp.exp2(reach[0:1, :]) * fresh
    reach[...] = reach[...] + passing

    @pl.when(c == count - 1)
    def _():
        end_ref[...] = run[...].astype(bf16)
        total_ref[...] = reach[...]


def states(axis, mix, halo, gain, vw, sw, raw, lens, bias, rate, cv, cs):
    tokens, mixed = mix.shape
    chunks = tokens // CHUNK
    inner = vw.shape[1]
    per = CHUNK // 16
    last = tokens // 16 - 1
    return pl.pallas_call(
        functools.partial(states_kernel, axis),
        grid=(chunks,),
        in_specs=[
            pl.BlockSpec((CHUNK, mixed), lambda c: (c, 0)),
            pl.BlockSpec((16, mixed), lambda c: (jnp.maximum(c * per - 1, 0), 0)),
            pl.BlockSpec((16, mixed), lambda c: (jnp.minimum(c * per + per, last), 0)),
            whole(halo.shape),
            whole(gain.shape),
            whole(vw.shape),
            whole(sw.shape),
            whole(raw.shape),
            SMEM_SPEC,
            SMEM_SPEC,
            SMEM_SPEC,
            whole(cv.shape),
            whole(cs.shape),
        ],
        out_specs=[
            pl.BlockSpec((CHUNK, 2 * mixed), lambda c: (c, 0)),
            pl.BlockSpec((1, 2, STATE, inner), lambda c: (c, 0, 0, 0)),
            whole((chunks, 32, CHUNK)),
            whole((chunks, 8, CHUNK)),
            whole((2, STATE, inner)),
            whole((8, inner)),
        ],
        out_shape=[
            jax.ShapeDtypeStruct((tokens, 2 * mixed), bf16),
            jax.ShapeDtypeStruct((chunks, 2, STATE, inner), bf16),
            jax.ShapeDtypeStruct((chunks, 32, CHUNK), f32),
            jax.ShapeDtypeStruct((chunks, 8, CHUNK), f32),
            jax.ShapeDtypeStruct((2, STATE, inner), bf16),
            jax.ShapeDtypeStruct((8, inner), f32),
        ],
        scratch_shapes=[
            pltpu.VMEM((CONV - 1, mixed // 128, CHUNK + 2 * REACH, 128), f32),
            pltpu.VMEM((2 * HALO, mixed), f32),
            pltpu.VMEM((2, STATE, inner), f32),
            pltpu.VMEM((8, inner), f32),
            pltpu.VMEM((64, 2 * inner), bf16),
            pltpu.SMEM((chunks + 2,), jnp.int32),
        ],
        compiler_params=params(),
        name="states",
    )(mix, mix, mix, halo, gain, vw, sw, raw, lens, bias, rate, cv, cs)


def exchange_kernel(
    seq_count,
    head_count,
    end_ref,
    total_ref,
    hop_ref,
    in_ref,
    far_ref,
    ends,
    totals,
    end_send,
    end_recv,
    total_send,
    total_recv,
    w_send,
    w_recv,
):
    me = lax.axis_index("seq")
    head = lax.axis_index("head")
    chips = head_count // 2
    half = hop_ref.shape[1] // 2
    up = head_peer(head, chips, 1, 0)
    down = head_peer(head, chips, chips - 1, 0)
    partner = head_peer(head, chips, 0, 1)
    greet(
        [{"seq": (me + k) % seq_count} for k in range(1, seq_count)]
        + [{"head": up}, {"head": down}, {"head": partner}]
    )
    started = []

    def start(copy):
        copy.start()
        started.append(copy)
        return copy

    top, bottom = pl.ds(0, half), pl.ds(half, half)
    t1 = start(remote(hop_ref.at[0, top], far_ref.at[2, top], w_send.at[0], w_recv.at[0], head=up))
    t3 = start(
        remote(hop_ref.at[1, bottom], far_ref.at[2, bottom], w_send.at[1], w_recv.at[1], head=down)
    )
    t2 = start(remote(hop_ref.at[0], far_ref.at[0], w_send.at[2], w_recv.at[2], head=partner))
    t4 = start(remote(hop_ref.at[1], far_ref.at[1], w_send.at[3], w_recv.at[3], head=partner))
    for k in range(1, seq_count):
        target = (me + k) % seq_count
        backward = (me + k) // seq_count
        start(remote(end_ref.at[backward], ends.at[k], end_send.at[k], end_recv.at[k], seq=target))
        start(remote(total_ref, totals.at[k], total_send.at[k], total_recv.at[k], seq=target))

    t1.wait_recv()
    t3.wait_recv()
    t5 = start(remote(far_ref.at[2], far_ref.at[3], w_send.at[4], w_recv.at[4], head=partner))
    for k in range(1, seq_count):
        target = (me + k) % seq_count
        remote(end_ref.at[0], ends.at[k], end_send.at[k], end_recv.at[k], seq=target).wait_recv()
        remote(total_ref, totals.at[k], total_send.at[k], total_recv.at[k], seq=target).wait_recv()
    in_ref[...] = jnp.zeros_like(in_ref)
    for k in range(seq_count - 1, 0, -1):

        @pl.when(k <= me)
        def _(k=k):
            in_ref[0] = in_ref[0] * jnp.exp2(totals[k, 0:1, :]) + ends[k].astype(f32)

    for k in range(1, seq_count):

        @pl.when(k > me)
        def _(k=k):
            in_ref[1] = in_ref[1] * jnp.exp2(totals[k, 0:1, :]) + ends[k].astype(f32)

    for copy in (t2, t4, t5):
        copy.wait_recv()
    for copy in started:
        copy.wait_send()


def exchange(mesh_shape, end, total, hop):
    seq_count, head_count = mesh_shape
    return pl.pallas_call(
        functools.partial(exchange_kernel, seq_count, head_count),
        in_specs=[whole(end.shape), whole(total.shape), ANY_SPEC],
        out_specs=[whole(end.shape), ANY_SPEC],
        out_shape=[
            jax.ShapeDtypeStruct(end.shape, f32),
            jax.ShapeDtypeStruct((4,) + hop.shape[1:], bf16),
        ],
        scratch_shapes=[
            pltpu.VMEM((seq_count,) + end.shape[1:], bf16),
            pltpu.VMEM((seq_count,) + total.shape, f32),
            pltpu.SemaphoreType.DMA((seq_count,)),
            pltpu.SemaphoreType.DMA((seq_count,)),
            pltpu.SemaphoreType.DMA((seq_count,)),
            pltpu.SemaphoreType.DMA((seq_count,)),
            pltpu.SemaphoreType.DMA((5,)),
            pltpu.SemaphoreType.DMA((5,)),
        ],
        compiler_params=params(collective_id=0, has_side_effects=True),
        name="exchange",
    )(end, total, hop)


def split(x, parts):
    pieces = []
    for _ in range(parts - 1):
        pieces.append(x.astype(bf16).astype(f32))
        x = x - pieces[-1]
    return pieces + [x]


def outputs_kernel(
    conv_ref, gate_ref, cols_ref, row_ref, fresh_ref, in_ref, skip_ref, gf_ref, gb_ref, ss_ref, entry, pick
):
    g = pl.program_id(0)
    chunks = fresh_ref.shape[0]
    inner = gate_ref.shape[1]
    mixed = conv_ref.shape[1] // 2
    group = conv_ref.shape[0] // CHUNK

    @pl.when(g == 0)
    def _():
        def passing(c):
            return jnp.exp2(head_lanes([cols_ref[c, h : h + 1, CHUNK - 1 :] for h in range(4)]))

        def forward(c, state):
            entry[0, c] = state.astype(bf16)
            return state * passing(c) + fresh_ref[c, 0].astype(f32)

        def backward(i, state):
            c = chunks - 1 - i
            entry[1, c] = state.astype(bf16)
            return state * passing(c) + fresh_ref[c, 1].astype(f32)

        lax.fori_loop(0, chunks, forward, in_ref[0])
        lax.fori_loop(0, chunks, backward, in_ref[1])
        line = lax.broadcasted_iota(jnp.int32, pick.shape[1:], 0)
        lane = lax.broadcasted_iota(jnp.int32, pick.shape[1:], 1)
        block = lane // CHUNK
        sign = jnp.where(block < 4, 1.0, -1.0)
        spot = lane - 8 * CHUNK
        wanted = (spot // inner) * 8 + (spot % inner) // HEAD_DIM
        chosen = jnp.where((line < 24) & (block < 8) & (line % 8 == block), sign, 0.0)
        opened = (line >= 64) & (block >= 8) & (line % 16 == wanted)
        for q in range(group):
            pick[q] = jnp.where(opened, 1.0, chosen).astype(bf16)

    i = lax.broadcasted_iota(jnp.int32, (CHUNK, CHUNK), 0)
    j = lax.broadcasted_iota(jnp.int32, (CHUNK, CHUNK), 1)
    lower = i >= j
    upper = i <= j
    low = j < HEAD_DIM
    skip = head_lanes([jnp.full((1, 1), skip_ref[h], f32) for h in range(4)])
    sub = lax.broadcasted_iota(jnp.int32, (8, CHUNK), 0)
    ones = jnp.ones((8, inner), bf16)
    sums = jnp.zeros((8, CHUNK), f32)
    for q in range(group):
        c = g * group + q
        rows = slice(q * CHUNK, (q + 1) * CHUNK)
        cols = cols_ref[c]
        row = row_ref[c]
        lines = jnp.concatenate(split(jnp.where(sub < 4, -row, row), 3), axis=0)
        for block in range(8):
            own = lax.broadcasted_iota(jnp.int32, lines.shape, 0) % 8 == block
            pick[q, 32:56, block * CHUNK : (block + 1) * CHUNK] = jnp.where(own, lines, 0.0).astype(
                bf16
            )
        left = jnp.concatenate(
            split(cols[0:8], 3)
            + [jnp.zeros((8, CHUNK), f32), jnp.ones((24, CHUNK), f32), jnp.zeros((8, CHUNK), f32)]
            + split(cols[8:24], 2),
            axis=0,
        ).astype(bf16)
        made = mm(left, pick[q], TN)
        pair = []
        for d, keep in ((0, lower), (1, upper)):
            base = d * mixed + inner
            write = conv_ref[rows, base : base + STATE]
            read = conv_ref[rows, base + STATE : base + 2 * STATE]
            pair.append(jnp.where(keep, mm(read, write, NT), 0.0))
        weights = ([], [])
        for h in range(4):
            arg = jnp.where(
                lower,
                made[:, h * CHUNK : (h + 1) * CHUNK],
                made[:, (4 + h) * CHUNK : (5 + h) * CHUNK],
            )
            table = jnp.exp2(arg)
            for d in range(2):
                weights[d].append((pair[d] * table).astype(bf16))
        gate = silu(gate_ref[rows, :].astype(f32))
        for d, out_ref in ((0, gf_ref), (1, gb_ref)):
            x = conv_ref[rows, d * mixed : d * mixed + inner]
            read = conv_ref[rows, d * mixed + inner + STATE : (d + 1) * mixed]
            local = []
            for p in range(2):
                half = x[:, p * CHUNK : (p + 1) * CHUNK]
                zero = jnp.zeros_like(half)
                stacked = jnp.concatenate(
                    [jnp.where(low, half, zero), jnp.where(low, zero, half)], axis=0
                )
                both = jnp.concatenate(weights[d][2 * p : 2 * p + 2], axis=1)
                local.append(mm(both, stacked))
            carried = mm(read, entry[d, c])
            at = 8 * CHUNK + d * inner
            scale = made[:, at : at + inner]
            out = jnp.concatenate(local, axis=1) + carried * scale + skip * x.astype(f32)
            gated = out * gate
            out_ref[rows, :] = gated.astype(bf16)
            square = mm(ones, (gated * gated).astype(bf16), NT)
            sums = jnp.where(sub == 2 * q + d, square, sums)
    ss_ref[...] = sums


def outputs(conv, gate, cols, row, fresh, incoming, skip):
    tokens, inner = gate.shape
    chunks = tokens // CHUNK
    rows = 4 * CHUNK
    return pl.pallas_call(
        outputs_kernel,
        grid=(tokens // rows,),
        in_specs=[
            pl.BlockSpec((rows, conv.shape[1]), lambda g: (g, 0)),
            pl.BlockSpec((rows, inner), lambda g: (g, 0)),
            whole(cols.shape),
            whole(row.shape),
            whole(fresh.shape),
            whole(incoming.shape),
            SMEM_SPEC,
        ],
        out_specs=[
            pl.BlockSpec((rows, inner), lambda g: (g, 0)),
            pl.BlockSpec((rows, inner), lambda g: (g, 0)),
            pl.BlockSpec((8, CHUNK), lambda g: (g, 0)),
        ],
        out_shape=[
            jax.ShapeDtypeStruct((tokens, inner), bf16),
            jax.ShapeDtypeStruct((tokens, inner), bf16),
            jax.ShapeDtypeStruct((2 * chunks, CHUNK), f32),
        ],
        scratch_shapes=[
            pltpu.VMEM((2, chunks, STATE, inner), bf16),
            pltpu.VMEM((4, 96, 8 * CHUNK + 2 * inner), bf16),
        ],
        compiler_params=params(),
        name="outputs",
    )(conv, gate, cols, row, fresh, incoming, skip)


def finish_kernel(
    head_count,
    gf_ref,
    gb_ref,
    ss_ref,
    gain_ref,
    hidden_ref,
    w_ref,
    hop_ref,
    far_ref,
    out_ref,
    sums,
    sending,
    arrived,
    total,
    rest,
    ss_send,
    ss_recv,
    send,
    recv,
    load,
):
    me = lax.axis_index("head")
    chips = head_count // 2
    inner = gain_ref.shape[0]
    rows = out_ref.shape[0]
    lines = ss_ref.shape[0] // head_count
    slots = [(dy, dc) for dy in range(chips) for dc in range(2)]
    peers = [head_peer(me, chips, dy, dc) for dy, dc in slots]
    residual = pltpu.make_async_copy(
        hidden_ref.at[pl.ds(pl.multiple_of(me * rows, rows), rows), :], rest, load
    )
    residual.start()
    greet([{"head": p} for p in peers[1:]])
    started = []
    for k in range(1, head_count):
        copy = remote(ss_ref, sums.at[k], ss_send.at[k], ss_recv.at[k], head=peers[k])
        copy.start()
        started.append(copy)
    for copy in started:
        copy.wait_recv()
    squares = ss_ref[...]
    for k in range(1, head_count):
        squares = squares + sums[k]
    total[...] = lax.rsqrt(squares * (1.0 / (inner * head_count)) + epsilon)
    gain = gain_ref[...].reshape(1, -1).astype(f32)

    def combine(owner, slot):
        scale = total[pl.ds(pl.multiple_of(owner * lines, lines), lines), :]
        scale = jnp.concatenate([scale, jnp.zeros((CHUNK - lines, CHUNK), f32)], axis=0).T
        for q in range(rows // CHUNK):
            at = pl.ds(pl.multiple_of(owner * rows + q * CHUNK, CHUNK), CHUNK)
            both = gf_ref[at, :].astype(f32) * scale[:, 2 * q : 2 * q + 1]
            both = both + gb_ref[at, :].astype(f32) * scale[:, 2 * q + 1 : 2 * q + 2]
            sending[slot, q * CHUNK : (q + 1) * CHUNK, :] = (both * gain).astype(bf16)

    order = sorted(range(1, head_count), key=lambda k: -min(slots[k][0], chips - slots[k][0]))
    copies = []
    for k in order:
        combine(peers[k], k)
        copy = remote(sending.at[k], arrived.at[k], send.at[k], recv.at[k], head=peers[k])
        copy.start()
        copies.append(copy)
    combine(me, 0)
    residual.wait()
    step = 256

    def add(rows_in, weight, first):
        for b in range(out_ref.shape[1] // step):
            lanes = slice(b * step, (b + 1) * step)
            term = mm(rows_in, weight[:, lanes])
            if first:
                rest_wide[:, lanes] = rest[:, lanes].astype(f32) + term
            else:
                rest_wide[:, lanes] = rest_wide[:, lanes] + term

    held = {
        1: hop_ref.at[2],
        2: hop_ref.at[0],
        3: far_ref.at[0],
        head_count - 2: hop_ref.at[1],
        head_count - 1: far_ref.at[1],
        4: far_ref.at[2],
        5: far_ref.at[3],
    }

    def body(rest_wide_ref):
        nonlocal rest_wide
        rest_wide = rest_wide_ref
        add(sending[0], w_ref[...], True)
        for copy, k in reversed(list(zip(copies, order))):
            copy.wait_recv()
            add(arrived[k], held[k], False)
        out_ref[...] = rest_wide_ref[...].astype(bf16)

    rest_wide = None
    pl.run_scoped(body, pltpu.VMEM(out_ref.shape, f32))
    for copy in started + copies:
        copy.wait_send()


def finish(head_count, gf, gb, ss, gain, hidden, w, hop, far):
    tokens, inner = gf.shape
    rows = tokens // head_count
    width = hidden.shape[1]
    return pl.pallas_call(
        functools.partial(finish_kernel, head_count),
        in_specs=[
            whole(gf.shape),
            whole(gb.shape),
            whole(ss.shape),
            whole(gain.shape),
            ANY_SPEC,
            whole(w.shape),
            whole(hop.shape),
            whole(far.shape),
        ],
        out_specs=whole((rows, width)),
        out_shape=jax.ShapeDtypeStruct((rows, width), bf16),
        scratch_shapes=[
            pltpu.VMEM((head_count,) + ss.shape, f32),
            pltpu.VMEM((head_count, rows, inner), bf16),
            pltpu.VMEM((head_count, rows, inner), bf16),
            pltpu.VMEM(ss.shape, f32),
            pltpu.VMEM((rows, width), bf16),
            pltpu.SemaphoreType.DMA((head_count,)),
            pltpu.SemaphoreType.DMA((head_count,)),
            pltpu.SemaphoreType.DMA((head_count,)),
            pltpu.SemaphoreType.DMA((head_count,)),
            pltpu.SemaphoreType.DMA,
        ],
        compiler_params=params(collective_id=1, has_side_effects=True),
        name="finish",
    )(gf, gb, ss, gain, hidden, w, hop, far)


def local(
    hidden_in,
    norm_gain,
    gate_weight,
    value_weight,
    state_weight,
    step_weight,
    step_bias,
    decay_log,
    skip_gain,
    conv_value,
    conv_state,
    output_gain,
    output_weight,
    piece_lengths,
):
    seq_count, head_count = lax.axis_size("seq"), lax.axis_size("head")
    shape = (seq_count, head_count)
    gate, mix, raw, halo, hop = project(
        shape, hidden_in, norm_gain, gate_weight, value_weight, state_weight, step_weight, output_weight
    )
    conv, fresh, cols, row, end, total = states(
        "seq",
        mix,
        halo,
        norm_gain,
        value_weight,
        state_weight,
        raw,
        piece_lengths,
        step_bias,
        decay_log,
        conv_value,
        conv_state,
    )
    incoming, far = exchange(shape, end, total, hop)
    gf, gb, ss = outputs(conv, gate, cols, row, fresh, incoming, skip_gain)
    return finish(head_count, gf, gb, ss, output_gain, hidden_in, output_weight, hop, far)


def solution(mesh):
    in_specs = (
        P("seq", None),
        P(),
        P(None, "head"),
        P(None, "head"),
        P(),
        P(None, "head"),
        P("head"),
        P("head"),
        P("head"),
        P(None, "head"),
        P(),
        P("head"),
        P("head", None),
        P(),
    )
    out_specs = P(("seq", "head"), None)
    return jax.shard_map(local, mesh=mesh, in_specs=in_specs, out_specs=out_specs, check_vma=False)
```

```python
import functools
import math

import jax
import jax.numpy as jnp
from jax import lax
from jax.experimental import pallas as pl
from jax.experimental.pallas import tpu as pltpu
from jax.sharding import PartitionSpec as P

HEAD_DIM = 64
STATE = 128
CONV = 4
CHUNK = 128
PIECES = 16
HALO = 16
REACH = 8
RESET = 256.0
LOG2E = math.log2(math.e)

f32 = jnp.float32
bf16 = jnp.bfloat16
epsilon = 1e-05
MESH = pl.DeviceIdType.MESH
NN = (((1,), (0,)), ((), ()))
NT = (((1,), (1,)), ((), ()))
TN = (((0,), (0,)), ((), ()))


def mm(a, b, dims=NN, precision=None):
    return lax.dot_general(a, b, dims, precision=precision, preferred_element_type=f32)


def silu(x):
    half = 0.5 * x
    return half * jnp.tanh(half) + half


def normalized(h, gain):
    wide = h.astype(f32)
    scale = lax.rsqrt(jnp.mean(wide * wide, axis=1, keepdims=True) + epsilon)
    return (wide * scale * gain.astype(f32)).astype(bf16)


def whole(shape):
    zeros = (0,) * len(shape)
    return pl.BlockSpec(shape, lambda *_: zeros)


SMEM_SPEC = pl.BlockSpec(memory_space=pltpu.SMEM)
ANY_SPEC = pl.BlockSpec(memory_space=pl.ANY)


def params(**kw):
    return pltpu.CompilerParams(vmem_limit_bytes=60 * 1024 * 1024, **kw)


def remote(src, dst, send, recv, **where):
    return pltpu.make_async_remote_copy(
        src_ref=src,
        dst_ref=dst,
        send_sem=send,
        recv_sem=recv,
        device_id=where,
        device_id_type=MESH,
    )


def greet(axes_and_peers):
    barrier = pltpu.get_barrier_semaphore()
    for where in axes_and_peers:
        pl.semaphore_signal(barrier, inc=1, device_id=where, device_id_type=MESH)
    pl.semaphore_wait(barrier, len(axes_and_peers))


def head_peer(me, chips, dy, dc):
    y, core = me // 2, me % 2
    return ((y + dy) % chips) * 2 + (core + dc) % 2


def project_copies(seq_count, head_count, hidden, w, halo, hop, send, recv):
    me = lax.axis_index("seq")
    head = lax.axis_index("head")
    chips = head_count // 2
    tokens = hidden.shape[0]
    after = (me + 1) % seq_count
    before = (me + seq_count - 1) % seq_count
    first, last = pl.ds(0, HALO), pl.ds(tokens - HALO, HALO)
    low, high = pl.ds(0, HALO), pl.ds(HALO, HALO)
    up = head_peer(head, chips, 1, 0)
    down = head_peer(head, chips, chips - 1, 0)
    partner = head_peer(head, chips, 0, 1)
    return (
        remote(hidden.at[last], halo.at[low], send.at[0], recv.at[0], seq=after),
        remote(hidden.at[first], halo.at[high], send.at[1], recv.at[1], seq=before),
        remote(w, hop.at[0], send.at[2], recv.at[2], head=up),
        remote(w, hop.at[1], send.at[3], recv.at[3], head=down),
        remote(w, hop.at[2], send.at[4], recv.at[4], head=partner),
    ), [{"seq": after}, {"seq": before}, {"head": up}, {"head": down}, {"head": partner}]


def project_kernel(
    mesh_shape,
    h_ref,
    gain_ref,
    gw_ref,
    vw_ref,
    sw_ref,
    tw_ref,
    hidden,
    w,
    gate_ref,
    mix_ref,
    raw_ref,
    halo,
    hop,
    turned,
    send,
    recv,
):
    i = pl.program_id(0)
    copies, peers = project_copies(*mesh_shape, hidden, w, halo, hop, send, recv)
    barrier = pltpu.get_barrier_semaphore()

    @pl.when(i == 0)
    def _():
        for where in peers:
            pl.semaphore_signal(barrier, inc=1, device_id=where, device_id_type=MESH)
        narrow = tw_ref[...].astype(f32)
        depth, few = narrow.shape
        padded = jnp.concatenate(
            [narrow, narrow, jnp.zeros((depth, CHUNK - 2 * few), f32)], axis=1
        )
        turned[...] = padded.T[:8].astype(bf16)

    @pl.when(i == 1)
    def _():
        pl.semaphore_wait(barrier, len(peers))
        for copy in copies:
            copy.start()

    inner = vw_ref.shape[1]
    n = normalized(h_ref[...], gain_ref[...].reshape(1, -1))
    gate = mm(n, gw_ref[...]).astype(bf16)
    for q in range(gate_ref.shape[0]):
        gate_ref[q, 0] = gate[q * CHUNK : (q + 1) * CHUNK]
    mix_ref[:, :inner] = mm(n, vw_ref[...]).astype(bf16)
    mix_ref[:, inner:] = mm(n, sw_ref[...]).astype(bf16)
    raw = mm(turned[...], n, NT)
    for q in range(raw.shape[1] // CHUNK):
        raw_ref[q] = raw[:, q * CHUNK : (q + 1) * CHUNK]

    @pl.when(i == pl.num_programs(0) - 1)
    def _():
        for copy in copies:
            copy.wait()


def project(mesh_shape, hidden, gain, gw, vw, sw, tw, w):
    tokens, width = hidden.shape
    inner = vw.shape[1]
    mixed = inner + sw.shape[1]
    rows = tokens // mesh_shape[1]
    rounds = rows // CHUNK
    return pl.pallas_call(
        functools.partial(project_kernel, mesh_shape),
        grid=(tokens // rows,),
        in_specs=[
            pl.BlockSpec((rows, width), lambda i: (i, 0)),
            whole(gain.shape),
            whole(gw.shape),
            whole(vw.shape),
            whole(sw.shape),
            whole(tw.shape),
            ANY_SPEC,
            ANY_SPEC,
        ],
        out_specs=[
            pl.BlockSpec((rounds, 1, CHUNK, inner), lambda i: (0, i, 0, 0)),
            pl.BlockSpec((rows, mixed), lambda i: (i, 0)),
            pl.BlockSpec((rows // CHUNK, 8, CHUNK), lambda i: (i, 0, 0)),
            ANY_SPEC,
            ANY_SPEC,
        ],
        out_shape=[
            jax.ShapeDtypeStruct((rounds, tokens // rows, CHUNK, inner), bf16),
            jax.ShapeDtypeStruct((tokens, mixed), bf16),
            jax.ShapeDtypeStruct((tokens // CHUNK, 8, CHUNK), f32),
            jax.ShapeDtypeStruct((2 * HALO, width), bf16),
            jax.ShapeDtypeStruct((3,) + w.shape, bf16),
        ],
        scratch_shapes=[
            pltpu.VMEM((8, width), bf16),
            pltpu.SemaphoreType.DMA((5,)),
            pltpu.SemaphoreType.DMA((5,)),
        ],
        compiler_params=params(collective_id=2, has_side_effects=True),
        name="project",
    )(hidden, gain, gw, vw, sw, tw, hidden, w)


def head_lanes(columns):
    low = lax.broadcasted_iota(jnp.int32, (columns[0].shape[0], 2 * HEAD_DIM), 1) < HEAD_DIM
    pairs = [
        jnp.where(low, columns[2 * p], columns[2 * p + 1]) for p in range(len(columns) // 2)
    ]
    return jnp.concatenate(pairs, axis=1)


def decays(first_row, raw, lens_ref, bias_ref, rate_ref):
    chunks = raw.shape[0]
    shape = (chunks, 8, CHUNK)
    sub = lax.broadcasted_iota(jnp.int32, shape, 1)
    upper = sub < 4
    head = jnp.where(upper, sub, sub - 4)
    pos = (
        first_row
        + lax.broadcasted_iota(jnp.int32, shape, 0) * CHUNK
        + lax.broadcasted_iota(jnp.int32, shape, 2)
    )
    start = jnp.zeros(shape, jnp.int32)
    stop = jnp.full(shape, 1 << 30, jnp.int32)
    edge = jnp.int32(0)
    for k in range(PIECES):
        start = jnp.where(pos >= edge, edge, start)
        edge = edge + lens_ref[k]
        stop = jnp.minimum(stop, jnp.where(edge > pos, edge, 1 << 30))
    since = pos - start
    until = stop - 1 - pos
    bias = jnp.zeros(shape, f32)
    rate = jnp.zeros(shape, f32)
    for h in range(4):
        bias = jnp.where(head == h, bias_ref[h], bias)
        rate = jnp.where(head == h, rate_ref[h], rate)
    rate = jnp.exp(rate) * (-LOG2E)
    z = raw + bias
    step = jnp.maximum(z, 0.0) + jnp.log1p(jnp.exp(-jnp.abs(z)))
    log = step * rate
    reset = jnp.where(since == 0, -RESET, 0.0)
    ones = (
        lax.broadcasted_iota(jnp.int32, (CHUNK, CHUNK), 0)
        <= lax.broadcasted_iota(jnp.int32, (CHUNK, CHUNK), 1)
    ).astype(f32)
    cum = mm(
        (log + reset).reshape(chunks * 8, CHUNK), ones, precision=lax.Precision.HIGHEST
    ).reshape(shape)
    excl = cum - log
    total = cum[:, :, CHUNK - 1 :]
    log_step = jnp.where(step > 0.0, jnp.log2(step), -RESET)
    row = jnp.where(upper, cum - log_step, excl + log_step)
    g1 = jnp.where(upper, cum, excl)
    g2 = jnp.where(upper, jnp.exp2(cum), jnp.exp2(total - cum) * step)
    g3 = jnp.where(upper, jnp.exp2(total - excl), jnp.exp2(excl) * step)
    g4 = jnp.where(upper, since, until).astype(f32)
    return row, g1, g2, g3, g4


def states_kernel(
    axis,
    mix_ref,
    before_ref,
    after_ref,
    halo_ref,
    gain_ref,
    vw_ref,
    sw_ref,
    raw_ref,
    lens_ref,
    bias_ref,
    rate_ref,
    cv_ref,
    cs_ref,
    conv_ref,
    fresh_ref,
    cols_ref,
    row_ref,
    end_ref,
    total_ref,
    prod,
    halo,
    run,
    reach,
    spread,
    near,
):
    c = pl.program_id(0)
    count = pl.num_programs(0)
    inner = vw_ref.shape[1]
    mixed = mix_ref.shape[1]
    blocks = mixed // 128
    first_row = lax.axis_index(axis) * (count * CHUNK)

    @pl.when(c == 0)
    def _():
        n = normalized(halo_ref[...], gain_ref[...].reshape(1, -1))
        halo[:, :inner] = mm(n, vw_ref[...]).astype(bf16).astype(f32)
        halo[:, inner:] = mm(n, sw_ref[...]).astype(bf16).astype(f32)
        row, g1, g2, g3, g4 = decays(first_row, raw_ref[...], lens_ref, bias_ref, rate_ref)
        row_ref[...] = row
        cols_ref[:, 0:8, :] = g1
        cols_ref[:, 8:16, :] = g2
        cols_ref[:, 16:24, :] = g3
        cols_ref[:, 24:32, :] = g4
        run[...] = jnp.zeros_like(run)
        reach[...] = jnp.zeros_like(reach)
        line = lax.broadcasted_iota(jnp.int32, spread.shape, 0) % 32
        lane = lax.broadcasted_iota(jnp.int32, spread.shape, 1)
        wanted = 12 + (lane // inner) * 8 + (lane % inner) // HEAD_DIM
        spread[...] = (line == wanted).astype(f32).astype(bf16)

        def clear(k, carry):
            near[k] = 0
            return carry

        lax.fori_loop(0, near.shape[0], clear, 0)

        def mark(k, edge):
            for shift in (-(CONV - 1), CONV - 2):
                at = (edge + shift - first_row + CHUNK) // CHUNK
                near[jnp.clip(at, 0, near.shape[0] - 1)] = 1
            return edge + lens_ref[jnp.minimum(k, PIECES - 1)]

        lax.fori_loop(0, PIECES + 1, mark, jnp.int32(0))

    taps = jnp.concatenate([cv_ref[...], cs_ref[...]], axis=1).astype(f32)
    here = slice(REACH, REACH + CHUNK)

    def put(rows, values):
        for k in range(CONV - 1):
            for b in range(blocks):
                lanes = slice(b * 128, (b + 1) * 128)
                prod[k, b, rows, :] = values[:, lanes] * taps[k : k + 1, lanes]

    put(here, mix_ref[...].astype(f32))
    ahead, behind = slice(0, REACH), slice(REACH + CHUNK, 2 * REACH + CHUNK)

    @pl.when(c == 0)
    def _():
        put(ahead, halo[HALO - REACH : HALO, :])

    @pl.when(c > 0)
    def _():
        put(ahead, before_ref[...].astype(f32)[16 - REACH :, :])

    @pl.when(c == count - 1)
    def _():
        put(behind, halo[HALO : HALO + REACH, :])

    @pl.when(c < count - 1)
    def _():
        put(behind, after_ref[...].astype(f32)[:REACH, :])

    cols = cols_ref[c]

    def convolve(masked):
        if masked:
            turned = jnp.concatenate([cols, jnp.zeros((CHUNK - 32, CHUNK), f32)], axis=0).T
            sides = [jnp.broadcast_to(turned[:, r : r + 1], (CHUNK, 128)) for r in (24, 28)]
        for b in range(blocks):
            lanes = slice(b * 128, (b + 1) * 128)
            centre = mix_ref[:, lanes].astype(f32) * taps[CONV - 1 : CONV, lanes]
            for d in range(2):
                total = centre
                for distance in range(1, CONV):
                    at = REACH + distance if d else REACH - distance
                    term = prod[CONV - 1 - distance, b, at : at + CHUNK, :]
                    if masked:
                        term = jnp.where(sides[d] >= distance, term, 0.0)
                    total = total + term
                at = d * mixed + b * 128
                conv_ref[0, 0, :, at : at + 128] = silu(total).astype(bf16)

    edges = near[c + 1]

    @pl.when(edges == 0)
    def _():
        convolve(False)

    @pl.when(edges != 0)
    def _():
        convolve(True)

    high = cols.astype(bf16).astype(f32)
    both = jnp.concatenate([high, cols - high], axis=0).astype(bf16)
    tails = mm(both, spread[...], TN)
    passing = head_lanes([cols[h : h + 1, CHUNK - 1 :] for h in range(4)])
    for d in range(2):
        x = conv_ref[0, 0, :, d * mixed : d * mixed + inner].astype(f32)
        write = conv_ref[0, 0, :, d * mixed + inner : d * mixed + inner + STATE]
        scaled = (x * tails[:, d * inner : (d + 1) * inner]).astype(bf16)
        fresh = mm(write, scaled, TN)
        fresh_ref[0, d] = fresh.astype(bf16)
        if d == 0:
            run[0] = run[0] * jnp.exp2(passing) + fresh
        else:
            run[1] = run[1] + jnp.exp2(reach[0:1, :]) * fresh
    reach[...] = reach[...] + passing

    @pl.when(c == count - 1)
    def _():
        end_ref[...] = run[...].astype(bf16)
        total_ref[...] = reach[...]


def states(axis, owners, mix, halo, gain, vw, sw, raw, lens, bias, rate, cv, cs):
    tokens, mixed = mix.shape
    chunks = tokens // CHUNK
    inner = vw.shape[1]
    rounds = chunks // owners
    per = CHUNK // 16
    last = tokens // 16 - 1
    return pl.pallas_call(
        functools.partial(states_kernel, axis),
        grid=(chunks,),
        in_specs=[
            pl.BlockSpec((CHUNK, mixed), lambda c: (c, 0)),
            pl.BlockSpec((16, mixed), lambda c: (jnp.maximum(c * per - 1, 0), 0)),
            pl.BlockSpec((16, mixed), lambda c: (jnp.minimum(c * per + per, last), 0)),
            whole(halo.shape),
            whole(gain.shape),
            whole(vw.shape),
            whole(sw.shape),
            whole(raw.shape),
            SMEM_SPEC,
            SMEM_SPEC,
            SMEM_SPEC,
            whole(cv.shape),
            whole(cs.shape),
        ],
        out_specs=[
            pl.BlockSpec((1, 1, CHUNK, 2 * mixed), lambda c: (c % rounds, c // rounds, 0, 0)),
            pl.BlockSpec((1, 2, STATE, inner), lambda c: (c, 0, 0, 0)),
            whole((chunks, 32, CHUNK)),
            whole((chunks, 8, CHUNK)),
            whole((2, STATE, inner)),
            whole((8, inner)),
        ],
        out_shape=[
            jax.ShapeDtypeStruct((rounds, owners, CHUNK, 2 * mixed), bf16),
            jax.ShapeDtypeStruct((chunks, 2, STATE, inner), bf16),
            jax.ShapeDtypeStruct((chunks, 32, CHUNK), f32),
            jax.ShapeDtypeStruct((chunks, 8, CHUNK), f32),
            jax.ShapeDtypeStruct((2, STATE, inner), bf16),
            jax.ShapeDtypeStruct((8, inner), f32),
        ],
        scratch_shapes=[
            pltpu.VMEM((CONV - 1, mixed // 128, CHUNK + 2 * REACH, 128), f32),
            pltpu.VMEM((2 * HALO, mixed), f32),
            pltpu.VMEM((2, STATE, inner), f32),
            pltpu.VMEM((8, inner), f32),
            pltpu.VMEM((64, 2 * inner), bf16),
            pltpu.SMEM((chunks + 2,), jnp.int32),
        ],
        compiler_params=params(),
        name="states",
    )(mix, mix, mix, halo, gain, vw, sw, raw, lens, bias, rate, cv, cs)


def split(x, parts):
    pieces = []
    for _ in range(parts - 1):
        pieces.append(x.astype(bf16).astype(f32))
        x = x - pieces[-1]
    return pieces + [x]


def finish_kernel(
    seq_count,
    head_count,
    end_ref,
    total_ref,
    cols_ref,
    row_ref,
    skip_ref,
    gain_ref,
    conv_hbm,
    gate_hbm,
    fresh_hbm,
    hidden_hbm,
    w_hbm,
    hop_hbm,
    out_ref,
    conv,
    gate,
    fresh,
    rest,
    weight,
    ends,
    totals,
    incoming,
    entry,
    pick,
    spread,
    inside,
    gated,
    squares,
    others,
    scales,
    sending,
    arrived,
    load,
    seq_send,
    seq_recv,
    w_send,
    w_recv,
    ss_send,
    ss_recv,
    send,
    recv,
):
    me = lax.axis_index("seq")
    head = lax.axis_index("head")
    chips = head_count // 2
    rounds, owners = conv.shape[0], conv.shape[1]
    chunks = rounds * owners
    inner = gate.shape[3]
    mixed = conv.shape[3] // 2
    rows = rounds * CHUNK
    slots = [(dy, dc) for dy in range(chips) for dc in range(2)]
    peers = [head_peer(head, chips, dy, dc) for dy, dc in slots]
    up, down, partner = peers[2], peers[2 * chips - 2], peers[1]

    def fetch(src, dst, n):
        copy = pltpu.make_async_copy(src, dst, load.at[n])
        copy.start()
        return copy

    def part(k):
        return pl.ds(k * inner, inner)

    conv_in = [fetch(conv_hbm.at[q], conv.at[q], q) for q in range(rounds)]
    fresh_in = fetch(fresh_hbm, fresh, rounds)
    gate_in = fetch(gate_hbm, gate, rounds + 1)
    mine = pl.ds(pl.multiple_of(head * rows, rows), rows)
    late = [
        fetch(hidden_hbm.at[mine, :], rest, rounds + 2),
        fetch(w_hbm, weight.at[part(0)], rounds + 3),
        fetch(hop_hbm.at[2], weight.at[part(1)], rounds + 4),
        fetch(hop_hbm.at[0], weight.at[part(2)], rounds + 5),
        fetch(hop_hbm.at[1], weight.at[part(2 * chips - 2)], rounds + 6),
    ]

    greet(
        [{"seq": (me + k) % seq_count} for k in range(1, seq_count)]
        + [{"head": p} for p in peers[1:]]
    )
    started = []

    def start(copy):
        copy.start()
        started.append(copy)
        return copy

    travelling = []
    for k in range(1, seq_count):
        target = (me + k) % seq_count
        backward = (me + k) // seq_count
        travelling.append(
            start(
                remote(
                    end_ref.at[backward], ends.at[k], seq_send.at[0, k], seq_recv.at[0, k], seq=target
                )
            )
        )
        travelling.append(
            start(remote(total_ref, totals.at[k], seq_send.at[1, k], seq_recv.at[1, k], seq=target))
        )
    half = inner // 2
    far = 4 * inner
    top, bottom = pl.ds(0, half), pl.ds(half, half)
    t1 = start(
        remote(
            hop_hbm.at[0, top], weight.at[pl.ds(far, half)], w_send.at[0], w_recv.at[0], head=up
        )
    )
    t3 = start(
        remote(
            hop_hbm.at[1, bottom],
            weight.at[pl.ds(far + half, half)],
            w_send.at[1],
            w_recv.at[1],
            head=down,
        )
    )
    t2 = start(remote(hop_hbm.at[0], weight.at[part(3)], w_send.at[2], w_recv.at[2], head=partner))
    t4 = start(
        remote(hop_hbm.at[1], weight.at[part(2 * chips - 1)], w_send.at[3], w_recv.at[3], head=partner)
    )

    i = lax.broadcasted_iota(jnp.int32, (CHUNK, CHUNK), 0)
    j = lax.broadcasted_iota(jnp.int32, (CHUNK, CHUNK), 1)
    lower = i >= j
    upper = i <= j
    low = j < HEAD_DIM
    skip = head_lanes([jnp.full((1, 1), skip_ref[h], f32) for h in range(4)])
    sub = lax.broadcasted_iota(jnp.int32, (8, CHUNK), 0)
    line = lax.broadcasted_iota(jnp.int32, pick.shape[1:], 0)
    block = lax.broadcasted_iota(jnp.int32, pick.shape[1:], 1) // CHUNK
    sign = jnp.where(block < 4, 1.0, -1.0)
    chosen = jnp.where((line < 24) & (line % 8 == block), sign, 0.0).astype(bf16)
    for u in range(pick.shape[0]):
        pick[u] = chosen
    line = lax.broadcasted_iota(jnp.int32, spread.shape, 0)
    lane = lax.broadcasted_iota(jnp.int32, spread.shape, 1)
    wanted = (lane // inner) * 8 + (lane % inner) // HEAD_DIM
    spread[...] = (line % 16 == wanted).astype(f32).astype(bf16)

    def within(q, d, u):
        c = d * rounds + q
        row = row_ref[c]
        lines = jnp.concatenate(split(jnp.where(sub < 4, -row, row), 3), axis=0)
        for n in range(8):
            own = lax.broadcasted_iota(jnp.int32, lines.shape, 0) % 8 == n
            pick[u, 32:56, n * CHUNK : (n + 1) * CHUNK] = jnp.where(own, lines, 0.0).astype(bf16)
        left = jnp.concatenate(
            split(cols_ref[c, 0:8, :], 3)
            + [jnp.zeros((8, CHUNK), f32), jnp.ones((24, CHUNK), f32), jnp.zeros((8, CHUNK), f32)],
            axis=0,
        ).astype(bf16)
        made = mm(left, pick[u], TN)
        pair = []
        for e, keep in ((0, lower), (1, upper)):
            base = e * mixed + inner
            write = conv[q, d, :, base : base + STATE]
            read = conv[q, d, :, base + STATE : base + 2 * STATE]
            pair.append(jnp.where(keep, mm(read, write, NT), 0.0))
        for p in range(2):
            weights = ([], [])
            for h in (2 * p, 2 * p + 1):
                table = jnp.exp2(
                    jnp.where(
                        lower,
                        made[:, h * CHUNK : (h + 1) * CHUNK],
                        made[:, (4 + h) * CHUNK : (5 + h) * CHUNK],
                    )
                )
                for e in range(2):
                    weights[e].append((pair[e] * table).astype(bf16))
            for e in range(2):
                at = e * mixed + p * CHUNK
                x = conv[q, d, :, at : at + CHUNK]
                zero = jnp.zeros_like(x)
                stacked = jnp.concatenate([jnp.where(low, x, zero), jnp.where(low, zero, x)], axis=0)
                made_here = mm(jnp.concatenate(weights[e], axis=1), stacked)
                made_here = made_here + skip[:, p * CHUNK : (p + 1) * CHUNK] * x.astype(f32)
                inside[q, d, :, e * inner + p * CHUNK : e * inner + (p + 1) * CHUNK] = made_here

    for q in range(rounds):
        conv_in[q].wait()

        def step(n, carry, q=q):
            for u in range(2):
                within(q, 2 * n + u, u)
            return carry

        lax.fori_loop(0, owners // 2, step, 0)

    for copy in travelling:
        copy.wait_recv()
    t1.wait_recv()
    t3.wait_recv()
    t5 = start(
        remote(weight.at[part(4)], weight.at[part(5)], w_send.at[4], w_recv.at[4], head=partner)
    )
    incoming[...] = jnp.zeros_like(incoming)
    for k in range(seq_count - 1, 0, -1):

        @pl.when(k <= me)
        def _(k=k):
            incoming[0] = incoming[0] * jnp.exp2(totals[k, 0:1, :]) + ends[k].astype(f32)

    for k in range(1, seq_count):

        @pl.when(k > me)
        def _(k=k):
            incoming[1] = incoming[1] * jnp.exp2(totals[k, 0:1, :]) + ends[k].astype(f32)

    fresh_in.wait()

    def passing(c):
        return jnp.exp2(head_lanes([cols_ref[c, h : h + 1, CHUNK - 1 :] for h in range(4)]))

    def walk(c, carry):
        b = chunks - 1 - c
        for e, at in ((0, c), (1, b)):
            state = incoming[e]
            entry[e, at] = state.astype(bf16)
            incoming[e] = state * passing(at) + fresh[at, e].astype(f32)
        return carry

    lax.fori_loop(0, chunks, walk, 0)
    gate_in.wait()

    ones = jnp.ones((8, inner), bf16)
    gain = gain_ref[...].reshape(1, -1).astype(f32)
    sixteen = lax.broadcasted_iota(jnp.int32, (2 * owners, CHUNK), 0)

    def carried(q, d, sums):
        c = d * rounds + q
        left = jnp.concatenate(split(cols_ref[c, 8:24, :], 2), axis=0).astype(bf16)
        scale = mm(left, spread[...], TN)
        act = silu(gate[q, d].astype(f32))
        for e in range(2):
            at = e * mixed + inner + STATE
            lanes = slice(e * inner, (e + 1) * inner)
            part_in = mm(conv[q, d, :, at : at + STATE], entry[e, c])
            value = (inside[q, d, :, lanes] + part_in * scale[:, lanes]) * act
            gated[q, d, :, lanes] = value.astype(bf16)
            square = mm(ones, (value * value).astype(bf16), NT)
            square = jnp.concatenate([square] * (2 * owners // 8), axis=0)
            sums = jnp.where(sixteen == 2 * d + e, square, sums)
        return sums

    def combine(q):
        for k in range(1, head_count):
            ss[q][k - 1].wait_recv()
        total = squares[q]
        for k in range(1, head_count):
            total = total + others[q, k]
        total = lax.rsqrt(total * (1.0 / (inner * head_count)) + epsilon)
        for d in range(owners):
            scales[q, d, 0:2, :] = total[2 * d : 2 * d + 2, :]
        for k in range(head_count):
            d = peers[k]
            scale = jnp.concatenate(
                [scales[q, d, 0:2, :], jnp.zeros((CHUNK - 2, CHUNK), f32)], axis=0
            ).T
            both = gated[q, d, :, :inner].astype(f32) * scale[:, 0:1]
            both = both + gated[q, d, :, inner:].astype(f32) * scale[:, 1:2]
            both = (both * gain).astype(bf16)
            if k == 0:
                arrived[q * CHUNK : (q + 1) * CHUNK, 0:inner] = both
            else:
                sending[q, k] = both
        return [
            start(
                remote(
                    sending.at[q, k],
                    arrived.at[pl.ds(q * CHUNK, CHUNK), part(k)],
                    send.at[q, k],
                    recv.at[q, k],
                    head=peers[k],
                )
            )
            for k in sorted(range(1, head_count), key=lambda k: -min(slots[k][0], chips - slots[k][0]))
        ]

    ss, pieces = [], []
    for q in range(rounds):
        squares[q] = lax.fori_loop(
            0, owners, lambda d, sums, q=q: carried(q, d, sums), jnp.zeros((2 * owners, CHUNK), f32)
        )
        ss.append(
            [
                start(
                    remote(
                        squares.at[q], others.at[q, k], ss_send.at[q, k], ss_recv.at[q, k], head=peers[k]
                    )
                )
                for k in range(1, head_count)
            ]
        )
        if q:
            pieces.append(combine(q - 1))
    pieces.append(combine(rounds - 1))

    for copy in late:
        copy.wait()
    for copy in (t2, t4, t5):
        copy.wait_recv()
    width = out_ref.shape[1]
    step_lanes = 256
    early = (rounds - 1) * CHUNK
    for first, count, done in ((0, early, pieces[:-1]), (early, CHUNK, pieces[-1:])):
        for batch in done:
            for copy in batch:
                copy.wait_recv()
        if count:

            def project_out(b, carry, first=first, count=count):
                lanes = pl.ds(pl.multiple_of(b * step_lanes, step_lanes), step_lanes)
                here = pl.ds(first, count)
                out_ref[here, lanes] = (
                    mm(arrived[here, :], weight[:, lanes]) + rest[here, lanes].astype(f32)
                ).astype(bf16)
                return carry

            lax.fori_loop(0, width // step_lanes, project_out, 0)
    for copy in started:
        copy.wait_send()


def finish(mesh_shape, end, total, cols, row, skip, gain, conv, gate, fresh, hidden, w, hop):
    seq_count, head_count = mesh_shape
    rounds, owners = conv.shape[:2]
    rows = rounds * CHUNK
    inner = gate.shape[3]
    width = hidden.shape[1]
    dma = pltpu.SemaphoreType.DMA
    return pl.pallas_call(
        functools.partial(finish_kernel, seq_count, head_count),
        in_specs=[
            whole(end.shape),
            whole(total.shape),
            whole(cols.shape),
            whole(row.shape),
            SMEM_SPEC,
            whole(gain.shape),
        ]
        + [ANY_SPEC] * 6,
        out_specs=whole((rows, width)),
        out_shape=jax.ShapeDtypeStruct((rows, width), bf16),
        scratch_shapes=[
            pltpu.VMEM(conv.shape, bf16),
            pltpu.VMEM(gate.shape, bf16),
            pltpu.VMEM(fresh.shape, bf16),
            pltpu.VMEM((rows, width), bf16),
            pltpu.VMEM((head_count * inner, width), bf16),
            pltpu.VMEM((seq_count,) + end.shape[1:], bf16),
            pltpu.VMEM((seq_count,) + total.shape, f32),
            pltpu.VMEM(end.shape, f32),
            pltpu.VMEM((2, rounds * owners) + end.shape[1:], bf16),
            pltpu.VMEM((2, 64, 8 * CHUNK), bf16),
            pltpu.VMEM((32, 2 * inner), bf16),
            pltpu.VMEM((rounds, owners, CHUNK, 2 * inner), f32),
            pltpu.VMEM((rounds, owners, CHUNK, 2 * inner), bf16),
            pltpu.VMEM((rounds, 2 * owners, CHUNK), f32),
            pltpu.VMEM((rounds, head_count, 2 * owners, CHUNK), f32),
            pltpu.VMEM((rounds, owners, 8, CHUNK), f32),
            pltpu.VMEM((rounds, head_count, CHUNK, inner), bf16),
            pltpu.VMEM((rows, head_count * inner), bf16),
            dma((rounds + 7,)),
            dma((2, seq_count)),
            dma((2, seq_count)),
            dma((5,)),
            dma((5,)),
            dma((rounds, head_count)),
            dma((rounds, head_count)),
            dma((rounds, head_count)),
            dma((rounds, head_count)),
        ],
        compiler_params=params(collective_id=1, has_side_effects=True),
        name="finish",
    )(end, total, cols, row, skip, gain, conv, gate, fresh, hidden, w, hop)


def local(
    hidden_in,
    norm_gain,
    gate_weight,
    value_weight,
    state_weight,
    step_weight,
    step_bias,
    decay_log,
    skip_gain,
    conv_value,
    conv_state,
    output_gain,
    output_weight,
    piece_lengths,
):
    seq_count, head_count = lax.axis_size("seq"), lax.axis_size("head")
    shape = (seq_count, head_count)
    gate, mix, raw, halo, hop = project(
        shape, hidden_in, norm_gain, gate_weight, value_weight, state_weight, step_weight, output_weight
    )
    conv, fresh, cols, row, end, total = states(
        "seq",
        head_count,
        mix,
        halo,
        norm_gain,
        value_weight,
        state_weight,
        raw,
        piece_lengths,
        step_bias,
        decay_log,
        conv_value,
        conv_state,
    )
    return finish(
        shape,
        end,
        total,
        cols,
        row,
        skip_gain,
        output_gain,
        conv,
        gate,
        fresh,
        hidden_in,
        output_weight,
        hop,
    )


def solution(mesh):
    in_specs = (
        P("seq", None),
        P(),
        P(None, "head"),
        P(None, "head"),
        P(),
        P(None, "head"),
        P("head"),
        P("head"),
        P("head"),
        P(None, "head"),
        P(),
        P("head"),
        P("head", None),
        P(),
    )
    out_specs = P(("seq", "head"), None)
    return jax.shard_map(local, mesh=mesh, in_specs=in_specs, out_specs=out_specs, check_vma=False)
```

```python
import functools
import math

import jax
import jax.numpy as jnp
from jax import lax
from jax.experimental import pallas as pl
from jax.experimental.pallas import tpu as pltpu
from jax.sharding import PartitionSpec as P

HEAD_DIM = 64
STATE = 128
CONV = 4
CHUNK = 128
PIECES = 16
HALO = 16
REACH = 8
RESET = 256.0
LOG2E = math.log2(math.e)

f32 = jnp.float32
bf16 = jnp.bfloat16
epsilon = 1e-05
MESH = pl.DeviceIdType.MESH
NN = (((1,), (0,)), ((), ()))
NT = (((1,), (1,)), ((), ()))
TN = (((0,), (0,)), ((), ()))


def mm(a, b, dims=NN, precision=None):
    return lax.dot_general(a, b, dims, precision=precision, preferred_element_type=f32)


def silu(x):
    half = 0.5 * x
    return half * jnp.tanh(half) + half


def normalized(h, gain):
    wide = h.astype(f32)
    scale = lax.rsqrt(jnp.mean(wide * wide, axis=1, keepdims=True) + epsilon)
    return (wide * scale * gain.astype(f32)).astype(bf16)


def whole(shape):
    zeros = (0,) * len(shape)
    return pl.BlockSpec(shape, lambda *_: zeros)


SMEM_SPEC = pl.BlockSpec(memory_space=pltpu.SMEM)
ANY_SPEC = pl.BlockSpec(memory_space=pl.ANY)


def params(**kw):
    return pltpu.CompilerParams(vmem_limit_bytes=60 * 1024 * 1024, **kw)


def remote(src, dst, send, recv, **where):
    return pltpu.make_async_remote_copy(
        src_ref=src,
        dst_ref=dst,
        send_sem=send,
        recv_sem=recv,
        device_id=where,
        device_id_type=MESH,
    )


def greet(axes_and_peers):
    barrier = pltpu.get_barrier_semaphore()
    for where in axes_and_peers:
        pl.semaphore_signal(barrier, inc=1, device_id=where, device_id_type=MESH)
    pl.semaphore_wait(barrier, len(axes_and_peers))


def head_peer(me, chips, dy, dc):
    y, core = me // 2, me % 2
    return ((y + dy) % chips) * 2 + (core + dc) % 2


def project_copies(seq_count, head_count, hidden, w, halo, hop, send, recv):
    me = lax.axis_index("seq")
    head = lax.axis_index("head")
    chips = head_count // 2
    tokens = hidden.shape[0]
    after = (me + 1) % seq_count
    before = (me + seq_count - 1) % seq_count
    first, last = pl.ds(0, HALO), pl.ds(tokens - HALO, HALO)
    low, high = pl.ds(0, HALO), pl.ds(HALO, HALO)
    half = w.shape[0] // 2
    top, bottom = pl.ds(0, half), pl.ds(half, half)
    up = head_peer(head, chips, 1, 0)
    down = head_peer(head, chips, chips - 1, 0)
    partner = head_peer(head, chips, 0, 1)
    return (
        remote(hidden.at[last], halo.at[low], send.at[0], recv.at[0], seq=after),
        remote(hidden.at[first], halo.at[high], send.at[1], recv.at[1], seq=before),
        remote(w.at[top], hop.at[0, top], send.at[2], recv.at[2], head=up),
        remote(w.at[bottom], hop.at[1, bottom], send.at[3], recv.at[3], head=down),
        remote(w, hop.at[2], send.at[4], recv.at[4], head=partner),
    ), [{"seq": after}, {"seq": before}, {"head": up}, {"head": down}, {"head": partner}]


def project_kernel(
    mesh_shape,
    h_ref,
    gain_ref,
    gw_ref,
    vw_ref,
    sw_ref,
    tw_ref,
    hidden,
    w,
    gate_ref,
    mix_ref,
    raw_ref,
    halo,
    hop,
    turned,
    rows,
    send,
    recv,
):
    i = pl.program_id(0)
    copies, peers = project_copies(*mesh_shape, hidden, w, halo, hop, send, recv)
    barrier = pltpu.get_barrier_semaphore()

    @pl.when(i == 0)
    def _():
        for where in peers:
            pl.semaphore_signal(barrier, inc=1, device_id=where, device_id_type=MESH)
        narrow = tw_ref[...].astype(f32)
        turned[...] = jnp.concatenate([narrow, narrow], axis=0).astype(bf16)

    @pl.when(i == 1)
    def _():
        pl.semaphore_wait(barrier, len(peers))
        for copy in copies:
            copy.start()

    inner = vw_ref.shape[1]
    gain = gain_ref[...].reshape(1, -1)
    for q in range(gate_ref.shape[0]):
        at = slice(q * CHUNK, (q + 1) * CHUNK)
        for r in range(0, CHUNK, 32):
            rows[q * CHUNK + r : q * CHUNK + r + 32, :] = normalized(
                h_ref[q * CHUNK + r : q * CHUNK + r + 32, :], gain
            )
        n = rows[at, :]
        gate_ref[q, 0] = mm(n, gw_ref[...]).astype(bf16)
        mix_ref[at, :inner] = mm(n, vw_ref[...]).astype(bf16)
        mix_ref[at, inner:] = mm(n, sw_ref[...]).astype(bf16)
        raw_ref[q] = mm(turned[...], n, NT)

    @pl.when(i == pl.num_programs(0) - 1)
    def _():
        for copy in copies:
            copy.wait()


def project(mesh_shape, hidden, gain, gw, vw, sw, tw, w):
    tokens, width = hidden.shape
    inner = vw.shape[1]
    mixed = inner + sw.shape[1]
    rows = tokens // mesh_shape[1]
    rounds = rows // CHUNK
    return pl.pallas_call(
        functools.partial(project_kernel, mesh_shape),
        grid=(tokens // rows,),
        in_specs=[
            pl.BlockSpec((rows, width), lambda i: (i, 0)),
            whole(gain.shape),
            whole(gw.shape),
            whole(vw.shape),
            whole(sw.shape),
            whole(tw.shape),
            ANY_SPEC,
            ANY_SPEC,
        ],
        out_specs=[
            pl.BlockSpec((rounds, 1, CHUNK, inner), lambda i: (0, i, 0, 0)),
            pl.BlockSpec((rows, mixed), lambda i: (i, 0)),
            pl.BlockSpec((rows // CHUNK, 8, CHUNK), lambda i: (i, 0, 0)),
            ANY_SPEC,
            ANY_SPEC,
        ],
        out_shape=[
            jax.ShapeDtypeStruct((rounds, tokens // rows, CHUNK, inner), bf16),
            jax.ShapeDtypeStruct((tokens, mixed), bf16),
            jax.ShapeDtypeStruct((tokens // CHUNK, 8, CHUNK), f32),
            jax.ShapeDtypeStruct((2 * HALO, width), bf16),
            jax.ShapeDtypeStruct((3,) + w.shape, bf16),
        ],
        scratch_shapes=[
            pltpu.VMEM((8, width), bf16),
            pltpu.VMEM((rows, width), bf16),
            pltpu.SemaphoreType.DMA((5,)),
            pltpu.SemaphoreType.DMA((5,)),
        ],
        compiler_params=params(collective_id=2, has_side_effects=True),
        name="project",
    )(hidden, gain, gw, vw, sw, tw, hidden, w)


def head_lanes(columns):
    low = lax.broadcasted_iota(jnp.int32, (columns[0].shape[0], 2 * HEAD_DIM), 1) < HEAD_DIM
    pairs = [
        jnp.where(low, columns[2 * p], columns[2 * p + 1]) for p in range(len(columns) // 2)
    ]
    return jnp.concatenate(pairs, axis=1)


def decays(first_row, raw, lens_ref, bias_ref, rate_ref):
    chunks = raw.shape[0]
    shape = (chunks, 8, CHUNK)
    sub = lax.broadcasted_iota(jnp.int32, shape, 1)
    upper = sub < 4
    head = jnp.where(upper, sub, sub - 4)
    pos = (
        first_row
        + lax.broadcasted_iota(jnp.int32, shape, 0) * CHUNK
        + lax.broadcasted_iota(jnp.int32, shape, 2)
    )
    start = jnp.zeros(shape, jnp.int32)
    stop = jnp.full(shape, 1 << 30, jnp.int32)
    edge = jnp.int32(0)
    for k in range(PIECES):
        start = jnp.where(pos >= edge, edge, start)
        edge = edge + lens_ref[k]
        stop = jnp.minimum(stop, jnp.where(edge > pos, edge, 1 << 30))
    since = pos - start
    until = stop - 1 - pos
    bias = jnp.zeros(shape, f32)
    rate = jnp.zeros(shape, f32)
    for h in range(4):
        bias = jnp.where(head == h, bias_ref[h], bias)
        rate = jnp.where(head == h, rate_ref[h], rate)
    rate = jnp.exp(rate) * (-LOG2E)
    z = raw + bias
    step = jnp.maximum(z, 0.0) + jnp.log1p(jnp.exp(-jnp.abs(z)))
    log = step * rate
    reset = jnp.where(since == 0, -RESET, 0.0)
    ones = (
        lax.broadcasted_iota(jnp.int32, (CHUNK, CHUNK), 0)
        <= lax.broadcasted_iota(jnp.int32, (CHUNK, CHUNK), 1)
    ).astype(f32)
    cum = mm(
        (log + reset).reshape(chunks * 8, CHUNK), ones, precision=lax.Precision.HIGHEST
    ).reshape(shape)
    excl = cum - log
    total = cum[:, :, CHUNK - 1 :]
    log_step = jnp.where(step > 0.0, jnp.log2(step), -RESET)
    row = jnp.where(upper, cum - log_step, excl + log_step)
    g1 = jnp.where(upper, cum, excl)
    g2 = jnp.where(upper, jnp.exp2(cum), jnp.exp2(total - cum) * step)
    g3 = jnp.where(upper, jnp.exp2(total - excl), jnp.exp2(excl) * step)
    g4 = jnp.where(upper, since, until).astype(f32)
    return row, g1, g2, g3, g4


def states_kernel(
    axis,
    mix_ref,
    before_ref,
    after_ref,
    halo_ref,
    gain_ref,
    vw_ref,
    sw_ref,
    raw_ref,
    lens_ref,
    bias_ref,
    rate_ref,
    cv_ref,
    cs_ref,
    conv_ref,
    fresh_ref,
    cols_ref,
    row_ref,
    end_ref,
    total_ref,
    prod,
    halo,
    run,
    reach,
    spread,
    near,
):
    g = pl.program_id(0)
    groups = pl.num_programs(0)
    inner = vw_ref.shape[1]
    rows, mixed = mix_ref.shape
    rounds = rows // CHUNK
    blocks = mixed // 128
    first_row = lax.axis_index(axis) * (groups * rows)

    @pl.when(g == 0)
    def _():
        n = normalized(halo_ref[...], gain_ref[...].reshape(1, -1))
        halo[:, :inner] = mm(n, vw_ref[...]).astype(bf16).astype(f32)
        halo[:, inner:] = mm(n, sw_ref[...]).astype(bf16).astype(f32)
        row, g1, g2, g3, g4 = decays(first_row, raw_ref[...], lens_ref, bias_ref, rate_ref)
        row_ref[...] = row
        cols_ref[:, 0:8, :] = g1
        cols_ref[:, 8:16, :] = g2
        cols_ref[:, 16:24, :] = g3
        cols_ref[:, 24:32, :] = g4
        run[...] = jnp.zeros_like(run)
        reach[...] = jnp.zeros_like(reach)
        line = lax.broadcasted_iota(jnp.int32, spread.shape, 0) % 32
        lane = lax.broadcasted_iota(jnp.int32, spread.shape, 1)
        wanted = 12 + (lane // inner) * 8 + (lane % inner) // HEAD_DIM
        spread[...] = (line == wanted).astype(f32).astype(bf16)

        def clear(k, carry):
            near[k] = 0
            return carry

        lax.fori_loop(0, near.shape[0], clear, 0)

        def mark(k, edge):
            for shift in (-(CONV - 1), CONV - 2):
                at = (edge + shift - first_row + rows) // rows
                near[jnp.clip(at, 0, near.shape[0] - 1)] = 1
            return edge + lens_ref[jnp.minimum(k, PIECES - 1)]

        lax.fori_loop(0, PIECES + 1, mark, jnp.int32(0))

    taps = jnp.concatenate([cv_ref[...], cs_ref[...]], axis=1).astype(f32) * 0.5

    def put(b, at, values):
        lanes = slice(b * 128, (b + 1) * 128)
        for k in range(CONV - 1):
            prod[k, b, at : at + values.shape[0], :] = values * taps[k : k + 1, lanes]

    def group(masked):
        for b in range(blocks):
            lanes = slice(b * 128, (b + 1) * 128)
            ahead = before_ref[:, lanes].astype(f32)[16 - REACH :, :]
            put(b, 0, jnp.where(g == 0, halo[HALO - REACH : HALO, lanes], ahead))
            behind = after_ref[:, lanes].astype(f32)[:REACH, :]
            put(b, REACH + rows, jnp.where(g == groups - 1, halo[HALO : HALO + REACH, lanes], behind))
            for q in range(rounds):
                put(b, REACH + q * CHUNK, mix_ref[q * CHUNK : (q + 1) * CHUNK, lanes].astype(f32))
        for q in range(rounds):
            chunk(q, masked)

    def chunk(q, masked):
        cols = cols_ref[g * rounds + q]
        high = cols.astype(bf16).astype(f32)
        both = jnp.concatenate([high, cols - high], axis=0).astype(bf16)
        tails = mm(both, spread[...], TN)
        passing = head_lanes([cols[h : h + 1, CHUNK - 1 :] for h in range(4)])
        if masked:
            turned = jnp.concatenate([cols, jnp.zeros((CHUNK - 32, CHUNK), f32)], axis=0).T
            sides = [jnp.broadcast_to(turned[:, r : r + 1], (CHUNK, 128)) for r in (24, 28)]
        write = [None, None]
        for b in [inner // 128] + list(range(inner // 128)) + list(range(inner // 128 + 1, blocks)):
            lanes = slice(b * 128, (b + 1) * 128)
            centre = mix_ref[q * CHUNK : (q + 1) * CHUNK, lanes].astype(f32) * taps[CONV - 1 : CONV, lanes]
            for d in range(2):
                half = centre
                for distance in range(1, CONV):
                    at = REACH + q * CHUNK + (distance if d else -distance)
                    term = prod[CONV - 1 - distance, b, at : at + CHUNK, :]
                    if masked:
                        term = jnp.where(sides[d] >= distance, term, 0.0)
                    half = half + term
                value = half * jnp.tanh(half) + half
                at = d * mixed + b * 128
                narrow = value.astype(bf16)
                conv_ref[q, 0, :, at : at + 128] = narrow
                if b == inner // 128:
                    write[d] = narrow
                elif b < inner // 128:
                    at = d * inner + b * 128
                    scaled = (value * tails[:, at : at + 128]).astype(bf16)
                    fresh = mm(write[d], scaled, TN)
                    fresh_ref[q, d, :, lanes] = fresh.astype(bf16)
                    if d == 0:
                        run[0, :, lanes] = run[0, :, lanes] * jnp.exp2(passing[:, lanes]) + fresh
                    else:
                        run[1, :, lanes] = run[1, :, lanes] + jnp.exp2(reach[0:1, lanes]) * fresh
        reach[...] = reach[...] + passing

    edges = near[g + 1]

    @pl.when(edges == 0)
    def _():
        group(False)

    @pl.when(edges != 0)
    def _():
        group(True)

    @pl.when(g == groups - 1)
    def _():
        end_ref[...] = run[...].astype(bf16)
        total_ref[...] = reach[...]


def states(axis, owners, mix, halo, gain, vw, sw, raw, lens, bias, rate, cv, cs):
    tokens, mixed = mix.shape
    chunks = tokens // CHUNK
    inner = vw.shape[1]
    rounds = chunks // owners
    rows = rounds * CHUNK
    per = rows // 16
    last = tokens // 16 - 1
    return pl.pallas_call(
        functools.partial(states_kernel, axis),
        grid=(owners,),
        in_specs=[
            pl.BlockSpec((rows, mixed), lambda c: (c, 0)),
            pl.BlockSpec((16, mixed), lambda c: (jnp.maximum(c * per - 1, 0), 0)),
            pl.BlockSpec((16, mixed), lambda c: (jnp.minimum(c * per + per, last), 0)),
            whole(halo.shape),
            whole(gain.shape),
            whole(vw.shape),
            whole(sw.shape),
            whole(raw.shape),
            SMEM_SPEC,
            SMEM_SPEC,
            SMEM_SPEC,
            whole(cv.shape),
            whole(cs.shape),
        ],
        out_specs=[
            pl.BlockSpec((rounds, 1, CHUNK, 2 * mixed), lambda c: (0, c, 0, 0)),
            pl.BlockSpec((rounds, 2, STATE, inner), lambda c: (c, 0, 0, 0)),
            whole((chunks, 32, CHUNK)),
            whole((chunks, 8, CHUNK)),
            whole((2, STATE, inner)),
            whole((8, inner)),
        ],
        out_shape=[
            jax.ShapeDtypeStruct((rounds, owners, CHUNK, 2 * mixed), bf16),
            jax.ShapeDtypeStruct((chunks, 2, STATE, inner), bf16),
            jax.ShapeDtypeStruct((chunks, 32, CHUNK), f32),
            jax.ShapeDtypeStruct((chunks, 8, CHUNK), f32),
            jax.ShapeDtypeStruct((2, STATE, inner), bf16),
            jax.ShapeDtypeStruct((8, inner), f32),
        ],
        scratch_shapes=[
            pltpu.VMEM((CONV - 1, mixed // 128, rows + 2 * REACH, 128), f32),
            pltpu.VMEM((2 * HALO, mixed), f32),
            pltpu.VMEM((2, STATE, inner), f32),
            pltpu.VMEM((8, inner), f32),
            pltpu.VMEM((64, 2 * inner), bf16),
            pltpu.SMEM((owners + 2,), jnp.int32),
        ],
        compiler_params=params(),
        name="states",
    )(mix, mix, mix, halo, gain, vw, sw, raw, lens, bias, rate, cv, cs)


def split(x, parts):
    pieces = []
    for _ in range(parts - 1):
        pieces.append(x.astype(bf16).astype(f32))
        x = x - pieces[-1]
    return pieces + [x]


def finish_kernel(
    seq_count,
    head_count,
    end_ref,
    total_ref,
    cols_ref,
    row_ref,
    skip_ref,
    gain_ref,
    conv_hbm,
    gate_hbm,
    fresh_hbm,
    hidden_hbm,
    w_hbm,
    hop_hbm,
    out_ref,
    conv,
    gate,
    fresh,
    rest,
    weight,
    ends,
    totals,
    incoming,
    entry,
    pick,
    spread,
    inside,
    gated,
    squares,
    others,
    scales,
    sending,
    arrived,
    load,
    seq_send,
    seq_recv,
    w_send,
    w_recv,
    ss_send,
    ss_recv,
    send,
    recv,
):
    me = lax.axis_index("seq")
    head = lax.axis_index("head")
    chips = head_count // 2
    rounds, owners = conv.shape[0], conv.shape[1]
    chunks = rounds * owners
    inner = gate.shape[3]
    mixed = conv.shape[3] // 2
    rows = rounds * CHUNK
    slots = [(dy, dc) for dy in range(chips) for dc in range(2)]
    peers = [head_peer(head, chips, dy, dc) for dy, dc in slots]
    up, down, partner = peers[2], peers[2 * chips - 2], peers[1]

    def fetch(src, dst, n):
        copy = pltpu.make_async_copy(src, dst, load.at[n])
        copy.start()
        return copy

    def part(k):
        return pl.ds(k * inner, inner)

    conv_in = [fetch(conv_hbm.at[q], conv.at[q], q) for q in range(rounds)]
    fresh_in = fetch(fresh_hbm, fresh, rounds)
    gate_in = fetch(gate_hbm, gate, rounds + 1)
    mine = pl.ds(pl.multiple_of(head * rows, rows), rows)
    half = inner // 2
    side = (2 * chips - 2) * inner
    far = 4 * inner
    top, bottom = pl.ds(0, half), pl.ds(half, half)
    late = [
        fetch(hidden_hbm.at[mine, :], rest, rounds + 2),
        fetch(w_hbm, weight.at[part(0)], rounds + 3),
        fetch(hop_hbm.at[2], weight.at[part(1)], rounds + 4),
        fetch(hop_hbm.at[0, top], weight.at[pl.ds(2 * inner, half)], rounds + 5),
        fetch(hop_hbm.at[1, bottom], weight.at[pl.ds(side + half, half)], rounds + 6),
    ]

    greet(
        [{"seq": (me + k) % seq_count} for k in range(1, seq_count)]
        + [{"head": p} for p in peers[1:]]
    )
    started = []

    def start(copy):
        copy.start()
        started.append(copy)
        return copy

    travelling = []
    for k in range(1, seq_count):
        target = (me + k) % seq_count
        backward = (me + k) // seq_count
        travelling.append(
            start(
                remote(
                    end_ref.at[backward], ends.at[k], seq_send.at[0, k], seq_recv.at[0, k], seq=target
                )
            )
        )
        travelling.append(
            start(remote(total_ref, totals.at[k], seq_send.at[1, k], seq_recv.at[1, k], seq=target))
        )
    def weigh(n, src, row, where, count=half):
        at = weight.at[pl.ds(row, count)]
        return start(remote(src, at, w_send.at[n], w_recv.at[n], head=where))

    u1 = weigh(0, w_hbm.at[bottom], 2 * inner + half, up)
    u2 = weigh(1, w_hbm.at[top], side, down)
    t1 = weigh(2, hop_hbm.at[0, top], far, up)
    t3 = weigh(3, hop_hbm.at[1, bottom], far + half, down)
    beside = [
        weigh(4, hop_hbm.at[0, top], 3 * inner, partner),
        weigh(5, hop_hbm.at[1, bottom], side + inner + half, partner),
    ]

    i = lax.broadcasted_iota(jnp.int32, (CHUNK, CHUNK), 0)
    j = lax.broadcasted_iota(jnp.int32, (CHUNK, CHUNK), 1)
    lower = i >= j
    upper = i <= j
    low = j < HEAD_DIM
    skip = head_lanes([jnp.full((1, 1), skip_ref[h], f32) for h in range(4)])
    sub = lax.broadcasted_iota(jnp.int32, (8, CHUNK), 0)
    line = lax.broadcasted_iota(jnp.int32, pick.shape[1:], 0)
    block = lax.broadcasted_iota(jnp.int32, pick.shape[1:], 1) // CHUNK
    sign = jnp.where(block < 4, 1.0, -1.0)
    chosen = jnp.where((line < 24) & (line % 8 == block), sign, 0.0).astype(bf16)
    for u in range(pick.shape[0]):
        pick[u] = chosen
    line = lax.broadcasted_iota(jnp.int32, spread.shape, 0)
    lane = lax.broadcasted_iota(jnp.int32, spread.shape, 1)
    wanted = (lane // inner) * 8 + (lane % inner) // HEAD_DIM
    spread[...] = (line % 16 == wanted).astype(f32).astype(bf16)

    def within(q, d, u):
        c = d * rounds + q
        row = row_ref[c]
        lines = jnp.concatenate(split(jnp.where(sub < 4, -row, row), 3), axis=0)
        for n in range(8):
            own = lax.broadcasted_iota(jnp.int32, lines.shape, 0) % 8 == n
            pick[u, 32:56, n * CHUNK : (n + 1) * CHUNK] = jnp.where(own, lines, 0.0).astype(bf16)
        left = jnp.concatenate(
            split(cols_ref[c, 0:8, :], 3)
            + [jnp.zeros((8, CHUNK), f32), jnp.ones((24, CHUNK), f32), jnp.zeros((8, CHUNK), f32)],
            axis=0,
        ).astype(bf16)
        made = mm(left, pick[u], TN)
        pair = []
        for e, keep in ((0, lower), (1, upper)):
            base = e * mixed + inner
            write = conv[q, d, :, base : base + STATE]
            read = conv[q, d, :, base + STATE : base + 2 * STATE]
            pair.append(jnp.where(keep, mm(read, write, NT), 0.0))
        for p in range(2):
            weights = ([], [])
            for h in (2 * p, 2 * p + 1):
                table = jnp.exp2(
                    jnp.where(
                        lower,
                        made[:, h * CHUNK : (h + 1) * CHUNK],
                        made[:, (4 + h) * CHUNK : (5 + h) * CHUNK],
                    )
                )
                for e in range(2):
                    weights[e].append((pair[e] * table).astype(bf16))
            for e in range(2):
                at = e * mixed + p * CHUNK
                x = conv[q, d, :, at : at + CHUNK]
                zero = jnp.zeros_like(x)
                stacked = jnp.concatenate([jnp.where(low, x, zero), jnp.where(low, zero, x)], axis=0)
                made_here = mm(jnp.concatenate(weights[e], axis=1), stacked)
                made_here = made_here + skip[:, p * CHUNK : (p + 1) * CHUNK] * x.astype(f32)
                inside[q, d, :, e * inner + p * CHUNK : e * inner + (p + 1) * CHUNK] = made_here

    for q in range(rounds):
        conv_in[q].wait()

        def step(n, carry, q=q):
            for u in range(2):
                within(q, 2 * n + u, u)
            return carry

        lax.fori_loop(0, owners // 2, step, 0)

    for copy in travelling:
        copy.wait_recv()
    for copy in (u1, u2, t1, t3):
        copy.wait_recv()
    beside += [
        weigh(6, weight.at[pl.ds(2 * inner + half, half)], 3 * inner + half, partner),
        weigh(7, weight.at[pl.ds(side, half)], side + inner, partner),
        weigh(8, weight.at[part(4)], 5 * inner, partner, inner),
    ]
    incoming[...] = jnp.zeros_like(incoming)
    for k in range(seq_count - 1, 0, -1):

        @pl.when(k <= me)
        def _(k=k):
            incoming[0] = incoming[0] * jnp.exp2(totals[k, 0:1, :]) + ends[k].astype(f32)

    for k in range(1, seq_count):

        @pl.when(k > me)
        def _(k=k):
            incoming[1] = incoming[1] * jnp.exp2(totals[k, 0:1, :]) + ends[k].astype(f32)

    fresh_in.wait()

    def passing(c):
        return jnp.exp2(head_lanes([cols_ref[c, h : h + 1, CHUNK - 1 :] for h in range(4)]))

    def walk(c, carry):
        b = chunks - 1 - c
        for e, at in ((0, c), (1, b)):
            state = incoming[e]
            entry[e, at] = state.astype(bf16)
            incoming[e] = state * passing(at) + fresh[at, e].astype(f32)
        return carry

    lax.fori_loop(0, chunks, walk, 0)
    gate_in.wait()

    ones = jnp.ones((8, inner), bf16)
    gain = gain_ref[...].reshape(1, -1).astype(f32)
    sixteen = lax.broadcasted_iota(jnp.int32, (2 * owners, CHUNK), 0)

    def carried(q, d, sums):
        c = d * rounds + q
        left = jnp.concatenate(split(cols_ref[c, 8:24, :], 2), axis=0).astype(bf16)
        scale = mm(left, spread[...], TN)
        act = silu(gate[q, d].astype(f32))
        for e in range(2):
            at = e * mixed + inner + STATE
            lanes = slice(e * inner, (e + 1) * inner)
            part_in = mm(conv[q, d, :, at : at + STATE], entry[e, c])
            value = (inside[q, d, :, lanes] + part_in * scale[:, lanes]) * act
            gated[q, d, :, lanes] = value.astype(bf16)
            square = mm(ones, (value * value).astype(bf16), NT)
            square = jnp.concatenate([square] * (2 * owners // 8), axis=0)
            sums = jnp.where(sixteen == 2 * d + e, square, sums)
        return sums

    def combine(q):
        for k in range(1, head_count):
            ss[q][k - 1].wait_recv()
        total = squares[q]
        for k in range(1, head_count):
            total = total + others[q, k]
        total = lax.rsqrt(total * (1.0 / (inner * head_count)) + epsilon)
        for d in range(owners):
            scales[q, d, 0:2, :] = total[2 * d : 2 * d + 2, :]
        for k in range(head_count):
            d = peers[k]
            scale = jnp.concatenate(
                [scales[q, d, 0:2, :], jnp.zeros((CHUNK - 2, CHUNK), f32)], axis=0
            ).T
            both = gated[q, d, :, :inner].astype(f32) * scale[:, 0:1]
            both = both + gated[q, d, :, inner:].astype(f32) * scale[:, 1:2]
            both = (both * gain).astype(bf16)
            if k == 0:
                arrived[q * CHUNK : (q + 1) * CHUNK, 0:inner] = both
            else:
                sending[q, k] = both
        return [
            start(
                remote(
                    sending.at[q, k],
                    arrived.at[pl.ds(q * CHUNK, CHUNK), part(k)],
                    send.at[q, k],
                    recv.at[q, k],
                    head=peers[k],
                )
            )
            for k in sorted(range(1, head_count), key=lambda k: -min(slots[k][0], chips - slots[k][0]))
        ]

    ss, pieces = [], []
    for q in range(rounds):
        squares[q] = lax.fori_loop(
            0, owners, lambda d, sums, q=q: carried(q, d, sums), jnp.zeros((2 * owners, CHUNK), f32)
        )
        ss.append(
            [
                start(
                    remote(
                        squares.at[q], others.at[q, k], ss_send.at[q, k], ss_recv.at[q, k], head=peers[k]
                    )
                )
                for k in range(1, head_count)
            ]
        )
        if q:
            pieces.append(combine(q - 1))
    pieces.append(combine(rounds - 1))

    for copy in late:
        copy.wait()
    for copy in beside:
        copy.wait_recv()
    width = out_ref.shape[1]
    step_lanes = 256
    early = (rounds - 1) * CHUNK
    for first, count, done in ((0, early, pieces[:-1]), (early, CHUNK, pieces[-1:])):
        for batch in done:
            for copy in batch:
                copy.wait_recv()
        if count:

            def project_out(b, carry, first=first, count=count):
                lanes = pl.ds(pl.multiple_of(b * step_lanes, step_lanes), step_lanes)
                here = pl.ds(first, count)
                out_ref[here, lanes] = (
                    mm(arrived[here, :], weight[:, lanes]) + rest[here, lanes].astype(f32)
                ).astype(bf16)
                return carry

            lax.fori_loop(0, width // step_lanes, project_out, 0)
    for copy in started:
        copy.wait_send()


def finish(mesh_shape, end, total, cols, row, skip, gain, conv, gate, fresh, hidden, w, hop):
    seq_count, head_count = mesh_shape
    rounds, owners = conv.shape[:2]
    rows = rounds * CHUNK
    inner = gate.shape[3]
    width = hidden.shape[1]
    dma = pltpu.SemaphoreType.DMA
    return pl.pallas_call(
        functools.partial(finish_kernel, seq_count, head_count),
        in_specs=[
            whole(end.shape),
            whole(total.shape),
            whole(cols.shape),
            whole(row.shape),
            SMEM_SPEC,
            whole(gain.shape),
        ]
        + [ANY_SPEC] * 6,
        out_specs=whole((rows, width)),
        out_shape=jax.ShapeDtypeStruct((rows, width), bf16),
        scratch_shapes=[
            pltpu.VMEM(conv.shape, bf16),
            pltpu.VMEM(gate.shape, bf16),
            pltpu.VMEM(fresh.shape, bf16),
            pltpu.VMEM((rows, width), bf16),
            pltpu.VMEM((head_count * inner, width), bf16),
            pltpu.VMEM((seq_count,) + end.shape[1:], bf16),
            pltpu.VMEM((seq_count,) + total.shape, f32),
            pltpu.VMEM(end.shape, f32),
            pltpu.VMEM((2, rounds * owners) + end.shape[1:], bf16),
            pltpu.VMEM((2, 64, 8 * CHUNK), bf16),
            pltpu.VMEM((32, 2 * inner), bf16),
            pltpu.VMEM((rounds, owners, CHUNK, 2 * inner), f32),
            pltpu.VMEM((rounds, owners, CHUNK, 2 * inner), bf16),
            pltpu.VMEM((rounds, 2 * owners, CHUNK), f32),
            pltpu.VMEM((rounds, head_count, 2 * owners, CHUNK), f32),
            pltpu.VMEM((rounds, owners, 8, CHUNK), f32),
            pltpu.VMEM((rounds, head_count, CHUNK, inner), bf16),
            pltpu.VMEM((rows, head_count * inner), bf16),
            dma((rounds + 7,)),
            dma((2, seq_count)),
            dma((2, seq_count)),
            dma((9,)),
            dma((9,)),
            dma((rounds, head_count)),
            dma((rounds, head_count)),
            dma((rounds, head_count)),
            dma((rounds, head_count)),
        ],
        compiler_params=params(collective_id=1, has_side_effects=True),
        name="finish",
    )(end, total, cols, row, skip, gain, conv, gate, fresh, hidden, w, hop)


def local(
    hidden_in,
    norm_gain,
    gate_weight,
    value_weight,
    state_weight,
    step_weight,
    step_bias,
    decay_log,
    skip_gain,
    conv_value,
    conv_state,
    output_gain,
    output_weight,
    piece_lengths,
):
    seq_count, head_count = lax.axis_size("seq"), lax.axis_size("head")
    shape = (seq_count, head_count)
    gate, mix, raw, halo, hop = project(
        shape, hidden_in, norm_gain, gate_weight, value_weight, state_weight, step_weight.T, output_weight
    )
    conv, fresh, cols, row, end, total = states(
        "seq",
        head_count,
        mix,
        halo,
        norm_gain,
        value_weight,
        state_weight,
        raw,
        piece_lengths,
        step_bias,
        decay_log,
        conv_value,
        conv_state,
    )
    return finish(
        shape,
        end,
        total,
        cols,
        row,
        skip_gain,
        output_gain,
        conv,
        gate,
        fresh,
        hidden_in,
        output_weight,
        hop,
    )


def solution(mesh):
    in_specs = (
        P("seq", None),
        P(),
        P(None, "head"),
        P(None, "head"),
        P(),
        P(None, "head"),
        P("head"),
        P("head"),
        P("head"),
        P(None, "head"),
        P(),
        P("head"),
        P("head", None),
        P(),
    )
    out_specs = P(("seq", "head"), None)
    return jax.shard_map(local, mesh=mesh, in_specs=in_specs, out_specs=out_specs, check_vma=False)
```

```python
import functools
import math

import jax
import jax.numpy as jnp
from jax import lax
from jax.experimental import pallas as pl
from jax.experimental.pallas import tpu as pltpu
from jax.sharding import PartitionSpec as P

HEAD_DIM = 64
STATE = 128
CONV = 4
CHUNK = 128
PIECES = 16
HALO = 16
REACH = 8
RESET = 256.0
LOG2E = math.log2(math.e)

f32 = jnp.float32
bf16 = jnp.bfloat16
epsilon = 1e-05
MESH = pl.DeviceIdType.MESH
NN = (((1,), (0,)), ((), ()))
NT = (((1,), (1,)), ((), ()))
TN = (((0,), (0,)), ((), ()))


def mm(a, b, dims=NN, precision=None):
    return lax.dot_general(a, b, dims, precision=precision, preferred_element_type=f32)


def silu(x):
    half = 0.5 * x
    return half * jnp.tanh(half) + half


def normalized(h, gain):
    wide = h.astype(f32)
    scale = lax.rsqrt(jnp.mean(wide * wide, axis=1, keepdims=True) + epsilon)
    return (wide * scale * gain.astype(f32)).astype(bf16)


def whole(shape):
    zeros = (0,) * len(shape)
    return pl.BlockSpec(shape, lambda *_: zeros)


SMEM_SPEC = pl.BlockSpec(memory_space=pltpu.SMEM)
ANY_SPEC = pl.BlockSpec(memory_space=pl.ANY)


def params(**kw):
    return pltpu.CompilerParams(vmem_limit_bytes=60 * 1024 * 1024, **kw)


def remote(src, dst, send, recv, **where):
    return pltpu.make_async_remote_copy(
        src_ref=src,
        dst_ref=dst,
        send_sem=send,
        recv_sem=recv,
        device_id=where,
        device_id_type=MESH,
    )


def greet(axes_and_peers):
    barrier = pltpu.get_barrier_semaphore()
    for where in axes_and_peers:
        pl.semaphore_signal(barrier, inc=1, device_id=where, device_id_type=MESH)
    pl.semaphore_wait(barrier, len(axes_and_peers))


def head_peer(me, chips, dy, dc):
    y, core = me // 2, me % 2
    return ((y + dy) % chips) * 2 + (core + dc) % 2


def project_copies(seq_count, head_count, hidden, w, halo, hop, send, recv):
    me = lax.axis_index("seq")
    head = lax.axis_index("head")
    chips = head_count // 2
    tokens = hidden.shape[0]
    after = (me + 1) % seq_count
    before = (me + seq_count - 1) % seq_count
    first, last = pl.ds(0, HALO), pl.ds(tokens - HALO, HALO)
    low, high = pl.ds(0, HALO), pl.ds(HALO, HALO)
    half = w.shape[0] // 2
    top, bottom = pl.ds(0, half), pl.ds(half, half)
    up = head_peer(head, chips, 1, 0)
    down = head_peer(head, chips, chips - 1, 0)
    partner = head_peer(head, chips, 0, 1)
    return (
        remote(hidden.at[last], halo.at[low], send.at[0], recv.at[0], seq=after),
        remote(hidden.at[first], halo.at[high], send.at[1], recv.at[1], seq=before),
        remote(w.at[top], hop.at[0, top], send.at[2], recv.at[2], head=up),
        remote(w.at[bottom], hop.at[1, bottom], send.at[3], recv.at[3], head=down),
        remote(w, hop.at[2], send.at[4], recv.at[4], head=partner),
    ), [{"seq": after}, {"seq": before}, {"head": up}, {"head": down}, {"head": partner}]


def project_kernel(
    mesh_shape,
    h_ref,
    gain_ref,
    gw_ref,
    vw_ref,
    sw_ref,
    tw_ref,
    hidden,
    w,
    gate_ref,
    mix_ref,
    raw_ref,
    halo,
    hop,
    turned,
    rows,
    send,
    recv,
):
    i = pl.program_id(0)
    copies, peers = project_copies(*mesh_shape, hidden, w, halo, hop, send, recv)
    barrier = pltpu.get_barrier_semaphore()

    @pl.when(i == 0)
    def _():
        for where in peers:
            pl.semaphore_signal(barrier, inc=1, device_id=where, device_id_type=MESH)
        narrow = tw_ref[...].astype(f32)
        turned[...] = jnp.concatenate([narrow, narrow], axis=0).astype(bf16)

    @pl.when(i == 1)
    def _():
        pl.semaphore_wait(barrier, len(peers))
        for copy in copies:
            copy.start()

    inner = vw_ref.shape[1]
    gain = gain_ref[...].reshape(1, -1)
    deep = min(256, h_ref.shape[0])
    for first in range(0, h_ref.shape[0], deep):
        for r in range(first, first + deep, 32):
            rows[r : r + 32, :] = normalized(h_ref[r : r + 32, :], gain)
        at = slice(first, first + deep)
        n = rows[at, :]
        gate = mm(n, gw_ref[...]).astype(bf16)
        mix_ref[at, :inner] = mm(n, vw_ref[...]).astype(bf16)
        mix_ref[at, inner:] = mm(n, sw_ref[...]).astype(bf16)
        raw = mm(turned[...], n, NT)
        for q in range(deep // CHUNK):
            part = slice(q * CHUNK, (q + 1) * CHUNK)
            gate_ref[first // CHUNK + q, 0] = gate[part]
            raw_ref[first // CHUNK + q] = raw[:, part]

    @pl.when(i == pl.num_programs(0) - 1)
    def _():
        for copy in copies:
            copy.wait()


def project(mesh_shape, hidden, gain, gw, vw, sw, tw, w):
    tokens, width = hidden.shape
    inner = vw.shape[1]
    mixed = inner + sw.shape[1]
    rows = tokens // mesh_shape[1]
    rounds = rows // CHUNK
    return pl.pallas_call(
        functools.partial(project_kernel, mesh_shape),
        grid=(tokens // rows,),
        in_specs=[
            pl.BlockSpec((rows, width), lambda i: (i, 0)),
            whole(gain.shape),
            whole(gw.shape),
            whole(vw.shape),
            whole(sw.shape),
            whole(tw.shape),
            ANY_SPEC,
            ANY_SPEC,
        ],
        out_specs=[
            pl.BlockSpec((rounds, 1, CHUNK, inner), lambda i: (0, i, 0, 0)),
            pl.BlockSpec((rows, mixed), lambda i: (i, 0)),
            pl.BlockSpec((rows // CHUNK, 8, CHUNK), lambda i: (i, 0, 0)),
            ANY_SPEC,
            ANY_SPEC,
        ],
        out_shape=[
            jax.ShapeDtypeStruct((rounds, tokens // rows, CHUNK, inner), bf16),
            jax.ShapeDtypeStruct((tokens, mixed), bf16),
            jax.ShapeDtypeStruct((tokens // CHUNK, 8, CHUNK), f32),
            jax.ShapeDtypeStruct((2 * HALO, width), bf16),
            jax.ShapeDtypeStruct((3,) + w.shape, bf16),
        ],
        scratch_shapes=[
            pltpu.VMEM((8, width), bf16),
            pltpu.VMEM((rows, width), bf16),
            pltpu.SemaphoreType.DMA((5,)),
            pltpu.SemaphoreType.DMA((5,)),
        ],
        compiler_params=params(collective_id=2, has_side_effects=True),
        name="project",
    )(hidden, gain, gw, vw, sw, tw, hidden, w)


def head_lanes(columns):
    low = lax.broadcasted_iota(jnp.int32, (columns[0].shape[0], 2 * HEAD_DIM), 1) < HEAD_DIM
    pairs = [
        jnp.where(low, columns[2 * p], columns[2 * p + 1]) for p in range(len(columns) // 2)
    ]
    return jnp.concatenate(pairs, axis=1)


def decays(first_row, raw, lens_ref, bias_ref, rate_ref):
    chunks = raw.shape[0]
    shape = (chunks, 8, CHUNK)
    sub = lax.broadcasted_iota(jnp.int32, shape, 1)
    upper = sub < 4
    head = jnp.where(upper, sub, sub - 4)
    pos = (
        first_row
        + lax.broadcasted_iota(jnp.int32, shape, 0) * CHUNK
        + lax.broadcasted_iota(jnp.int32, shape, 2)
    )
    start = jnp.zeros(shape, jnp.int32)
    stop = jnp.full(shape, 1 << 30, jnp.int32)
    edge = jnp.int32(0)
    for k in range(PIECES):
        start = jnp.where(pos >= edge, edge, start)
        edge = edge + lens_ref[k]
        stop = jnp.minimum(stop, jnp.where(edge > pos, edge, 1 << 30))
    since = pos - start
    until = stop - 1 - pos
    bias = jnp.zeros(shape, f32)
    rate = jnp.zeros(shape, f32)
    for h in range(4):
        bias = jnp.where(head == h, bias_ref[h], bias)
        rate = jnp.where(head == h, rate_ref[h], rate)
    rate = jnp.exp(rate) * (-LOG2E)
    z = raw + bias
    step = jnp.maximum(z, 0.0) + jnp.log1p(jnp.exp(-jnp.abs(z)))
    log = step * rate
    reset = jnp.where(since == 0, -RESET, 0.0)
    ones = (
        lax.broadcasted_iota(jnp.int32, (CHUNK, CHUNK), 0)
        <= lax.broadcasted_iota(jnp.int32, (CHUNK, CHUNK), 1)
    ).astype(f32)
    cum = mm(
        (log + reset).reshape(chunks * 8, CHUNK), ones, precision=lax.Precision.HIGHEST
    ).reshape(shape)
    excl = cum - log
    total = cum[:, :, CHUNK - 1 :]
    log_step = jnp.where(step > 0.0, jnp.log2(step), -RESET)
    row = jnp.where(upper, cum - log_step, excl + log_step)
    g1 = jnp.where(upper, cum, excl)
    g2 = jnp.where(upper, jnp.exp2(cum), jnp.exp2(total - cum) * step)
    g3 = jnp.where(upper, jnp.exp2(total - excl), jnp.exp2(excl) * step)
    g4 = jnp.where(upper, since, until).astype(f32)
    return row, g1, g2, g3, g4


def states_kernel(
    axis,
    mix_ref,
    before_ref,
    after_ref,
    halo_ref,
    gain_ref,
    vw_ref,
    sw_ref,
    raw_ref,
    lens_ref,
    bias_ref,
    rate_ref,
    cv_ref,
    cs_ref,
    conv_ref,
    fresh_ref,
    cols_ref,
    row_ref,
    end_ref,
    total_ref,
    prod,
    halo,
    run,
    reach,
    spread,
    near,
):
    g = pl.program_id(0)
    groups = pl.num_programs(0)
    inner = vw_ref.shape[1]
    rows, mixed = mix_ref.shape
    rounds = rows // CHUNK
    blocks = mixed // 128
    first_row = lax.axis_index(axis) * (groups * rows)

    @pl.when(g == 0)
    def _():
        n = normalized(halo_ref[...], gain_ref[...].reshape(1, -1))
        halo[:, :inner] = mm(n, vw_ref[...]).astype(bf16).astype(f32)
        halo[:, inner:] = mm(n, sw_ref[...]).astype(bf16).astype(f32)
        row, g1, g2, g3, g4 = decays(first_row, raw_ref[...], lens_ref, bias_ref, rate_ref)
        row_ref[...] = row
        cols_ref[:, 0:8, :] = g1
        cols_ref[:, 8:16, :] = g2
        cols_ref[:, 16:24, :] = g3
        cols_ref[:, 24:32, :] = g4
        run[...] = jnp.zeros_like(run)
        reach[...] = jnp.zeros_like(reach)
        line = lax.broadcasted_iota(jnp.int32, spread.shape, 0) % 32
        lane = lax.broadcasted_iota(jnp.int32, spread.shape, 1)
        wanted = 12 + (lane // inner) * 8 + (lane % inner) // HEAD_DIM
        spread[...] = (line == wanted).astype(f32).astype(bf16)

        def clear(k, carry):
            near[k] = 0
            return carry

        lax.fori_loop(0, near.shape[0], clear, 0)

        def mark(k, edge):
            for shift in (-(CONV - 1), CONV - 2):
                at = (edge + shift - first_row + rows) // rows
                near[jnp.clip(at, 0, near.shape[0] - 1)] = 1
            return edge + lens_ref[jnp.minimum(k, PIECES - 1)]

        lax.fori_loop(0, PIECES + 1, mark, jnp.int32(0))

    taps = jnp.concatenate([cv_ref[...], cs_ref[...]], axis=1).astype(f32) * 0.5

    def put(b, at, values):
        lanes = slice(b * 128, (b + 1) * 128)
        for k in range(CONV - 1):
            prod[k, b, at : at + values.shape[0], :] = values * taps[k : k + 1, lanes]

    def ready(q):
        for b in range(blocks):
            lanes = slice(b * 128, (b + 1) * 128)
            put(b, REACH + q * CHUNK, mix_ref[q * CHUNK : (q + 1) * CHUNK, lanes].astype(f32))

    def group(masked):
        for b in range(blocks):
            lanes = slice(b * 128, (b + 1) * 128)
            ahead = before_ref[:, lanes].astype(f32)[16 - REACH :, :]
            put(b, 0, jnp.where(g == 0, halo[HALO - REACH : HALO, lanes], ahead))
            behind = after_ref[:, lanes].astype(f32)[:REACH, :]
            put(b, REACH + rows, jnp.where(g == groups - 1, halo[HALO : HALO + REACH, lanes], behind))
        ready(0)
        for q in range(rounds):
            if q + 1 < rounds:
                ready(q + 1)
            chunk(q, masked)

    def chunk(q, masked):
        cols = cols_ref[g * rounds + q]
        high = cols.astype(bf16).astype(f32)
        both = jnp.concatenate([high, cols - high], axis=0).astype(bf16)
        tails = mm(both, spread[...], TN)
        passing = head_lanes([cols[h : h + 1, CHUNK - 1 :] for h in range(4)])
        if masked:
            turned = jnp.concatenate([cols, jnp.zeros((CHUNK - 32, CHUNK), f32)], axis=0).T
            sides = [jnp.broadcast_to(turned[:, r : r + 1], (CHUNK, 128)) for r in (24, 28)]
        write = [None, None]
        for b in [inner // 128] + list(range(inner // 128)) + list(range(inner // 128 + 1, blocks)):
            lanes = slice(b * 128, (b + 1) * 128)
            centre = mix_ref[q * CHUNK : (q + 1) * CHUNK, lanes].astype(f32) * taps[CONV - 1 : CONV, lanes]
            for d in range(2):
                half = centre
                for distance in range(1, CONV):
                    at = REACH + q * CHUNK + (distance if d else -distance)
                    term = prod[CONV - 1 - distance, b, at : at + CHUNK, :]
                    if masked:
                        term = jnp.where(sides[d] >= distance, term, 0.0)
                    half = half + term
                value = half * jnp.tanh(half) + half
                at = d * mixed + b * 128
                narrow = value.astype(bf16)
                conv_ref[q, 0, :, at : at + 128] = narrow
                if b == inner // 128:
                    write[d] = narrow
                elif b < inner // 128:
                    at = d * inner + b * 128
                    scaled = (value * tails[:, at : at + 128]).astype(bf16)
                    fresh = mm(write[d], scaled, TN)
                    fresh_ref[q, d, :, lanes] = fresh.astype(bf16)
                    if d == 0:
                        run[0, :, lanes] = run[0, :, lanes] * jnp.exp2(passing[:, lanes]) + fresh
                    else:
                        run[1, :, lanes] = run[1, :, lanes] + jnp.exp2(reach[0:1, lanes]) * fresh
        reach[...] = reach[...] + passing

    edges = near[g + 1]

    @pl.when(edges == 0)
    def _():
        group(False)

    @pl.when(edges != 0)
    def _():
        group(True)

    @pl.when(g == groups - 1)
    def _():
        end_ref[...] = run[...].astype(bf16)
        total_ref[...] = reach[...]


def states(axis, owners, mix, halo, gain, vw, sw, raw, lens, bias, rate, cv, cs):
    tokens, mixed = mix.shape
    chunks = tokens // CHUNK
    inner = vw.shape[1]
    rounds = chunks // owners
    rows = rounds * CHUNK
    per = rows // 16
    last = tokens // 16 - 1
    return pl.pallas_call(
        functools.partial(states_kernel, axis),
        grid=(owners,),
        in_specs=[
            pl.BlockSpec((rows, mixed), lambda c: (c, 0)),
            pl.BlockSpec((16, mixed), lambda c: (jnp.maximum(c * per - 1, 0), 0)),
            pl.BlockSpec((16, mixed), lambda c: (jnp.minimum(c * per + per, last), 0)),
            whole(halo.shape),
            whole(gain.shape),
            whole(vw.shape),
            whole(sw.shape),
            whole(raw.shape),
            SMEM_SPEC,
            SMEM_SPEC,
            SMEM_SPEC,
            whole(cv.shape),
            whole(cs.shape),
        ],
        out_specs=[
            pl.BlockSpec((rounds, 1, CHUNK, 2 * mixed), lambda c: (0, c, 0, 0)),
            pl.BlockSpec((rounds, 2, STATE, inner), lambda c: (c, 0, 0, 0)),
            whole((chunks, 32, CHUNK)),
            whole((chunks, 8, CHUNK)),
            whole((2, STATE, inner)),
            whole((8, inner)),
        ],
        out_shape=[
            jax.ShapeDtypeStruct((rounds, owners, CHUNK, 2 * mixed), bf16),
            jax.ShapeDtypeStruct((chunks, 2, STATE, inner), bf16),
            jax.ShapeDtypeStruct((chunks, 32, CHUNK), f32),
            jax.ShapeDtypeStruct((chunks, 8, CHUNK), f32),
            jax.ShapeDtypeStruct((2, STATE, inner), bf16),
            jax.ShapeDtypeStruct((8, inner), f32),
        ],
        scratch_shapes=[
            pltpu.VMEM((CONV - 1, mixed // 128, rows + 2 * REACH, 128), f32),
            pltpu.VMEM((2 * HALO, mixed), f32),
            pltpu.VMEM((2, STATE, inner), f32),
            pltpu.VMEM((8, inner), f32),
            pltpu.VMEM((64, 2 * inner), bf16),
            pltpu.SMEM((owners + 2,), jnp.int32),
        ],
        compiler_params=params(),
        name="states",
    )(mix, mix, mix, halo, gain, vw, sw, raw, lens, bias, rate, cv, cs)


def split(x, parts):
    pieces = []
    for _ in range(parts - 1):
        pieces.append(x.astype(bf16).astype(f32))
        x = x - pieces[-1]
    return pieces + [x]


def finish_kernel(
    seq_count,
    head_count,
    end_ref,
    total_ref,
    cols_ref,
    row_ref,
    skip_ref,
    gain_ref,
    conv_hbm,
    gate_hbm,
    fresh_hbm,
    hidden_hbm,
    w_hbm,
    hop_hbm,
    out_ref,
    conv,
    gate,
    fresh,
    rest,
    weight,
    ends,
    totals,
    incoming,
    entry,
    pick,
    spread,
    inside,
    gated,
    squares,
    others,
    sending,
    arrived,
    load,
    seq_send,
    seq_recv,
    w_send,
    w_recv,
    ss_send,
    ss_recv,
    send,
    recv,
):
    me = lax.axis_index("seq")
    head = lax.axis_index("head")
    chips = head_count // 2
    rounds, owners = conv.shape[0], conv.shape[1]
    chunks = rounds * owners
    inner = gate.shape[3]
    mixed = conv.shape[3] // 2
    rows = rounds * CHUNK
    slots = [(dy, dc) for dy in range(chips) for dc in range(2)]
    peers = [head_peer(head, chips, dy, dc) for dy, dc in slots]
    up, down, partner = peers[2], peers[2 * chips - 2], peers[1]

    def fetch(src, dst, n):
        copy = pltpu.make_async_copy(src, dst, load.at[n])
        copy.start()
        return copy

    def part(k):
        return pl.ds(k * inner, inner)

    conv_in = [fetch(conv_hbm.at[q], conv.at[q], q) for q in range(rounds)]
    fresh_in = fetch(fresh_hbm, fresh, rounds)
    gate_in = fetch(gate_hbm, gate, rounds + 1)
    mine = pl.ds(pl.multiple_of(head * rows, rows), rows)
    half = inner // 2
    side = (2 * chips - 2) * inner
    far = 4 * inner
    top, bottom = pl.ds(0, half), pl.ds(half, half)
    late = [
        fetch(hidden_hbm.at[mine, :], rest, rounds + 2),
        fetch(w_hbm, weight.at[part(0)], rounds + 3),
        fetch(hop_hbm.at[2], weight.at[part(1)], rounds + 4),
        fetch(hop_hbm.at[0, top], weight.at[pl.ds(2 * inner, half)], rounds + 5),
        fetch(hop_hbm.at[1, bottom], weight.at[pl.ds(side + half, half)], rounds + 6),
    ]

    greet(
        [{"seq": (me + k) % seq_count} for k in range(1, seq_count)]
        + [{"head": p} for p in peers[1:]]
    )
    started = []

    def start(copy):
        copy.start()
        started.append(copy)
        return copy

    travelling = []
    for k in range(1, seq_count):
        target = (me + k) % seq_count
        backward = (me + k) // seq_count
        travelling.append(
            start(
                remote(
                    end_ref.at[backward], ends.at[k], seq_send.at[0, k], seq_recv.at[0, k], seq=target
                )
            )
        )
        travelling.append(
            start(remote(total_ref, totals.at[k], seq_send.at[1, k], seq_recv.at[1, k], seq=target))
        )
    def weigh(n, src, row, where, count=half):
        at = weight.at[pl.ds(row, count)]
        return start(remote(src, at, w_send.at[n], w_recv.at[n], head=where))

    u1 = weigh(0, w_hbm.at[bottom], 2 * inner + half, up)
    u2 = weigh(1, w_hbm.at[top], side, down)
    t1 = weigh(2, hop_hbm.at[0, top], far, up)
    t3 = weigh(3, hop_hbm.at[1, bottom], far + half, down)
    beside = [
        weigh(4, hop_hbm.at[0, top], 3 * inner, partner),
        weigh(5, hop_hbm.at[1, bottom], side + inner + half, partner),
    ]

    def cross():
        for copy in (u1, u2, t1, t3):
            copy.wait_recv()
        return [
            weigh(6, weight.at[pl.ds(2 * inner + half, half)], 3 * inner + half, partner),
            weigh(7, weight.at[pl.ds(side, half)], side + inner, partner),
            weigh(8, weight.at[part(4)], 5 * inner, partner, inner),
        ]

    i = lax.broadcasted_iota(jnp.int32, (CHUNK, CHUNK), 0)
    j = lax.broadcasted_iota(jnp.int32, (CHUNK, CHUNK), 1)
    lower = i >= j
    upper = i <= j
    low = j < HEAD_DIM
    skip = head_lanes([jnp.full((1, 1), skip_ref[h], f32) for h in range(4)])
    sub = lax.broadcasted_iota(jnp.int32, (8, CHUNK), 0)
    line = lax.broadcasted_iota(jnp.int32, pick.shape[1:], 0)
    block = lax.broadcasted_iota(jnp.int32, pick.shape[1:], 1) // CHUNK
    sign = jnp.where(block < 4, 1.0, -1.0)
    chosen = jnp.where((line < 24) & (line % 8 == block), sign, 0.0).astype(bf16)
    for u in range(pick.shape[0]):
        pick[u] = chosen
    line = lax.broadcasted_iota(jnp.int32, spread.shape, 0)
    lane = lax.broadcasted_iota(jnp.int32, spread.shape, 1)
    wanted = (lane // inner) * 8 + (lane % inner) // HEAD_DIM
    spread[...] = (line % 16 == wanted).astype(f32).astype(bf16)

    def within(q, d, u):
        c = d * rounds + q
        row = row_ref[c]
        lines = jnp.concatenate(split(jnp.where(sub < 4, -row, row), 3), axis=0)
        for n in range(8):
            own = lax.broadcasted_iota(jnp.int32, lines.shape, 0) % 8 == n
            pick[u, 32:56, n * CHUNK : (n + 1) * CHUNK] = jnp.where(own, lines, 0.0).astype(bf16)
        left = jnp.concatenate(
            split(cols_ref[c, 0:8, :], 3)
            + [jnp.zeros((8, CHUNK), f32), jnp.ones((24, CHUNK), f32), jnp.zeros((8, CHUNK), f32)],
            axis=0,
        ).astype(bf16)
        made = mm(left, pick[u], TN)
        pair = []
        for e, keep in ((0, lower), (1, upper)):
            base = e * mixed + inner
            write = conv[q, d, :, base : base + STATE]
            read = conv[q, d, :, base + STATE : base + 2 * STATE]
            pair.append(jnp.where(keep, mm(read, write, NT), 0.0))
        for p in range(2):
            weights = ([], [])
            for h in (2 * p, 2 * p + 1):
                table = jnp.exp2(
                    jnp.where(
                        lower,
                        made[:, h * CHUNK : (h + 1) * CHUNK],
                        made[:, (4 + h) * CHUNK : (5 + h) * CHUNK],
                    )
                )
                for e in range(2):
                    weights[e].append((pair[e] * table).astype(bf16))
            for e in range(2):
                at = e * mixed + p * CHUNK
                x = conv[q, d, :, at : at + CHUNK]
                zero = jnp.zeros_like(x)
                stacked = jnp.concatenate([jnp.where(low, x, zero), jnp.where(low, zero, x)], axis=0)
                made_here = mm(jnp.concatenate(weights[e], axis=1), stacked)
                made_here = made_here + skip[:, p * CHUNK : (p + 1) * CHUNK] * x.astype(f32)
                inside[q, d, :, e * inner + p * CHUNK : e * inner + (p + 1) * CHUNK] = made_here

    for q in range(rounds):
        conv_in[q].wait()

        def step(n, carry, q=q):
            for u in range(2):
                within(q, 2 * n + u, u)
            return carry

        lax.fori_loop(0, owners // 2, step, 0)

    for copy in travelling:
        copy.wait_recv()
    incoming[...] = jnp.zeros_like(incoming)
    for k in range(seq_count - 1, 0, -1):

        @pl.when(k <= me)
        def _(k=k):
            incoming[0] = incoming[0] * jnp.exp2(totals[k, 0:1, :]) + ends[k].astype(f32)

    for k in range(1, seq_count):

        @pl.when(k > me)
        def _(k=k):
            incoming[1] = incoming[1] * jnp.exp2(totals[k, 0:1, :]) + ends[k].astype(f32)

    fresh_in.wait()

    def passing(c):
        return jnp.exp2(head_lanes([cols_ref[c, h : h + 1, CHUNK - 1 :] for h in range(4)]))

    def walk(n, carry):
        for e in range(2):
            at = [2 * n, 2 * n + 1] if e == 0 else [chunks - 1 - 2 * n, chunks - 2 - 2 * n]
            factors = [passing(c) for c in at]
            for lanes in (slice(0, inner // 2), slice(inner // 2, inner)):
                state = incoming[e, :, lanes]
                for c, factor in zip(at, factors):
                    entry[e, c, :, lanes] = state.astype(bf16)
                    state = state * factor[:, lanes] + fresh[c, e, :, lanes].astype(f32)
                incoming[e, :, lanes] = state
        return carry

    lax.fori_loop(0, chunks // 2, walk, 0)
    gate_in.wait()

    ones = jnp.ones((8, inner), bf16)
    gain = gain_ref[...].reshape(1, -1).astype(f32)
    sixteen = lax.broadcasted_iota(jnp.int32, (2 * owners, CHUNK), 0)

    def carried(q, d, sums):
        c = d * rounds + q
        left = jnp.concatenate(split(cols_ref[c, 8:24, :], 2), axis=0).astype(bf16)
        scale = mm(left, spread[...], TN)
        act = silu(gate[q, d].astype(f32))
        for e in range(2):
            at = e * mixed + inner + STATE
            lanes = slice(e * inner, (e + 1) * inner)
            part_in = mm(conv[q, d, :, at : at + STATE], entry[e, c])
            value = (inside[q, d, :, lanes] + part_in * scale[:, lanes]) * act
            gated[q, d, :, lanes] = value.astype(bf16)
            square = mm(ones, (value * value).astype(bf16), NT)
            square = jnp.concatenate([square] * (2 * owners // 8), axis=0)
            sums = jnp.where(sixteen == 2 * d + e, square, sums)
        return sums

    def combine(q):
        for k in range(1, head_count):
            ss[q][k - 1].wait_recv()
        total = squares[q]
        for k in range(1, head_count):
            total = total + others[q, k]
        total = lax.rsqrt(total * (1.0 / (inner * head_count)) + epsilon)
        scale = jnp.concatenate([total, jnp.zeros((CHUNK - 2 * owners, CHUNK), f32)], axis=0).T
        for d in range(owners):
            both = gated[q, d, :, :inner].astype(f32) * scale[:, 2 * d : 2 * d + 1]
            both = both + gated[q, d, :, inner:].astype(f32) * scale[:, 2 * d + 1 : 2 * d + 2]
            sending[q, d] = (both * gain).astype(bf16)
        arrived[q * CHUNK : (q + 1) * CHUNK, 0:inner] = sending[q, head]
        return [
            start(
                remote(
                    sending.at[q, peers[k]],
                    arrived.at[pl.ds(q * CHUNK, CHUNK), part(k)],
                    send.at[q, k],
                    recv.at[q, k],
                    head=peers[k],
                )
            )
            for k in sorted(range(1, head_count), key=lambda k: -min(slots[k][0], chips - slots[k][0]))
        ]

    ss, pieces = [], []
    for q in range(rounds):
        def some(n, sums, q=q):
            for u in range(4):
                sums = carried(q, 4 * n + u, sums)
            return sums

        squares[q] = lax.fori_loop(0, owners // 4, some, jnp.zeros((2 * owners, CHUNK), f32))
        ss.append(
            [
                start(
                    remote(
                        squares.at[q], others.at[q, k], ss_send.at[q, k], ss_recv.at[q, k], head=peers[k]
                    )
                )
                for k in range(1, head_count)
            ]
        )
        if q:
            pieces.append(combine(q - 1))
        if q == 0:
            beside += cross()
    pieces.append(combine(rounds - 1))

    for copy in late:
        copy.wait()
    for copy in beside:
        copy.wait_recv()
    width = out_ref.shape[1]
    step_lanes = 256
    early = (rounds - 1) * CHUNK
    for first, count, done in ((0, early, pieces[:-1]), (early, CHUNK, pieces[-1:])):
        for batch in done:
            for copy in batch:
                copy.wait_recv()
        if count:

            def project_out(b, carry, first=first, count=count):
                lanes = pl.ds(pl.multiple_of(b * step_lanes, step_lanes), step_lanes)
                here = pl.ds(first, count)
                out_ref[here, lanes] = (
                    mm(arrived[here, :], weight[:, lanes]) + rest[here, lanes].astype(f32)
                ).astype(bf16)
                return carry

            lax.fori_loop(0, width // step_lanes, project_out, 0)
    for copy in started:
        copy.wait_send()


def finish(mesh_shape, end, total, cols, row, skip, gain, conv, gate, fresh, hidden, w, hop):
    seq_count, head_count = mesh_shape
    rounds, owners = conv.shape[:2]
    rows = rounds * CHUNK
    inner = gate.shape[3]
    width = hidden.shape[1]
    dma = pltpu.SemaphoreType.DMA
    return pl.pallas_call(
        functools.partial(finish_kernel, seq_count, head_count),
        in_specs=[
            whole(end.shape),
            whole(total.shape),
            whole(cols.shape),
            whole(row.shape),
            SMEM_SPEC,
            whole(gain.shape),
        ]
        + [ANY_SPEC] * 6,
        out_specs=whole((rows, width)),
        out_shape=jax.ShapeDtypeStruct((rows, width), bf16),
        scratch_shapes=[
            pltpu.VMEM(conv.shape, bf16),
            pltpu.VMEM(gate.shape, bf16),
            pltpu.VMEM(fresh.shape, bf16),
            pltpu.VMEM((rows, width), bf16),
            pltpu.VMEM((head_count * inner, width), bf16),
            pltpu.VMEM((seq_count,) + end.shape[1:], bf16),
            pltpu.VMEM((seq_count,) + total.shape, f32),
            pltpu.VMEM(end.shape, f32),
            pltpu.VMEM((2, rounds * owners) + end.shape[1:], bf16),
            pltpu.VMEM((2, 64, 8 * CHUNK), bf16),
            pltpu.VMEM((32, 2 * inner), bf16),
            pltpu.VMEM((rounds, owners, CHUNK, 2 * inner), f32),
            pltpu.VMEM((rounds, owners, CHUNK, 2 * inner), bf16),
            pltpu.VMEM((rounds, 2 * owners, CHUNK), f32),
            pltpu.VMEM((rounds, head_count, 2 * owners, CHUNK), f32),
            pltpu.VMEM((rounds, head_count, CHUNK, inner), bf16),
            pltpu.VMEM((rows, head_count * inner), bf16),
            dma((rounds + 7,)),
            dma((2, seq_count)),
            dma((2, seq_count)),
            dma((9,)),
            dma((9,)),
            dma((rounds, head_count)),
            dma((rounds, head_count)),
            dma((rounds, head_count)),
            dma((rounds, head_count)),
        ],
        compiler_params=params(collective_id=1, has_side_effects=True),
        name="finish",
    )(end, total, cols, row, skip, gain, conv, gate, fresh, hidden, w, hop)


def local(
    hidden_in,
    norm_gain,
    gate_weight,
    value_weight,
    state_weight,
    step_weight,
    step_bias,
    decay_log,
    skip_gain,
    conv_value,
    conv_state,
    output_gain,
    output_weight,
    piece_lengths,
):
    seq_count, head_count = lax.axis_size("seq"), lax.axis_size("head")
    shape = (seq_count, head_count)
    gate, mix, raw, halo, hop = project(
        shape, hidden_in, norm_gain, gate_weight, value_weight, state_weight, step_weight.T, output_weight
    )
    conv, fresh, cols, row, end, total = states(
        "seq",
        head_count,
        mix,
        halo,
        norm_gain,
        value_weight,
        state_weight,
        raw,
        piece_lengths,
        step_bias,
        decay_log,
        conv_value,
        conv_state,
    )
    return finish(
        shape,
        end,
        total,
        cols,
        row,
        skip_gain,
        output_gain,
        conv,
        gate,
        fresh,
        hidden_in,
        output_weight,
        hop,
    )


def solution(mesh):
    in_specs = (
        P("seq", None),
        P(),
        P(None, "head"),
        P(None, "head"),
        P(),
        P(None, "head"),
        P("head"),
        P("head"),
        P("head"),
        P(None, "head"),
        P(),
        P("head"),
        P("head", None),
        P(),
    )
    out_specs = P(("seq", "head"), None)
    return jax.shard_map(local, mesh=mesh, in_specs=in_specs, out_specs=out_specs, check_vma=False)
```

```python
import functools
import math

import jax
import jax.numpy as jnp
from jax import lax
from jax.experimental import pallas as pl
from jax.experimental.pallas import tpu as pltpu
from jax.sharding import PartitionSpec as P

HEAD_DIM = 64
STATE = 128
CONV = 4
CHUNK = 128
PIECES = 16
HALO = 16
REACH = 8
RESET = 256.0
LOG2E = math.log2(math.e)

f32 = jnp.float32
bf16 = jnp.bfloat16
epsilon = 1e-05
MESH = pl.DeviceIdType.MESH
NN = (((1,), (0,)), ((), ()))
NT = (((1,), (1,)), ((), ()))
TN = (((0,), (0,)), ((), ()))


def mm(a, b, dims=NN, precision=None):
    return lax.dot_general(a, b, dims, precision=precision, preferred_element_type=f32)


def silu(x):
    half = 0.5 * x
    return half * jnp.tanh(half) + half


def normalized(h, gain):
    wide = h.astype(f32)
    scale = lax.rsqrt(jnp.mean(wide * wide, axis=1, keepdims=True) + epsilon)
    return (wide * scale * gain.astype(f32)).astype(bf16)


def whole(shape):
    zeros = (0,) * len(shape)
    return pl.BlockSpec(shape, lambda *_: zeros)


SMEM_SPEC = pl.BlockSpec(memory_space=pltpu.SMEM)
ANY_SPEC = pl.BlockSpec(memory_space=pl.ANY)


def params(**kw):
    return pltpu.CompilerParams(vmem_limit_bytes=60 * 1024 * 1024, **kw)


def remote(src, dst, send, recv, **where):
    return pltpu.make_async_remote_copy(
        src_ref=src,
        dst_ref=dst,
        send_sem=send,
        recv_sem=recv,
        device_id=where,
        device_id_type=MESH,
    )


def greet(axes_and_peers):
    barrier = pltpu.get_barrier_semaphore()
    for where in axes_and_peers:
        pl.semaphore_signal(barrier, inc=1, device_id=where, device_id_type=MESH)
    pl.semaphore_wait(barrier, len(axes_and_peers))


def head_peer(me, chips, dy, dc):
    y, core = me // 2, me % 2
    return ((y + dy) % chips) * 2 + (core + dc) % 2


def project_copies(seq_count, head_count, hidden, w, halo, hop, send, recv):
    me = lax.axis_index("seq")
    head = lax.axis_index("head")
    chips = head_count // 2
    tokens = hidden.shape[0]
    after = (me + 1) % seq_count
    before = (me + seq_count - 1) % seq_count
    first, last = pl.ds(0, HALO), pl.ds(tokens - HALO, HALO)
    low, high = pl.ds(0, HALO), pl.ds(HALO, HALO)
    half = w.shape[0] // 2
    top, bottom = pl.ds(0, half), pl.ds(half, half)
    up = head_peer(head, chips, 1, 0)
    down = head_peer(head, chips, chips - 1, 0)
    partner = head_peer(head, chips, 0, 1)
    return (
        remote(hidden.at[last], halo.at[low], send.at[0], recv.at[0], seq=after),
        remote(hidden.at[first], halo.at[high], send.at[1], recv.at[1], seq=before),
        remote(w.at[top], hop.at[0, top], send.at[2], recv.at[2], head=up),
        remote(w.at[bottom], hop.at[1, bottom], send.at[3], recv.at[3], head=down),
        remote(w, hop.at[2], send.at[4], recv.at[4], head=partner),
    ), [{"seq": after}, {"seq": before}, {"head": up}, {"head": down}, {"head": partner}]


def project_kernel(
    mesh_shape,
    h_ref,
    gain_ref,
    vw_ref,
    sw_ref,
    tw_ref,
    hidden,
    w,
    norm_ref,
    mix_ref,
    raw_ref,
    halo,
    hop,
    turned,
    rows,
    send,
    recv,
):
    i = pl.program_id(0)
    copies, peers = project_copies(*mesh_shape, hidden, w, halo, hop, send, recv)
    barrier = pltpu.get_barrier_semaphore()

    @pl.when(i == 0)
    def _():
        for where in peers:
            pl.semaphore_signal(barrier, inc=1, device_id=where, device_id_type=MESH)
        narrow = tw_ref[...].astype(f32)
        turned[...] = jnp.concatenate([narrow, narrow], axis=0).astype(bf16)

    @pl.when(i == 1)
    def _():
        pl.semaphore_wait(barrier, len(peers))
        for copy in copies:
            copy.start()

    inner = vw_ref.shape[1]
    gain = gain_ref[...].reshape(1, -1)
    deep = min(256, h_ref.shape[0])
    for first in range(0, h_ref.shape[0], deep):
        for r in range(first, first + deep, 32):
            n = normalized(h_ref[r : r + 32, :], gain)
            rows[r : r + 32, :] = n
            norm_ref[r // CHUNK, 0, r % CHUNK : r % CHUNK + 32, :] = n
        at = slice(first, first + deep)
        n = rows[at, :]
        mix_ref[at, :inner] = mm(n, vw_ref[...]).astype(bf16)
        mix_ref[at, inner:] = mm(n, sw_ref[...]).astype(bf16)
        raw = mm(turned[...], n, NT)
        for q in range(deep // CHUNK):
            raw_ref[first // CHUNK + q] = raw[:, q * CHUNK : (q + 1) * CHUNK]

    @pl.when(i == pl.num_programs(0) - 1)
    def _():
        for copy in copies:
            copy.wait()


def project(mesh_shape, hidden, gain, vw, sw, tw, w):
    tokens, width = hidden.shape
    inner = vw.shape[1]
    mixed = inner + sw.shape[1]
    rows = tokens // mesh_shape[1]
    rounds = rows // CHUNK
    return pl.pallas_call(
        functools.partial(project_kernel, mesh_shape),
        grid=(tokens // rows,),
        in_specs=[
            pl.BlockSpec((rows, width), lambda i: (i, 0)),
            whole(gain.shape),
            whole(vw.shape),
            whole(sw.shape),
            whole(tw.shape),
            ANY_SPEC,
            ANY_SPEC,
        ],
        out_specs=[
            pl.BlockSpec((rounds, 1, CHUNK, width), lambda i: (0, i, 0, 0)),
            pl.BlockSpec((rows, mixed), lambda i: (i, 0)),
            pl.BlockSpec((rows // CHUNK, 8, CHUNK), lambda i: (i, 0, 0)),
            ANY_SPEC,
            ANY_SPEC,
        ],
        out_shape=[
            jax.ShapeDtypeStruct((rounds, tokens // rows, CHUNK, width), bf16),
            jax.ShapeDtypeStruct((tokens, mixed), bf16),
            jax.ShapeDtypeStruct((tokens // CHUNK, 8, CHUNK), f32),
            jax.ShapeDtypeStruct((2 * HALO, width), bf16),
            jax.ShapeDtypeStruct((3,) + w.shape, bf16),
        ],
        scratch_shapes=[
            pltpu.VMEM((8, width), bf16),
            pltpu.VMEM((rows, width), bf16),
            pltpu.SemaphoreType.DMA((5,)),
            pltpu.SemaphoreType.DMA((5,)),
        ],
        compiler_params=params(collective_id=2, has_side_effects=True),
        name="project",
    )(hidden, gain, vw, sw, tw, hidden, w)


def head_lanes(columns):
    low = lax.broadcasted_iota(jnp.int32, (columns[0].shape[0], 2 * HEAD_DIM), 1) < HEAD_DIM
    pairs = [
        jnp.where(low, columns[2 * p], columns[2 * p + 1]) for p in range(len(columns) // 2)
    ]
    return jnp.concatenate(pairs, axis=1)


def decays(first_row, raw, lens_ref, bias_ref, rate_ref):
    chunks = raw.shape[0]
    shape = (chunks, 8, CHUNK)
    sub = lax.broadcasted_iota(jnp.int32, shape, 1)
    upper = sub < 4
    head = jnp.where(upper, sub, sub - 4)
    pos = (
        first_row
        + lax.broadcasted_iota(jnp.int32, shape, 0) * CHUNK
        + lax.broadcasted_iota(jnp.int32, shape, 2)
    )
    start = jnp.zeros(shape, jnp.int32)
    stop = jnp.full(shape, 1 << 30, jnp.int32)
    edge = jnp.int32(0)
    for k in range(PIECES):
        start = jnp.where(pos >= edge, edge, start)
        edge = edge + lens_ref[k]
        stop = jnp.minimum(stop, jnp.where(edge > pos, edge, 1 << 30))
    since = pos - start
    until = stop - 1 - pos
    bias = jnp.zeros(shape, f32)
    rate = jnp.zeros(shape, f32)
    for h in range(4):
        bias = jnp.where(head == h, bias_ref[h], bias)
        rate = jnp.where(head == h, rate_ref[h], rate)
    rate = jnp.exp(rate) * (-LOG2E)
    z = raw + bias
    step = jnp.maximum(z, 0.0) + jnp.log1p(jnp.exp(-jnp.abs(z)))
    log = step * rate
    reset = jnp.where(since == 0, -RESET, 0.0)
    ones = (
        lax.broadcasted_iota(jnp.int32, (CHUNK, CHUNK), 0)
        <= lax.broadcasted_iota(jnp.int32, (CHUNK, CHUNK), 1)
    ).astype(f32)
    cum = mm(
        (log + reset).reshape(chunks * 8, CHUNK), ones, precision=lax.Precision.HIGHEST
    ).reshape(shape)
    excl = cum - log
    total = cum[:, :, CHUNK - 1 :]
    log_step = jnp.where(step > 0.0, jnp.log2(step), -RESET)
    row = jnp.where(upper, cum - log_step, excl + log_step)
    g1 = jnp.where(upper, cum, excl)
    g2 = jnp.where(upper, jnp.exp2(cum), jnp.exp2(total - cum) * step)
    g3 = jnp.where(upper, jnp.exp2(total - excl), jnp.exp2(excl) * step)
    g4 = jnp.where(upper, since, until).astype(f32)
    return row, g1, g2, g3, g4


def states_kernel(
    axis,
    mix_ref,
    before_ref,
    after_ref,
    halo_ref,
    gain_ref,
    vw_ref,
    sw_ref,
    raw_ref,
    lens_ref,
    bias_ref,
    rate_ref,
    cv_ref,
    cs_ref,
    conv_ref,
    fresh_ref,
    cols_ref,
    row_ref,
    end_ref,
    total_ref,
    prod,
    halo,
    run,
    reach,
    spread,
    near,
):
    g = pl.program_id(0)
    groups = pl.num_programs(0)
    inner = vw_ref.shape[1]
    rows, mixed = mix_ref.shape
    rounds = rows // CHUNK
    blocks = mixed // 128
    first_row = lax.axis_index(axis) * (groups * rows)

    @pl.when(g == 0)
    def _():
        n = normalized(halo_ref[...], gain_ref[...].reshape(1, -1))
        halo[:, :inner] = mm(n, vw_ref[...]).astype(bf16).astype(f32)
        halo[:, inner:] = mm(n, sw_ref[...]).astype(bf16).astype(f32)
        row, g1, g2, g3, g4 = decays(first_row, raw_ref[...], lens_ref, bias_ref, rate_ref)
        row_ref[...] = row
        cols_ref[:, 0:8, :] = g1
        cols_ref[:, 8:16, :] = g2
        cols_ref[:, 16:24, :] = g3
        cols_ref[:, 24:32, :] = g4
        run[...] = jnp.zeros_like(run)
        reach[...] = jnp.zeros_like(reach)
        line = lax.broadcasted_iota(jnp.int32, spread.shape, 0) % 32
        lane = lax.broadcasted_iota(jnp.int32, spread.shape, 1)
        wanted = 12 + (lane // inner) * 8 + (lane % inner) // HEAD_DIM
        spread[...] = (line == wanted).astype(f32).astype(bf16)

        def clear(k, carry):
            near[k] = 0
            return carry

        lax.fori_loop(0, near.shape[0], clear, 0)

        def mark(k, edge):
            for shift in (-(CONV - 1), CONV - 2):
                at = (edge + shift - first_row + rows) // rows
                near[jnp.clip(at, 0, near.shape[0] - 1)] = 1
            return edge + lens_ref[jnp.minimum(k, PIECES - 1)]

        lax.fori_loop(0, PIECES + 1, mark, jnp.int32(0))

    taps = jnp.concatenate([cv_ref[...], cs_ref[...]], axis=1).astype(f32) * 0.5

    def put(b, at, values):
        lanes = slice(b * 128, (b + 1) * 128)
        for k in range(CONV - 1):
            prod[k, b, at : at + values.shape[0], :] = values * taps[k : k + 1, lanes]

    def ready(q):
        for b in range(blocks):
            lanes = slice(b * 128, (b + 1) * 128)
            put(b, REACH + q * CHUNK, mix_ref[q * CHUNK : (q + 1) * CHUNK, lanes].astype(f32))

    def group(masked):
        for b in range(blocks):
            lanes = slice(b * 128, (b + 1) * 128)
            ahead = before_ref[:, lanes].astype(f32)[16 - REACH :, :]
            put(b, 0, jnp.where(g == 0, halo[HALO - REACH : HALO, lanes], ahead))
            behind = after_ref[:, lanes].astype(f32)[:REACH, :]
            put(b, REACH + rows, jnp.where(g == groups - 1, halo[HALO : HALO + REACH, lanes], behind))
        ready(0)
        for q in range(rounds):
            if q + 1 < rounds:
                ready(q + 1)
            chunk(q, masked)

    def chunk(q, masked):
        cols = cols_ref[g * rounds + q]
        high = cols.astype(bf16).astype(f32)
        both = jnp.concatenate([high, cols - high], axis=0).astype(bf16)
        tails = mm(both, spread[...], TN)
        passing = head_lanes([cols[h : h + 1, CHUNK - 1 :] for h in range(4)])
        if masked:
            turned = jnp.concatenate([cols, jnp.zeros((CHUNK - 32, CHUNK), f32)], axis=0).T
            sides = [jnp.broadcast_to(turned[:, r : r + 1], (CHUNK, 128)) for r in (24, 28)]
        write = [None, None]
        for b in [inner // 128] + list(range(inner // 128)) + list(range(inner // 128 + 1, blocks)):
            lanes = slice(b * 128, (b + 1) * 128)
            centre = mix_ref[q * CHUNK : (q + 1) * CHUNK, lanes].astype(f32) * taps[CONV - 1 : CONV, lanes]
            for d in range(2):
                half = centre
                for distance in range(1, CONV):
                    at = REACH + q * CHUNK + (distance if d else -distance)
                    term = prod[CONV - 1 - distance, b, at : at + CHUNK, :]
                    if masked:
                        term = jnp.where(sides[d] >= distance, term, 0.0)
                    half = half + term
                value = half * jnp.tanh(half) + half
                at = d * mixed + b * 128
                narrow = value.astype(bf16)
                conv_ref[q, 0, :, at : at + 128] = narrow
                if b == inner // 128:
                    write[d] = narrow
                elif b < inner // 128:
                    at = d * inner + b * 128
                    scaled = (value * tails[:, at : at + 128]).astype(bf16)
                    fresh = mm(write[d], scaled, TN)
                    fresh_ref[q, d, :, lanes] = fresh.astype(bf16)
                    if d == 0:
                        run[0, :, lanes] = run[0, :, lanes] * jnp.exp2(passing[:, lanes]) + fresh
                    else:
                        run[1, :, lanes] = run[1, :, lanes] + jnp.exp2(reach[0:1, lanes]) * fresh
        reach[...] = reach[...] + passing

    edges = near[g + 1]

    @pl.when(edges == 0)
    def _():
        group(False)

    @pl.when(edges != 0)
    def _():
        group(True)

    @pl.when(g == groups - 1)
    def _():
        end_ref[...] = run[...].astype(bf16)
        total_ref[...] = reach[...]


def states(axis, owners, mix, halo, gain, vw, sw, raw, lens, bias, rate, cv, cs):
    tokens, mixed = mix.shape
    chunks = tokens // CHUNK
    inner = vw.shape[1]
    rounds = chunks // owners
    rows = rounds * CHUNK
    per = rows // 16
    last = tokens // 16 - 1
    return pl.pallas_call(
        functools.partial(states_kernel, axis),
        grid=(owners,),
        in_specs=[
            pl.BlockSpec((rows, mixed), lambda c: (c, 0)),
            pl.BlockSpec((16, mixed), lambda c: (jnp.maximum(c * per - 1, 0), 0)),
            pl.BlockSpec((16, mixed), lambda c: (jnp.minimum(c * per + per, last), 0)),
            whole(halo.shape),
            whole(gain.shape),
            whole(vw.shape),
            whole(sw.shape),
            whole(raw.shape),
            SMEM_SPEC,
            SMEM_SPEC,
            SMEM_SPEC,
            whole(cv.shape),
            whole(cs.shape),
        ],
        out_specs=[
            pl.BlockSpec((rounds, 1, CHUNK, 2 * mixed), lambda c: (0, c, 0, 0)),
            pl.BlockSpec((rounds, 2, STATE, inner), lambda c: (c, 0, 0, 0)),
            whole((chunks, 32, CHUNK)),
            whole((chunks, 8, CHUNK)),
            whole((2, STATE, inner)),
            whole((8, inner)),
        ],
        out_shape=[
            jax.ShapeDtypeStruct((rounds, owners, CHUNK, 2 * mixed), bf16),
            jax.ShapeDtypeStruct((chunks, 2, STATE, inner), bf16),
            jax.ShapeDtypeStruct((chunks, 32, CHUNK), f32),
            jax.ShapeDtypeStruct((chunks, 8, CHUNK), f32),
            jax.ShapeDtypeStruct((2, STATE, inner), bf16),
            jax.ShapeDtypeStruct((8, inner), f32),
        ],
        scratch_shapes=[
            pltpu.VMEM((CONV - 1, mixed // 128, rows + 2 * REACH, 128), f32),
            pltpu.VMEM((2 * HALO, mixed), f32),
            pltpu.VMEM((2, STATE, inner), f32),
            pltpu.VMEM((8, inner), f32),
            pltpu.VMEM((64, 2 * inner), bf16),
            pltpu.SMEM((owners + 2,), jnp.int32),
        ],
        compiler_params=params(),
        name="states",
    )(mix, mix, mix, halo, gain, vw, sw, raw, lens, bias, rate, cv, cs)


def split(x, parts):
    pieces = []
    for _ in range(parts - 1):
        pieces.append(x.astype(bf16).astype(f32))
        x = x - pieces[-1]
    return pieces + [x]


def finish_kernel(
    seq_count,
    head_count,
    end_ref,
    total_ref,
    cols_ref,
    row_ref,
    skip_ref,
    gain_ref,
    gw_ref,
    conv_hbm,
    norm_hbm,
    fresh_hbm,
    hidden_hbm,
    w_hbm,
    hop_hbm,
    out_ref,
    conv,
    normed,
    gate,
    fresh,
    rest,
    weight,
    ends,
    totals,
    incoming,
    entry,
    pick,
    spread,
    inside,
    gated,
    squares,
    others,
    sending,
    arrived,
    load,
    seq_send,
    seq_recv,
    w_send,
    w_recv,
    ss_send,
    ss_recv,
    send,
    recv,
):
    me = lax.axis_index("seq")
    head = lax.axis_index("head")
    chips = head_count // 2
    rounds, owners = conv.shape[0], conv.shape[1]
    chunks = rounds * owners
    inner = gate.shape[3]
    mixed = conv.shape[3] // 2
    rows = rounds * CHUNK
    slots = [(dy, dc) for dy in range(chips) for dc in range(2)]
    peers = [head_peer(head, chips, dy, dc) for dy, dc in slots]
    up, down, partner = peers[2], peers[2 * chips - 2], peers[1]

    def fetch(src, dst, n):
        copy = pltpu.make_async_copy(src, dst, load.at[n])
        copy.start()
        return copy

    def part(k):
        return pl.ds(k * inner, inner)

    conv_in, norm_in = [], []
    for q in range(rounds):
        conv_in.append(fetch(conv_hbm.at[q], conv.at[q], q))
        norm_in.append(fetch(norm_hbm.at[q], normed.at[q], rounds + 7 + q))
    fresh_in = fetch(fresh_hbm, fresh, rounds)
    mine = pl.ds(pl.multiple_of(head * rows, rows), rows)
    half = inner // 2
    side = (2 * chips - 2) * inner
    far = 4 * inner
    top, bottom = pl.ds(0, half), pl.ds(half, half)
    late = [
        fetch(hidden_hbm.at[mine, :], rest, rounds + 2),
        fetch(w_hbm, weight.at[part(0)], rounds + 3),
        fetch(hop_hbm.at[2], weight.at[part(1)], rounds + 4),
        fetch(hop_hbm.at[0, top], weight.at[pl.ds(2 * inner, half)], rounds + 5),
        fetch(hop_hbm.at[1, bottom], weight.at[pl.ds(side + half, half)], rounds + 6),
    ]

    greet(
        [{"seq": (me + k) % seq_count} for k in range(1, seq_count)]
        + [{"head": p} for p in peers[1:]]
    )
    started = []

    def start(copy):
        copy.start()
        started.append(copy)
        return copy

    travelling = []
    for k in range(1, seq_count):
        target = (me + k) % seq_count
        backward = (me + k) // seq_count
        travelling.append(
            start(
                remote(
                    end_ref.at[backward], ends.at[k], seq_send.at[0, k], seq_recv.at[0, k], seq=target
                )
            )
        )
        travelling.append(
            start(remote(total_ref, totals.at[k], seq_send.at[1, k], seq_recv.at[1, k], seq=target))
        )
    def weigh(n, src, row, where, count=half):
        at = weight.at[pl.ds(row, count)]
        return start(remote(src, at, w_send.at[n], w_recv.at[n], head=where))

    u1 = weigh(0, w_hbm.at[bottom], 2 * inner + half, up)
    u2 = weigh(1, w_hbm.at[top], side, down)
    t1 = weigh(2, hop_hbm.at[0, top], far, up)
    t3 = weigh(3, hop_hbm.at[1, bottom], far + half, down)
    beside = [
        weigh(4, hop_hbm.at[0, top], 3 * inner, partner),
        weigh(5, hop_hbm.at[1, bottom], side + inner + half, partner),
    ]

    def cross():
        for copy in (u1, u2, t1, t3):
            copy.wait_recv()
        return [
            weigh(6, weight.at[pl.ds(2 * inner + half, half)], 3 * inner + half, partner),
            weigh(7, weight.at[pl.ds(side, half)], side + inner, partner),
            weigh(8, weight.at[part(4)], 5 * inner, partner, inner),
        ]

    i = lax.broadcasted_iota(jnp.int32, (CHUNK, CHUNK), 0)
    j = lax.broadcasted_iota(jnp.int32, (CHUNK, CHUNK), 1)
    lower = i >= j
    upper = i <= j
    low = j < HEAD_DIM
    skip = head_lanes([jnp.full((1, 1), skip_ref[h], f32) for h in range(4)])
    sub = lax.broadcasted_iota(jnp.int32, (8, CHUNK), 0)
    line = lax.broadcasted_iota(jnp.int32, pick.shape[1:], 0)
    block = lax.broadcasted_iota(jnp.int32, pick.shape[1:], 1) // CHUNK
    sign = jnp.where(block < 4, 1.0, -1.0)
    chosen = jnp.where((line < 24) & (line % 8 == block), sign, 0.0).astype(bf16)
    for u in range(pick.shape[0]):
        pick[u] = chosen
    line = lax.broadcasted_iota(jnp.int32, spread.shape, 0)
    lane = lax.broadcasted_iota(jnp.int32, spread.shape, 1)
    wanted = (lane // inner) * 8 + (lane % inner) // HEAD_DIM
    spread[...] = (line % 16 == wanted).astype(f32).astype(bf16)

    def within(q, d, u):
        c = d * rounds + q
        row = row_ref[c]
        lines = jnp.concatenate(split(jnp.where(sub < 4, -row, row), 3), axis=0)
        for n in range(8):
            own = lax.broadcasted_iota(jnp.int32, lines.shape, 0) % 8 == n
            pick[u, 32:56, n * CHUNK : (n + 1) * CHUNK] = jnp.where(own, lines, 0.0).astype(bf16)
        left = jnp.concatenate(
            split(cols_ref[c, 0:8, :], 3)
            + [jnp.zeros((8, CHUNK), f32), jnp.ones((24, CHUNK), f32), jnp.zeros((8, CHUNK), f32)],
            axis=0,
        ).astype(bf16)
        made = mm(left, pick[u], TN)
        pair = []
        for e, keep in ((0, lower), (1, upper)):
            base = e * mixed + inner
            write = conv[q, d, :, base : base + STATE]
            read = conv[q, d, :, base + STATE : base + 2 * STATE]
            pair.append(jnp.where(keep, mm(read, write, NT), 0.0))
        for p in range(2):
            weights = ([], [])
            for h in (2 * p, 2 * p + 1):
                table = jnp.exp2(
                    jnp.where(
                        lower,
                        made[:, h * CHUNK : (h + 1) * CHUNK],
                        made[:, (4 + h) * CHUNK : (5 + h) * CHUNK],
                    )
                )
                for e in range(2):
                    weights[e].append((pair[e] * table).astype(bf16))
            for e in range(2):
                at = e * mixed + p * CHUNK
                x = conv[q, d, :, at : at + CHUNK]
                zero = jnp.zeros_like(x)
                stacked = jnp.concatenate([jnp.where(low, x, zero), jnp.where(low, zero, x)], axis=0)
                made_here = mm(jnp.concatenate(weights[e], axis=1), stacked)
                made_here = made_here + skip[:, p * CHUNK : (p + 1) * CHUNK] * x.astype(f32)
                inside[q, d, :, e * inner + p * CHUNK : e * inner + (p + 1) * CHUNK] = made_here

    def gates(q, n):
        two = normed[q, pl.ds(2 * n, 2)].reshape(2 * CHUNK, normed.shape[3])
        two = mm(two, gw_ref[...]).astype(bf16)
        for u in range(2):
            gate[q, 2 * n + u] = two[u * CHUNK : (u + 1) * CHUNK]

    for q in range(rounds):
        conv_in[q].wait()
        norm_in[q].wait()

        def step(n, carry, q=q):
            if q < 2:
                gates(q, n)
            for u in range(2):
                within(q, 2 * n + u, u)
            return carry

        lax.fori_loop(0, owners // 2, step, 0)

    for copy in travelling:
        copy.wait_recv()
    incoming[...] = jnp.zeros_like(incoming)
    for k in range(seq_count - 1, 0, -1):

        @pl.when(k <= me)
        def _(k=k):
            incoming[0] = incoming[0] * jnp.exp2(totals[k, 0:1, :]) + ends[k].astype(f32)

    for k in range(1, seq_count):

        @pl.when(k > me)
        def _(k=k):
            incoming[1] = incoming[1] * jnp.exp2(totals[k, 0:1, :]) + ends[k].astype(f32)

    fresh_in.wait()

    def passing(c):
        return jnp.exp2(head_lanes([cols_ref[c, h : h + 1, CHUNK - 1 :] for h in range(4)]))

    def walk(n, carry):
        for e in range(2):
            at = [2 * n, 2 * n + 1] if e == 0 else [chunks - 1 - 2 * n, chunks - 2 - 2 * n]
            factors = [passing(c) for c in at]
            for lanes in (slice(0, inner // 2), slice(inner // 2, inner)):
                state = incoming[e, :, lanes]
                for c, factor in zip(at, factors):
                    entry[e, c, :, lanes] = state.astype(bf16)
                    state = state * factor[:, lanes] + fresh[c, e, :, lanes].astype(f32)
                incoming[e, :, lanes] = state
        return carry

    lax.fori_loop(0, chunks // 2, walk, 0)

    ones = jnp.ones((8, inner), bf16)
    gain = gain_ref[...].reshape(1, -1).astype(f32)
    sixteen = lax.broadcasted_iota(jnp.int32, (2 * owners, CHUNK), 0)

    def carried(q, d, sums):
        c = d * rounds + q
        left = jnp.concatenate(split(cols_ref[c, 8:24, :], 2), axis=0).astype(bf16)
        scale = mm(left, spread[...], TN)
        act = silu(gate[q, d].astype(f32))
        for e in range(2):
            at = e * mixed + inner + STATE
            lanes = slice(e * inner, (e + 1) * inner)
            part_in = mm(conv[q, d, :, at : at + STATE], entry[e, c])
            value = (inside[q, d, :, lanes] + part_in * scale[:, lanes]) * act
            gated[q, d, :, lanes] = value.astype(bf16)
            square = mm(ones, (value * value).astype(bf16), NT)
            square = jnp.concatenate([square] * (2 * owners // 8), axis=0)
            sums = jnp.where(sixteen == 2 * d + e, square, sums)
        return sums

    def combine(q):
        for k in range(1, head_count):
            ss[q][k - 1].wait_recv()
        total = squares[q]
        for k in range(1, head_count):
            total = total + others[q, k]
        total = lax.rsqrt(total * (1.0 / (inner * head_count)) + epsilon)
        scale = jnp.concatenate([total, jnp.zeros((CHUNK - 2 * owners, CHUNK), f32)], axis=0).T
        for d in range(owners):
            both = gated[q, d, :, :inner].astype(f32) * scale[:, 2 * d : 2 * d + 1]
            both = both + gated[q, d, :, inner:].astype(f32) * scale[:, 2 * d + 1 : 2 * d + 2]
            sending[q, d] = (both * gain).astype(bf16)
        arrived[q * CHUNK : (q + 1) * CHUNK, 0:inner] = sending[q, head]
        return [
            start(
                remote(
                    sending.at[q, peers[k]],
                    arrived.at[pl.ds(q * CHUNK, CHUNK), part(k)],
                    send.at[q, k],
                    recv.at[q, k],
                    head=peers[k],
                )
            )
            for k in sorted(range(1, head_count), key=lambda k: -min(slots[k][0], chips - slots[k][0]))
        ]

    ss, pieces = [], []
    for q in range(rounds):
        if q >= 2:

            def later(n, carry, q=q):
                gates(q, n)
                return carry

            lax.fori_loop(0, owners // 2, later, 0)

        def some(n, sums, q=q):
            for u in range(4):
                sums = carried(q, 4 * n + u, sums)
            return sums

        squares[q] = lax.fori_loop(0, owners // 4, some, jnp.zeros((2 * owners, CHUNK), f32))
        ss.append(
            [
                start(
                    remote(
                        squares.at[q], others.at[q, k], ss_send.at[q, k], ss_recv.at[q, k], head=peers[k]
                    )
                )
                for k in range(1, head_count)
            ]
        )
        if q:
            pieces.append(combine(q - 1))
        if q == 0:
            beside += cross()
    pieces.append(combine(rounds - 1))

    for copy in late:
        copy.wait()
    for copy in beside:
        copy.wait_recv()
    width = out_ref.shape[1]
    step_lanes = 256
    early = (rounds - 1) * CHUNK
    for first, count, done in ((0, early, pieces[:-1]), (early, CHUNK, pieces[-1:])):
        for batch in done:
            for copy in batch:
                copy.wait_recv()
        if count:

            def project_out(b, carry, first=first, count=count):
                lanes = pl.ds(pl.multiple_of(b * step_lanes, step_lanes), step_lanes)
                here = pl.ds(first, count)
                out_ref[here, lanes] = (
                    mm(arrived[here, :], weight[:, lanes]) + rest[here, lanes].astype(f32)
                ).astype(bf16)
                return carry

            lax.fori_loop(0, width // step_lanes, project_out, 0)
    for copy in started:
        copy.wait_send()


def finish(mesh_shape, end, total, cols, row, skip, gain, gw, conv, normed, fresh, hidden, w, hop):
    seq_count, head_count = mesh_shape
    rounds, owners = conv.shape[:2]
    rows = rounds * CHUNK
    inner = gw.shape[1]
    width = hidden.shape[1]
    dma = pltpu.SemaphoreType.DMA
    return pl.pallas_call(
        functools.partial(finish_kernel, seq_count, head_count),
        in_specs=[
            whole(end.shape),
            whole(total.shape),
            whole(cols.shape),
            whole(row.shape),
            SMEM_SPEC,
            whole(gain.shape),
            whole(gw.shape),
        ]
        + [ANY_SPEC] * 6,
        out_specs=whole((rows, width)),
        out_shape=jax.ShapeDtypeStruct((rows, width), bf16),
        scratch_shapes=[
            pltpu.VMEM(conv.shape, bf16),
            pltpu.VMEM(normed.shape, bf16),
            pltpu.VMEM((rounds, owners, CHUNK, inner), bf16),
            pltpu.VMEM(fresh.shape, bf16),
            pltpu.VMEM((rows, width), bf16),
            pltpu.VMEM((head_count * inner, width), bf16),
            pltpu.VMEM((seq_count,) + end.shape[1:], bf16),
            pltpu.VMEM((seq_count,) + total.shape, f32),
            pltpu.VMEM(end.shape, f32),
            pltpu.VMEM((2, rounds * owners) + end.shape[1:], bf16),
            pltpu.VMEM((2, 64, 8 * CHUNK), bf16),
            pltpu.VMEM((32, 2 * inner), bf16),
            pltpu.VMEM((rounds, owners, CHUNK, 2 * inner), f32),
            pltpu.VMEM((rounds, owners, CHUNK, 2 * inner), bf16),
            pltpu.VMEM((rounds, 2 * owners, CHUNK), f32),
            pltpu.VMEM((rounds, head_count, 2 * owners, CHUNK), f32),
            pltpu.VMEM((rounds, head_count, CHUNK, inner), bf16),
            pltpu.VMEM((rows, head_count * inner), bf16),
            dma((2 * rounds + 7,)),
            dma((2, seq_count)),
            dma((2, seq_count)),
            dma((9,)),
            dma((9,)),
            dma((rounds, head_count)),
            dma((rounds, head_count)),
            dma((rounds, head_count)),
            dma((rounds, head_count)),
        ],
        compiler_params=params(collective_id=1, has_side_effects=True),
        name="finish",
    )(end, total, cols, row, skip, gain, gw, conv, normed, fresh, hidden, w, hop)


def local(
    hidden_in,
    norm_gain,
    gate_weight,
    value_weight,
    state_weight,
    step_weight,
    step_bias,
    decay_log,
    skip_gain,
    conv_value,
    conv_state,
    output_gain,
    output_weight,
    piece_lengths,
):
    seq_count, head_count = lax.axis_size("seq"), lax.axis_size("head")
    shape = (seq_count, head_count)
    normed, mix, raw, halo, hop = project(
        shape, hidden_in, norm_gain, value_weight, state_weight, step_weight.T, output_weight
    )
    conv, fresh, cols, row, end, total = states(
        "seq",
        head_count,
        mix,
        halo,
        norm_gain,
        value_weight,
        state_weight,
        raw,
        piece_lengths,
        step_bias,
        decay_log,
        conv_value,
        conv_state,
    )
    return finish(
        shape,
        end,
        total,
        cols,
        row,
        skip_gain,
        output_gain,
        gate_weight,
        conv,
        normed,
        fresh,
        hidden_in,
        output_weight,
        hop,
    )


def solution(mesh):
    in_specs = (
        P("seq", None),
        P(),
        P(None, "head"),
        P(None, "head"),
        P(),
        P(None, "head"),
        P("head"),
        P("head"),
        P("head"),
        P(None, "head"),
        P(),
        P("head"),
        P("head", None),
        P(),
    )
    out_specs = P(("seq", "head"), None)
    return jax.shard_map(local, mesh=mesh, in_specs=in_specs, out_specs=out_specs, check_vma=False)
```

```python
import functools
import math

import jax
import jax.numpy as jnp
from jax import lax
from jax.experimental import pallas as pl
from jax.experimental.pallas import tpu as pltpu
from jax.sharding import PartitionSpec as P

HEAD_DIM = 64
STATE = 128
CONV = 4
CHUNK = 128
PIECES = 16
HALO = 16
REACH = 8
RESET = 256.0
LOG2E = math.log2(math.e)

f32 = jnp.float32
bf16 = jnp.bfloat16
epsilon = 1e-05
MESH = pl.DeviceIdType.MESH
NN = (((1,), (0,)), ((), ()))
NT = (((1,), (1,)), ((), ()))
TN = (((0,), (0,)), ((), ()))


def mm(a, b, dims=NN, precision=None):
    return lax.dot_general(a, b, dims, precision=precision, preferred_element_type=f32)


def silu(x):
    half = 0.5 * x
    return half * jnp.tanh(half) + half


def normalized(h, gain):
    wide = h.astype(f32)
    scale = lax.rsqrt(jnp.mean(wide * wide, axis=1, keepdims=True) + epsilon)
    return (wide * scale * gain.astype(f32)).astype(bf16)


def whole(shape):
    zeros = (0,) * len(shape)
    return pl.BlockSpec(shape, lambda *_: zeros)


SMEM_SPEC = pl.BlockSpec(memory_space=pltpu.SMEM)
ANY_SPEC = pl.BlockSpec(memory_space=pl.ANY)


def params(**kw):
    return pltpu.CompilerParams(vmem_limit_bytes=60 * 1024 * 1024, **kw)


def remote(src, dst, send, recv, **where):
    return pltpu.make_async_remote_copy(
        src_ref=src,
        dst_ref=dst,
        send_sem=send,
        recv_sem=recv,
        device_id=where,
        device_id_type=MESH,
    )


def greet(axes_and_peers):
    barrier = pltpu.get_barrier_semaphore()
    for where in axes_and_peers:
        pl.semaphore_signal(barrier, inc=1, device_id=where, device_id_type=MESH)
    pl.semaphore_wait(barrier, len(axes_and_peers))


def head_peer(me, chips, dy, dc):
    y, core = me // 2, me % 2
    return ((y + dy) % chips) * 2 + (core + dc) % 2


def project_copies(seq_count, hidden, halo, send, recv):
    me = lax.axis_index("seq")
    tokens = hidden.shape[0]
    after = (me + 1) % seq_count
    before = (me + seq_count - 1) % seq_count
    first, last = pl.ds(0, HALO), pl.ds(tokens - HALO, HALO)
    low, high = pl.ds(0, HALO), pl.ds(HALO, HALO)
    return (
        remote(hidden.at[last], halo.at[low], send.at[0], recv.at[0], seq=after),
        remote(hidden.at[first], halo.at[high], send.at[1], recv.at[1], seq=before),
    ), [{"seq": after}, {"seq": before}]


def project_kernel(
    seq_count,
    h_ref,
    gain_ref,
    vw_ref,
    sw_ref,
    tw_ref,
    hidden,
    norm_ref,
    mix_ref,
    raw_ref,
    halo,
    turned,
    rows,
    send,
    recv,
):
    i = pl.program_id(0)
    copies, peers = project_copies(seq_count, hidden, halo, send, recv)
    barrier = pltpu.get_barrier_semaphore()

    @pl.when(i == 0)
    def _():
        for where in peers:
            pl.semaphore_signal(barrier, inc=1, device_id=where, device_id_type=MESH)
        narrow = tw_ref[...].astype(f32)
        turned[...] = jnp.concatenate([narrow, narrow], axis=0).astype(bf16)

    @pl.when(i == 1)
    def _():
        pl.semaphore_wait(barrier, len(peers))
        for copy in copies:
            copy.start()

    inner = vw_ref.shape[1]
    gain = gain_ref[...].reshape(1, -1)
    deep = min(256, h_ref.shape[0])
    for first in range(0, h_ref.shape[0], deep):
        for r in range(first, first + deep, 32):
            n = normalized(h_ref[r : r + 32, :], gain)
            rows[r : r + 32, :] = n
            norm_ref[r // CHUNK, 0, r % CHUNK : r % CHUNK + 32, :] = n
        at = slice(first, first + deep)
        n = rows[at, :]
        mix_ref[at, :inner] = mm(n, vw_ref[...]).astype(bf16)
        mix_ref[at, inner:] = mm(n, sw_ref[...]).astype(bf16)
        raw = mm(turned[...], n, NT)
        for q in range(deep // CHUNK):
            raw_ref[first // CHUNK + q] = raw[:, q * CHUNK : (q + 1) * CHUNK]

    @pl.when(i == pl.num_programs(0) - 1)
    def _():
        for copy in copies:
            copy.wait()


def project(mesh_shape, hidden, gain, vw, sw, tw):
    tokens, width = hidden.shape
    inner = vw.shape[1]
    mixed = inner + sw.shape[1]
    rows = tokens // mesh_shape[1]
    rounds = rows // CHUNK
    return pl.pallas_call(
        functools.partial(project_kernel, mesh_shape[0]),
        grid=(tokens // rows,),
        in_specs=[
            pl.BlockSpec((rows, width), lambda i: (i, 0)),
            whole(gain.shape),
            whole(vw.shape),
            whole(sw.shape),
            whole(tw.shape),
            ANY_SPEC,
        ],
        out_specs=[
            pl.BlockSpec((rounds, 1, CHUNK, width), lambda i: (0, i, 0, 0)),
            pl.BlockSpec((rows, mixed), lambda i: (i, 0)),
            pl.BlockSpec((rows // CHUNK, 8, CHUNK), lambda i: (i, 0, 0)),
            ANY_SPEC,
        ],
        out_shape=[
            jax.ShapeDtypeStruct((rounds, tokens // rows, CHUNK, width), bf16),
            jax.ShapeDtypeStruct((tokens, mixed), bf16),
            jax.ShapeDtypeStruct((tokens // CHUNK, 8, CHUNK), f32),
            jax.ShapeDtypeStruct((2 * HALO, width), bf16),
        ],
        scratch_shapes=[
            pltpu.VMEM((8, width), bf16),
            pltpu.VMEM((rows, width), bf16),
            pltpu.SemaphoreType.DMA((2,)),
            pltpu.SemaphoreType.DMA((2,)),
        ],
        compiler_params=params(collective_id=2, has_side_effects=True),
        name="project",
    )(hidden, gain, vw, sw, tw, hidden)


def head_lanes(columns):
    low = lax.broadcasted_iota(jnp.int32, (columns[0].shape[0], 2 * HEAD_DIM), 1) < HEAD_DIM
    pairs = [
        jnp.where(low, columns[2 * p], columns[2 * p + 1]) for p in range(len(columns) // 2)
    ]
    return jnp.concatenate(pairs, axis=1)


def decays(first_row, raw, lens_ref, bias_ref, rate_ref):
    chunks = raw.shape[0]
    shape = (chunks, 8, CHUNK)
    sub = lax.broadcasted_iota(jnp.int32, shape, 1)
    upper = sub < 4
    head = jnp.where(upper, sub, sub - 4)
    pos = (
        first_row
        + lax.broadcasted_iota(jnp.int32, shape, 0) * CHUNK
        + lax.broadcasted_iota(jnp.int32, shape, 2)
    )
    start = jnp.zeros(shape, jnp.int32)
    stop = jnp.full(shape, 1 << 30, jnp.int32)
    edge = jnp.int32(0)
    for k in range(PIECES):
        start = jnp.where(pos >= edge, edge, start)
        edge = edge + lens_ref[k]
        stop = jnp.minimum(stop, jnp.where(edge > pos, edge, 1 << 30))
    since = pos - start
    until = stop - 1 - pos
    bias = jnp.zeros(shape, f32)
    rate = jnp.zeros(shape, f32)
    for h in range(4):
        bias = jnp.where(head == h, bias_ref[h], bias)
        rate = jnp.where(head == h, rate_ref[h], rate)
    rate = jnp.exp(rate) * (-LOG2E)
    z = raw + bias
    step = jnp.maximum(z, 0.0) + jnp.log1p(jnp.exp(-jnp.abs(z)))
    log = step * rate
    reset = jnp.where(since == 0, -RESET, 0.0)
    ones = (
        lax.broadcasted_iota(jnp.int32, (CHUNK, CHUNK), 0)
        <= lax.broadcasted_iota(jnp.int32, (CHUNK, CHUNK), 1)
    ).astype(f32)
    cum = mm(
        (log + reset).reshape(chunks * 8, CHUNK), ones, precision=lax.Precision.HIGHEST
    ).reshape(shape)
    excl = cum - log
    total = cum[:, :, CHUNK - 1 :]
    log_step = jnp.where(step > 0.0, jnp.log2(step), -RESET)
    row = jnp.where(upper, cum - log_step, excl + log_step)
    g1 = jnp.where(upper, cum, excl)
    g2 = jnp.where(upper, jnp.exp2(cum), jnp.exp2(total - cum) * step)
    g3 = jnp.where(upper, jnp.exp2(total - excl), jnp.exp2(excl) * step)
    g4 = jnp.where(upper, since, until).astype(f32)
    return row, g1, g2, g3, g4


def states_kernel(
    axis,
    mix_ref,
    before_ref,
    after_ref,
    halo_ref,
    gain_ref,
    vw_ref,
    sw_ref,
    raw_ref,
    lens_ref,
    bias_ref,
    rate_ref,
    cv_ref,
    cs_ref,
    conv_ref,
    fresh_ref,
    cols_ref,
    row_ref,
    end_ref,
    total_ref,
    prod,
    halo,
    run,
    reach,
    spread,
    near,
):
    g = pl.program_id(0)
    groups = pl.num_programs(0)
    inner = vw_ref.shape[1]
    rows, mixed = mix_ref.shape
    rounds = rows // CHUNK
    blocks = mixed // 128
    first_row = lax.axis_index(axis) * (groups * rows)

    @pl.when(g == 0)
    def _():
        n = normalized(halo_ref[...], gain_ref[...].reshape(1, -1))
        halo[:, :inner] = mm(n, vw_ref[...]).astype(bf16).astype(f32)
        halo[:, inner:] = mm(n, sw_ref[...]).astype(bf16).astype(f32)
        row, g1, g2, g3, g4 = decays(first_row, raw_ref[...], lens_ref, bias_ref, rate_ref)
        row_ref[...] = row
        cols_ref[:, 0:8, :] = g1
        cols_ref[:, 8:16, :] = g2
        cols_ref[:, 16:24, :] = g3
        cols_ref[:, 24:32, :] = g4
        run[...] = jnp.zeros_like(run)
        reach[...] = jnp.zeros_like(reach)
        line = lax.broadcasted_iota(jnp.int32, spread.shape, 0) % 32
        lane = lax.broadcasted_iota(jnp.int32, spread.shape, 1)
        wanted = 12 + (lane // inner) * 8 + (lane % inner) // HEAD_DIM
        spread[...] = (line == wanted).astype(f32).astype(bf16)

        def clear(k, carry):
            near[k] = 0
            return carry

        lax.fori_loop(0, near.shape[0], clear, 0)

        def mark(k, edge):
            for shift in (-(CONV - 1), CONV - 2):
                at = (edge + shift - first_row + rows) // rows
                near[jnp.clip(at, 0, near.shape[0] - 1)] = 1
            return edge + lens_ref[jnp.minimum(k, PIECES - 1)]

        lax.fori_loop(0, PIECES + 1, mark, jnp.int32(0))

    taps = jnp.concatenate([cv_ref[...], cs_ref[...]], axis=1).astype(f32) * 0.5

    def put(b, at, values):
        lanes = slice(b * 128, (b + 1) * 128)
        for k in range(CONV - 1):
            prod[k, b, at : at + values.shape[0], :] = values * taps[k : k + 1, lanes]

    def ready(q):
        for b in range(blocks):
            lanes = slice(b * 128, (b + 1) * 128)
            put(b, REACH + q * CHUNK, mix_ref[q * CHUNK : (q + 1) * CHUNK, lanes].astype(f32))

    def group(masked):
        for b in range(blocks):
            lanes = slice(b * 128, (b + 1) * 128)
            ahead = before_ref[:, lanes].astype(f32)[16 - REACH :, :]
            put(b, 0, jnp.where(g == 0, halo[HALO - REACH : HALO, lanes], ahead))
            behind = after_ref[:, lanes].astype(f32)[:REACH, :]
            put(b, REACH + rows, jnp.where(g == groups - 1, halo[HALO : HALO + REACH, lanes], behind))
        ready(0)
        for q in range(rounds):
            if q + 1 < rounds:
                ready(q + 1)
            chunk(q, masked)

    def chunk(q, masked):
        cols = cols_ref[g * rounds + q]
        high = cols.astype(bf16).astype(f32)
        both = jnp.concatenate([high, cols - high], axis=0).astype(bf16)
        tails = mm(both, spread[...], TN)
        passing = head_lanes([cols[h : h + 1, CHUNK - 1 :] for h in range(4)])
        if masked:
            turned = jnp.concatenate([cols, jnp.zeros((CHUNK - 32, CHUNK), f32)], axis=0).T
            sides = [jnp.broadcast_to(turned[:, r : r + 1], (CHUNK, 128)) for r in (24, 28)]
        write = [None, None]
        for b in [inner // 128] + list(range(inner // 128)) + list(range(inner // 128 + 1, blocks)):
            lanes = slice(b * 128, (b + 1) * 128)
            centre = mix_ref[q * CHUNK : (q + 1) * CHUNK, lanes].astype(f32) * taps[CONV - 1 : CONV, lanes]
            for d in range(2):
                half = centre
                for distance in range(1, CONV):
                    at = REACH + q * CHUNK + (distance if d else -distance)
                    term = prod[CONV - 1 - distance, b, at : at + CHUNK, :]
                    if masked:
                        term = jnp.where(sides[d] >= distance, term, 0.0)
                    half = half + term
                value = half * jnp.tanh(half) + half
                at = d * mixed + b * 128
                narrow = value.astype(bf16)
                conv_ref[q, 0, :, at : at + 128] = narrow
                if b == inner // 128:
                    write[d] = narrow
                elif b < inner // 128:
                    at = d * inner + b * 128
                    scaled = (value * tails[:, at : at + 128]).astype(bf16)
                    fresh = mm(write[d], scaled, TN)
                    fresh_ref[q, d, :, lanes] = fresh.astype(bf16)
                    if d == 0:
                        run[0, :, lanes] = run[0, :, lanes] * jnp.exp2(passing[:, lanes]) + fresh
                    else:
                        run[1, :, lanes] = run[1, :, lanes] + jnp.exp2(reach[0:1, lanes]) * fresh
        reach[...] = reach[...] + passing

    edges = near[g + 1]

    @pl.when(edges == 0)
    def _():
        group(False)

    @pl.when(edges != 0)
    def _():
        group(True)

    @pl.when(g == groups - 1)
    def _():
        end_ref[...] = run[...].astype(bf16)
        total_ref[...] = reach[...]


def states(axis, owners, mix, halo, gain, vw, sw, raw, lens, bias, rate, cv, cs):
    tokens, mixed = mix.shape
    chunks = tokens // CHUNK
    inner = vw.shape[1]
    rounds = chunks // owners
    rows = rounds * CHUNK
    per = rows // 16
    last = tokens // 16 - 1
    return pl.pallas_call(
        functools.partial(states_kernel, axis),
        grid=(owners,),
        in_specs=[
            pl.BlockSpec((rows, mixed), lambda c: (c, 0)),
            pl.BlockSpec((16, mixed), lambda c: (jnp.maximum(c * per - 1, 0), 0)),
            pl.BlockSpec((16, mixed), lambda c: (jnp.minimum(c * per + per, last), 0)),
            whole(halo.shape),
            whole(gain.shape),
            whole(vw.shape),
            whole(sw.shape),
            whole(raw.shape),
            SMEM_SPEC,
            SMEM_SPEC,
            SMEM_SPEC,
            whole(cv.shape),
            whole(cs.shape),
        ],
        out_specs=[
            pl.BlockSpec((rounds, 1, CHUNK, 2 * mixed), lambda c: (0, c, 0, 0)),
            pl.BlockSpec((rounds, 2, STATE, inner), lambda c: (c, 0, 0, 0)),
            whole((chunks, 32, CHUNK)),
            whole((chunks, 8, CHUNK)),
            whole((2, STATE, inner)),
            whole((8, inner)),
        ],
        out_shape=[
            jax.ShapeDtypeStruct((rounds, owners, CHUNK, 2 * mixed), bf16),
            jax.ShapeDtypeStruct((chunks, 2, STATE, inner), bf16),
            jax.ShapeDtypeStruct((chunks, 32, CHUNK), f32),
            jax.ShapeDtypeStruct((chunks, 8, CHUNK), f32),
            jax.ShapeDtypeStruct((2, STATE, inner), bf16),
            jax.ShapeDtypeStruct((8, inner), f32),
        ],
        scratch_shapes=[
            pltpu.VMEM((CONV - 1, mixed // 128, rows + 2 * REACH, 128), f32),
            pltpu.VMEM((2 * HALO, mixed), f32),
            pltpu.VMEM((2, STATE, inner), f32),
            pltpu.VMEM((8, inner), f32),
            pltpu.VMEM((64, 2 * inner), bf16),
            pltpu.SMEM((owners + 2,), jnp.int32),
        ],
        compiler_params=params(),
        name="states",
    )(mix, mix, mix, halo, gain, vw, sw, raw, lens, bias, rate, cv, cs)


def split(x, parts):
    pieces = []
    for _ in range(parts - 1):
        pieces.append(x.astype(bf16).astype(f32))
        x = x - pieces[-1]
    return pieces + [x]


def finish_kernel(
    seq_count,
    head_count,
    end_ref,
    total_ref,
    cols_ref,
    row_ref,
    skip_ref,
    gain_ref,
    gw_ref,
    conv_hbm,
    norm_hbm,
    fresh_hbm,
    hidden_hbm,
    w_hbm,
    out_ref,
    conv,
    normed,
    gate,
    fresh,
    rest,
    weight,
    ends,
    totals,
    incoming,
    entry,
    pick,
    spread,
    inside,
    gated,
    squares,
    others,
    sending,
    arrived,
    load,
    seq_send,
    seq_recv,
    w_send,
    w_recv,
    ss_send,
    ss_recv,
    send,
    recv,
):
    me = lax.axis_index("seq")
    head = lax.axis_index("head")
    chips = head_count // 2
    rounds, owners = conv.shape[0], conv.shape[1]
    chunks = rounds * owners
    inner = gate.shape[3]
    mixed = conv.shape[3] // 2
    rows = rounds * CHUNK
    slots = [(dy, dc) for dy in range(chips) for dc in range(2)]
    peers = [head_peer(head, chips, dy, dc) for dy, dc in slots]
    up, down, partner = peers[2], peers[2 * chips - 2], peers[1]

    def fetch(src, dst, n):
        copy = pltpu.make_async_copy(src, dst, load.at[n])
        copy.start()
        return copy

    def part(k):
        return pl.ds(k * inner, inner)

    conv_in, norm_in = [], []
    for q in range(rounds):
        conv_in.append(fetch(conv_hbm.at[q], conv.at[q], q))
        norm_in.append(fetch(norm_hbm.at[q], normed.at[q], rounds + 7 + q))
    fresh_in = fetch(fresh_hbm, fresh, rounds)
    mine = pl.ds(pl.multiple_of(head * rows, rows), rows)
    half = inner // 2
    side = (2 * chips - 2) * inner
    far = 4 * inner
    top, bottom = pl.ds(0, half), pl.ds(half, half)
    late = [
        fetch(hidden_hbm.at[mine, :], rest, rounds + 2),
        fetch(w_hbm, weight.at[part(0)], rounds + 3),
    ]

    greet(
        [{"seq": (me + k) % seq_count} for k in range(1, seq_count)]
        + [{"head": p} for p in peers[1:]]
    )
    started = []

    def start(copy):
        copy.start()
        started.append(copy)
        return copy

    travelling = []
    for k in range(1, seq_count):
        target = (me + k) % seq_count
        backward = (me + k) // seq_count
        travelling.append(
            start(
                remote(
                    end_ref.at[backward], ends.at[k], seq_send.at[0, k], seq_recv.at[0, k], seq=target
                )
            )
        )
        travelling.append(
            start(remote(total_ref, totals.at[k], seq_send.at[1, k], seq_recv.at[1, k], seq=target))
        )
    def weigh(n, src, row, where, count=half):
        at = weight.at[pl.ds(row, count)]
        return start(remote(src, at, w_send.at[n], w_recv.at[n], head=where))

    u1 = weigh(0, w_hbm.at[top], 2 * inner, up)
    u2 = weigh(1, w_hbm.at[bottom], side + half, down)
    u3 = weigh(2, w_hbm.at[bottom], 2 * inner + half, up)
    u4 = weigh(3, w_hbm.at[top], side, down)
    beside = [weigh(4, w_hbm, inner, partner, inner)]

    def onward():
        u1.wait_recv()
        t1 = weigh(5, weight.at[pl.ds(2 * inner, half)], far, up)
        u2.wait_recv()
        return t1, weigh(6, weight.at[pl.ds(side + half, half)], far + half, down)

    def cross():
        for copy in (u3, u4) + second:
            copy.wait_recv()
        return [
            weigh(7, weight.at[part(2)], 3 * inner, partner, inner),
            weigh(8, weight.at[part(2 * chips - 2)], side + inner, partner, inner),
            weigh(9, weight.at[part(4)], 5 * inner, partner, inner),
        ]

    i = lax.broadcasted_iota(jnp.int32, (CHUNK, CHUNK), 0)
    j = lax.broadcasted_iota(jnp.int32, (CHUNK, CHUNK), 1)
    lower = i >= j
    upper = i <= j
    low = j < HEAD_DIM
    skip = head_lanes([jnp.full((1, 1), skip_ref[h], f32) for h in range(4)])
    sub = lax.broadcasted_iota(jnp.int32, (8, CHUNK), 0)
    line = lax.broadcasted_iota(jnp.int32, pick.shape[1:], 0)
    block = lax.broadcasted_iota(jnp.int32, pick.shape[1:], 1) // CHUNK
    sign = jnp.where(block < 4, 1.0, -1.0)
    chosen = jnp.where((line < 24) & (line % 8 == block), sign, 0.0).astype(bf16)
    for u in range(pick.shape[0]):
        pick[u] = chosen
    line = lax.broadcasted_iota(jnp.int32, spread.shape, 0)
    lane = lax.broadcasted_iota(jnp.int32, spread.shape, 1)
    wanted = (lane // inner) * 8 + (lane % inner) // HEAD_DIM
    spread[...] = (line % 16 == wanted).astype(f32).astype(bf16)

    def within(q, d, u):
        c = d * rounds + q
        row = row_ref[c]
        lines = jnp.concatenate(split(jnp.where(sub < 4, -row, row), 3), axis=0)
        for n in range(8):
            own = lax.broadcasted_iota(jnp.int32, lines.shape, 0) % 8 == n
            pick[u, 32:56, n * CHUNK : (n + 1) * CHUNK] = jnp.where(own, lines, 0.0).astype(bf16)
        left = jnp.concatenate(
            split(cols_ref[c, 0:8, :], 3)
            + [jnp.zeros((8, CHUNK), f32), jnp.ones((24, CHUNK), f32), jnp.zeros((8, CHUNK), f32)],
            axis=0,
        ).astype(bf16)
        made = mm(left, pick[u], TN)
        pair = []
        for e, keep in ((0, lower), (1, upper)):
            base = e * mixed + inner
            write = conv[q, d, :, base : base + STATE]
            read = conv[q, d, :, base + STATE : base + 2 * STATE]
            pair.append(jnp.where(keep, mm(read, write, NT), 0.0))
        for p in range(2):
            weights = ([], [])
            for h in (2 * p, 2 * p + 1):
                table = jnp.exp2(
                    jnp.where(
                        lower,
                        made[:, h * CHUNK : (h + 1) * CHUNK],
                        made[:, (4 + h) * CHUNK : (5 + h) * CHUNK],
                    )
                )
                for e in range(2):
                    weights[e].append((pair[e] * table).astype(bf16))
            for e in range(2):
                at = e * mixed + p * CHUNK
                x = conv[q, d, :, at : at + CHUNK]
                zero = jnp.zeros_like(x)
                stacked = jnp.concatenate([jnp.where(low, x, zero), jnp.where(low, zero, x)], axis=0)
                made_here = mm(jnp.concatenate(weights[e], axis=1), stacked)
                made_here = made_here + skip[:, p * CHUNK : (p + 1) * CHUNK] * x.astype(f32)
                inside[q, d, :, e * inner + p * CHUNK : e * inner + (p + 1) * CHUNK] = made_here

    def gates(q, n):
        two = normed[q, pl.ds(2 * n, 2)].reshape(2 * CHUNK, normed.shape[3])
        two = mm(two, gw_ref[...]).astype(bf16)
        for u in range(2):
            gate[q, 2 * n + u] = two[u * CHUNK : (u + 1) * CHUNK]

    for q in range(rounds):
        conv_in[q].wait()
        norm_in[q].wait()

        def step(n, carry, q=q):
            if q < 2:
                gates(q, n)
            for u in range(2):
                within(q, 2 * n + u, u)
            return carry

        lax.fori_loop(0, owners // 2, step, 0)

    second = onward()

    for copy in travelling:
        copy.wait_recv()
    incoming[...] = jnp.zeros_like(incoming)
    for k in range(seq_count - 1, 0, -1):

        @pl.when(k <= me)
        def _(k=k):
            incoming[0] = incoming[0] * jnp.exp2(totals[k, 0:1, :]) + ends[k].astype(f32)

    for k in range(1, seq_count):

        @pl.when(k > me)
        def _(k=k):
            incoming[1] = incoming[1] * jnp.exp2(totals[k, 0:1, :]) + ends[k].astype(f32)

    fresh_in.wait()

    def passing(c):
        return jnp.exp2(head_lanes([cols_ref[c, h : h + 1, CHUNK - 1 :] for h in range(4)]))

    def walk(n, carry):
        for e in range(2):
            at = [2 * n, 2 * n + 1] if e == 0 else [chunks - 1 - 2 * n, chunks - 2 - 2 * n]
            factors = [passing(c) for c in at]
            for lanes in (slice(0, inner // 2), slice(inner // 2, inner)):
                state = incoming[e, :, lanes]
                for c, factor in zip(at, factors):
                    entry[e, c, :, lanes] = state.astype(bf16)
                    state = state * factor[:, lanes] + fresh[c, e, :, lanes].astype(f32)
                incoming[e, :, lanes] = state
        return carry

    lax.fori_loop(0, chunks // 2, walk, 0)

    ones = jnp.ones((8, inner), bf16)
    gain = gain_ref[...].reshape(1, -1).astype(f32)
    sixteen = lax.broadcasted_iota(jnp.int32, (2 * owners, CHUNK), 0)

    def carried(q, d, sums):
        c = d * rounds + q
        left = jnp.concatenate(split(cols_ref[c, 8:24, :], 2), axis=0).astype(bf16)
        scale = mm(left, spread[...], TN)
        act = silu(gate[q, d].astype(f32))
        for e in range(2):
            at = e * mixed + inner + STATE
            lanes = slice(e * inner, (e + 1) * inner)
            part_in = mm(conv[q, d, :, at : at + STATE], entry[e, c])
            value = (inside[q, d, :, lanes] + part_in * scale[:, lanes]) * act
            gated[q, d, :, lanes] = value.astype(bf16)
            square = mm(ones, (value * value).astype(bf16), NT)
            square = jnp.concatenate([square] * (2 * owners // 8), axis=0)
            sums = jnp.where(sixteen == 2 * d + e, square, sums)
        return sums

    def combine(q):
        for k in range(1, head_count):
            ss[q][k - 1].wait_recv()
        total = squares[q]
        for k in range(1, head_count):
            total = total + others[q, k]
        total = lax.rsqrt(total * (1.0 / (inner * head_count)) + epsilon)
        scale = jnp.concatenate([total, jnp.zeros((CHUNK - 2 * owners, CHUNK), f32)], axis=0).T
        for d in range(owners):
            both = gated[q, d, :, :inner].astype(f32) * scale[:, 2 * d : 2 * d + 1]
            both = both + gated[q, d, :, inner:].astype(f32) * scale[:, 2 * d + 1 : 2 * d + 2]
            sending[q, d] = (both * gain).astype(bf16)
        arrived[q * CHUNK : (q + 1) * CHUNK, 0:inner] = sending[q, head]
        return [
            start(
                remote(
                    sending.at[q, peers[k]],
                    arrived.at[pl.ds(q * CHUNK, CHUNK), part(k)],
                    send.at[q, k],
                    recv.at[q, k],
                    head=peers[k],
                )
            )
            for k in sorted(range(1, head_count), key=lambda k: -min(slots[k][0], chips - slots[k][0]))
        ]

    ss, pieces = [], []
    for q in range(rounds):
        if q >= 2:

            def later(n, carry, q=q):
                gates(q, n)
                return carry

            lax.fori_loop(0, owners // 2, later, 0)

        def some(n, sums, q=q):
            for u in range(4):
                sums = carried(q, 4 * n + u, sums)
            return sums

        squares[q] = lax.fori_loop(0, owners // 4, some, jnp.zeros((2 * owners, CHUNK), f32))
        ss.append(
            [
                start(
                    remote(
                        squares.at[q], others.at[q, k], ss_send.at[q, k], ss_recv.at[q, k], head=peers[k]
                    )
                )
                for k in range(1, head_count)
            ]
        )
        if q:
            pieces.append(combine(q - 1))
        if q == 0:
            beside += cross()
    pieces.append(combine(rounds - 1))

    for copy in late:
        copy.wait()
    for copy in beside:
        copy.wait_recv()
    width = out_ref.shape[1]
    step_lanes = 256
    early = (rounds - 1) * CHUNK
    for first, count, done in ((0, early, pieces[:-1]), (early, CHUNK, pieces[-1:])):
        for batch in done:
            for copy in batch:
                copy.wait_recv()
        if count:

            def project_out(b, carry, first=first, count=count):
                lanes = pl.ds(pl.multiple_of(b * step_lanes, step_lanes), step_lanes)
                here = pl.ds(first, count)
                out_ref[here, lanes] = (
                    mm(arrived[here, :], weight[:, lanes]) + rest[here, lanes].astype(f32)
                ).astype(bf16)
                return carry

            lax.fori_loop(0, width // step_lanes, project_out, 0)
    for copy in started:
        copy.wait_send()


def finish(mesh_shape, end, total, cols, row, skip, gain, gw, conv, normed, fresh, hidden, w):
    seq_count, head_count = mesh_shape
    rounds, owners = conv.shape[:2]
    rows = rounds * CHUNK
    inner = gw.shape[1]
    width = hidden.shape[1]
    dma = pltpu.SemaphoreType.DMA
    return pl.pallas_call(
        functools.partial(finish_kernel, seq_count, head_count),
        in_specs=[
            whole(end.shape),
            whole(total.shape),
            whole(cols.shape),
            whole(row.shape),
            SMEM_SPEC,
            whole(gain.shape),
            whole(gw.shape),
        ]
        + [ANY_SPEC] * 5,
        out_specs=whole((rows, width)),
        out_shape=jax.ShapeDtypeStruct((rows, width), bf16),
        scratch_shapes=[
            pltpu.VMEM(conv.shape, bf16),
            pltpu.VMEM(normed.shape, bf16),
            pltpu.VMEM((rounds, owners, CHUNK, inner), bf16),
            pltpu.VMEM(fresh.shape, bf16),
            pltpu.VMEM((rows, width), bf16),
            pltpu.VMEM((head_count * inner, width), bf16),
            pltpu.VMEM((seq_count,) + end.shape[1:], bf16),
            pltpu.VMEM((seq_count,) + total.shape, f32),
            pltpu.VMEM(end.shape, f32),
            pltpu.VMEM((2, rounds * owners) + end.shape[1:], bf16),
            pltpu.VMEM((2, 64, 8 * CHUNK), bf16),
            pltpu.VMEM((32, 2 * inner), bf16),
            pltpu.VMEM((rounds, owners, CHUNK, 2 * inner), f32),
            pltpu.VMEM((rounds, owners, CHUNK, 2 * inner), bf16),
            pltpu.VMEM((rounds, 2 * owners, CHUNK), f32),
            pltpu.VMEM((rounds, head_count, 2 * owners, CHUNK), f32),
            pltpu.VMEM((rounds, head_count, CHUNK, inner), bf16),
            pltpu.VMEM((rows, head_count * inner), bf16),
            dma((2 * rounds + 7,)),
            dma((2, seq_count)),
            dma((2, seq_count)),
            dma((10,)),
            dma((10,)),
            dma((rounds, head_count)),
            dma((rounds, head_count)),
            dma((rounds, head_count)),
            dma((rounds, head_count)),
        ],
        compiler_params=params(collective_id=1, has_side_effects=True),
        name="finish",
    )(end, total, cols, row, skip, gain, gw, conv, normed, fresh, hidden, w)


def local(
    hidden_in,
    norm_gain,
    gate_weight,
    value_weight,
    state_weight,
    step_weight,
    step_bias,
    decay_log,
    skip_gain,
    conv_value,
    conv_state,
    output_gain,
    output_weight,
    piece_lengths,
):
    seq_count, head_count = lax.axis_size("seq"), lax.axis_size("head")
    shape = (seq_count, head_count)
    normed, mix, raw, halo = project(
        shape, hidden_in, norm_gain, value_weight, state_weight, step_weight.T
    )
    conv, fresh, cols, row, end, total = states(
        "seq",
        head_count,
        mix,
        halo,
        norm_gain,
        value_weight,
        state_weight,
        raw,
        piece_lengths,
        step_bias,
        decay_log,
        conv_value,
        conv_state,
    )
    return finish(
        shape,
        end,
        total,
        cols,
        row,
        skip_gain,
        output_gain,
        gate_weight,
        conv,
        normed,
        fresh,
        hidden_in,
        output_weight,
    )


def solution(mesh):
    in_specs = (
        P("seq", None),
        P(),
        P(None, "head"),
        P(None, "head"),
        P(),
        P(None, "head"),
        P("head"),
        P("head"),
        P("head"),
        P(None, "head"),
        P(),
        P("head"),
        P("head", None),
        P(),
    )
    out_specs = P(("seq", "head"), None)
    return jax.shard_map(local, mesh=mesh, in_specs=in_specs, out_specs=out_specs, check_vma=False)
```

```python
import functools
import math

import jax
import jax.numpy as jnp
from jax import lax
from jax.experimental import pallas as pl
from jax.experimental.pallas import tpu as pltpu
from jax.sharding import PartitionSpec as P

HEAD_DIM = 64
STATE = 128
CONV = 4
CHUNK = 128
PIECES = 16
HALO = 16
REACH = 8
RESET = 256.0
LOG2E = math.log2(math.e)

f32 = jnp.float32
bf16 = jnp.bfloat16
epsilon = 1e-05
MESH = pl.DeviceIdType.MESH
NN = (((1,), (0,)), ((), ()))
NT = (((1,), (1,)), ((), ()))
TN = (((0,), (0,)), ((), ()))


def mm(a, b, dims=NN, precision=None):
    return lax.dot_general(a, b, dims, precision=precision, preferred_element_type=f32)


def silu(x):
    half = 0.5 * x
    return half * jnp.tanh(half) + half


def normalized(h, gain):
    wide = h.astype(f32)
    scale = lax.rsqrt(jnp.mean(wide * wide, axis=1, keepdims=True) + epsilon)
    return (wide * scale * gain.astype(f32)).astype(bf16)


def whole(shape):
    zeros = (0,) * len(shape)
    return pl.BlockSpec(shape, lambda *_: zeros)


SMEM_SPEC = pl.BlockSpec(memory_space=pltpu.SMEM)
ANY_SPEC = pl.BlockSpec(memory_space=pl.ANY)


def params(**kw):
    return pltpu.CompilerParams(vmem_limit_bytes=60 * 1024 * 1024, **kw)


def remote(src, dst, send, recv, **where):
    return pltpu.make_async_remote_copy(
        src_ref=src,
        dst_ref=dst,
        send_sem=send,
        recv_sem=recv,
        device_id=where,
        device_id_type=MESH,
    )


def greet(axes_and_peers):
    barrier = pltpu.get_barrier_semaphore()
    for where in axes_and_peers:
        pl.semaphore_signal(barrier, inc=1, device_id=where, device_id_type=MESH)
    pl.semaphore_wait(barrier, len(axes_and_peers))


def head_peer(me, chips, dy, dc):
    y, core = me // 2, me % 2
    return ((y + dy) % chips) * 2 + (core + dc) % 2


def project_copies(seq_count, head_count, hidden, w, halo, hop, send, recv):
    me = lax.axis_index("seq")
    head = lax.axis_index("head")
    chips = head_count // 2
    tokens = hidden.shape[0]
    after = (me + 1) % seq_count
    before = (me + seq_count - 1) % seq_count
    first, last = pl.ds(0, HALO), pl.ds(tokens - HALO, HALO)
    low, high = pl.ds(0, HALO), pl.ds(HALO, HALO)
    half = w.shape[0] // 2
    top, bottom = pl.ds(0, half), pl.ds(half, half)
    up = head_peer(head, chips, 1, 0)
    down = head_peer(head, chips, chips - 1, 0)
    partner = head_peer(head, chips, 0, 1)
    return (
        remote(hidden.at[last], halo.at[low], send.at[0], recv.at[0], seq=after),
        remote(hidden.at[first], halo.at[high], send.at[1], recv.at[1], seq=before),
        remote(w.at[top], hop.at[0, top], send.at[2], recv.at[2], head=up),
        remote(w.at[bottom], hop.at[1, bottom], send.at[3], recv.at[3], head=down),
        remote(w, hop.at[2], send.at[4], recv.at[4], head=partner),
    ), [{"seq": after}, {"seq": before}, {"head": up}, {"head": down}, {"head": partner}]


def project_kernel(
    mesh_shape,
    h_ref,
    gain_ref,
    vw_ref,
    sw_ref,
    tw_ref,
    hidden,
    w,
    mix_ref,
    raw_ref,
    halo,
    hop,
    turned,
    rows,
    send,
    recv,
):
    i = pl.program_id(0)
    copies, peers = project_copies(*mesh_shape, hidden, w, halo, hop, send, recv)
    barrier = pltpu.get_barrier_semaphore()

    @pl.when(i == 0)
    def _():
        for where in peers:
            pl.semaphore_signal(barrier, inc=1, device_id=where, device_id_type=MESH)
        narrow = tw_ref[...].astype(f32)
        turned[...] = jnp.concatenate([narrow, narrow], axis=0).astype(bf16)

    @pl.when(i == 1)
    def _():
        pl.semaphore_wait(barrier, len(peers))
        for copy in copies:
            copy.start()

    inner = vw_ref.shape[1]
    gain = gain_ref[...].reshape(1, -1)
    deep = min(256, h_ref.shape[0])
    for first in range(0, h_ref.shape[0], deep):
        for r in range(first, first + deep, 32):
            rows[r : r + 32, :] = normalized(h_ref[r : r + 32, :], gain)
        at = slice(first, first + deep)
        n = rows[at, :]
        mix_ref[at, :inner] = mm(n, vw_ref[...]).astype(bf16)
        mix_ref[at, inner:] = mm(n, sw_ref[...]).astype(bf16)
        raw = mm(turned[...], n, NT)
        for q in range(deep // CHUNK):
            raw_ref[first // CHUNK + q] = raw[:, q * CHUNK : (q + 1) * CHUNK]

    @pl.when(i == pl.num_programs(0) - 1)
    def _():
        for copy in copies:
            copy.wait()


def project(mesh_shape, hidden, gain, vw, sw, tw, w):
    tokens, width = hidden.shape
    inner = vw.shape[1]
    mixed = inner + sw.shape[1]
    rows = tokens // mesh_shape[1]
    return pl.pallas_call(
        functools.partial(project_kernel, mesh_shape),
        grid=(tokens // rows,),
        in_specs=[
            pl.BlockSpec((rows, width), lambda i: (i, 0)),
            whole(gain.shape),
            whole(vw.shape),
            whole(sw.shape),
            whole(tw.shape),
            ANY_SPEC,
            ANY_SPEC,
        ],
        out_specs=[
            pl.BlockSpec((rows, mixed), lambda i: (i, 0)),
            pl.BlockSpec((rows // CHUNK, 8, CHUNK), lambda i: (i, 0, 0)),
            ANY_SPEC,
            ANY_SPEC,
        ],
        out_shape=[
            jax.ShapeDtypeStruct((tokens, mixed), bf16),
            jax.ShapeDtypeStruct((tokens // CHUNK, 8, CHUNK), f32),
            jax.ShapeDtypeStruct((2 * HALO, width), bf16),
            jax.ShapeDtypeStruct((3,) + w.shape, bf16),
        ],
        scratch_shapes=[
            pltpu.VMEM((8, width), bf16),
            pltpu.VMEM((rows, width), bf16),
            pltpu.SemaphoreType.DMA((5,)),
            pltpu.SemaphoreType.DMA((5,)),
        ],
        compiler_params=params(collective_id=2, has_side_effects=True),
        name="project",
    )(hidden, gain, vw, sw, tw, hidden, w)


def head_lanes(columns):
    low = lax.broadcasted_iota(jnp.int32, (columns[0].shape[0], 2 * HEAD_DIM), 1) < HEAD_DIM
    pairs = [
        jnp.where(low, columns[2 * p], columns[2 * p + 1]) for p in range(len(columns) // 2)
    ]
    return jnp.concatenate(pairs, axis=1)


def decays(first_row, raw, lens_ref, bias_ref, rate_ref):
    chunks = raw.shape[0]
    shape = (chunks, 8, CHUNK)
    sub = lax.broadcasted_iota(jnp.int32, shape, 1)
    upper = sub < 4
    head = jnp.where(upper, sub, sub - 4)
    pos = (
        first_row
        + lax.broadcasted_iota(jnp.int32, shape, 0) * CHUNK
        + lax.broadcasted_iota(jnp.int32, shape, 2)
    )
    start = jnp.zeros(shape, jnp.int32)
    stop = jnp.full(shape, 1 << 30, jnp.int32)
    edge = jnp.int32(0)
    for k in range(PIECES):
        start = jnp.where(pos >= edge, edge, start)
        edge = edge + lens_ref[k]
        stop = jnp.minimum(stop, jnp.where(edge > pos, edge, 1 << 30))
    since = pos - start
    until = stop - 1 - pos
    bias = jnp.zeros(shape, f32)
    rate = jnp.zeros(shape, f32)
    for h in range(4):
        bias = jnp.where(head == h, bias_ref[h], bias)
        rate = jnp.where(head == h, rate_ref[h], rate)
    rate = jnp.exp(rate) * (-LOG2E)
    z = raw + bias
    step = jnp.maximum(z, 0.0) + jnp.log1p(jnp.exp(-jnp.abs(z)))
    log = step * rate
    reset = jnp.where(since == 0, -RESET, 0.0)
    ones = (
        lax.broadcasted_iota(jnp.int32, (CHUNK, CHUNK), 0)
        <= lax.broadcasted_iota(jnp.int32, (CHUNK, CHUNK), 1)
    ).astype(f32)
    cum = mm(
        (log + reset).reshape(chunks * 8, CHUNK), ones, precision=lax.Precision.HIGHEST
    ).reshape(shape)
    excl = cum - log
    total = cum[:, :, CHUNK - 1 :]
    log_step = jnp.where(step > 0.0, jnp.log2(step), -RESET)
    row = jnp.where(upper, cum - log_step, excl + log_step)
    g1 = jnp.where(upper, cum, excl)
    g2 = jnp.where(upper, jnp.exp2(cum), jnp.exp2(total - cum) * step)
    g3 = jnp.where(upper, jnp.exp2(total - excl), jnp.exp2(excl) * step)
    g4 = jnp.where(upper, since, until).astype(f32)
    return row, g1, g2, g3, g4


def states_kernel(
    axis,
    mix_ref,
    before_ref,
    after_ref,
    halo_ref,
    gain_ref,
    vw_ref,
    sw_ref,
    raw_ref,
    lens_ref,
    bias_ref,
    rate_ref,
    cv_ref,
    cs_ref,
    conv_ref,
    fresh_ref,
    cols_ref,
    row_ref,
    end_ref,
    total_ref,
    prod,
    halo,
    run,
    reach,
    spread,
    near,
):
    g = pl.program_id(0)
    groups = pl.num_programs(0)
    inner = vw_ref.shape[1]
    rows, mixed = mix_ref.shape
    rounds = rows // CHUNK
    blocks = mixed // 128
    first_row = lax.axis_index(axis) * (groups * rows)

    @pl.when(g == 0)
    def _():
        n = normalized(halo_ref[...], gain_ref[...].reshape(1, -1))
        halo[:, :inner] = mm(n, vw_ref[...]).astype(bf16).astype(f32)
        halo[:, inner:] = mm(n, sw_ref[...]).astype(bf16).astype(f32)
        row, g1, g2, g3, g4 = decays(first_row, raw_ref[...], lens_ref, bias_ref, rate_ref)
        row_ref[...] = row
        cols_ref[:, 0:8, :] = g1
        cols_ref[:, 8:16, :] = g2
        cols_ref[:, 16:24, :] = g3
        cols_ref[:, 24:32, :] = g4
        run[...] = jnp.zeros_like(run)
        reach[...] = jnp.zeros_like(reach)
        line = lax.broadcasted_iota(jnp.int32, spread.shape, 0) % 32
        lane = lax.broadcasted_iota(jnp.int32, spread.shape, 1)
        wanted = 12 + (lane // inner) * 8 + (lane % inner) // HEAD_DIM
        spread[...] = (line == wanted).astype(f32).astype(bf16)

        def clear(k, carry):
            near[k] = 0
            return carry

        lax.fori_loop(0, near.shape[0], clear, 0)

        def mark(k, edge):
            for shift in (-(CONV - 1), CONV - 2):
                at = (edge + shift - first_row + rows) // rows
                near[jnp.clip(at, 0, near.shape[0] - 1)] = 1
            return edge + lens_ref[jnp.minimum(k, PIECES - 1)]

        lax.fori_loop(0, PIECES + 1, mark, jnp.int32(0))

    taps = jnp.concatenate([cv_ref[...], cs_ref[...]], axis=1).astype(f32) * 0.5

    def put(b, at, values):
        lanes = slice(b * 128, (b + 1) * 128)
        for k in range(CONV - 1):
            prod[k, b, at : at + values.shape[0], :] = values * taps[k : k + 1, lanes]

    def ready(q):
        for b in range(blocks):
            lanes = slice(b * 128, (b + 1) * 128)
            put(b, REACH + q * CHUNK, mix_ref[q * CHUNK : (q + 1) * CHUNK, lanes].astype(f32))

    def group(masked):
        for b in range(blocks):
            lanes = slice(b * 128, (b + 1) * 128)
            ahead = before_ref[:, lanes].astype(f32)[16 - REACH :, :]
            put(b, 0, jnp.where(g == 0, halo[HALO - REACH : HALO, lanes], ahead))
            behind = after_ref[:, lanes].astype(f32)[:REACH, :]
            put(b, REACH + rows, jnp.where(g == groups - 1, halo[HALO : HALO + REACH, lanes], behind))
        ready(0)
        for q in range(rounds):
            if q + 1 < rounds:
                ready(q + 1)
            chunk(q, masked)

    def chunk(q, masked):
        cols = cols_ref[g * rounds + q]
        high = cols.astype(bf16).astype(f32)
        both = jnp.concatenate([high, cols - high], axis=0).astype(bf16)
        tails = mm(both, spread[...], TN)
        passing = head_lanes([cols[h : h + 1, CHUNK - 1 :] for h in range(4)])
        if masked:
            turned = jnp.concatenate([cols, jnp.zeros((CHUNK - 32, CHUNK), f32)], axis=0).T
            sides = [jnp.broadcast_to(turned[:, r : r + 1], (CHUNK, 128)) for r in (24, 28)]
        write = [None, None]
        for b in [inner // 128] + list(range(inner // 128)) + list(range(inner // 128 + 1, blocks)):
            lanes = slice(b * 128, (b + 1) * 128)
            centre = mix_ref[q * CHUNK : (q + 1) * CHUNK, lanes].astype(f32) * taps[CONV - 1 : CONV, lanes]
            for d in range(2):
                half = centre
                for distance in range(1, CONV):
                    at = REACH + q * CHUNK + (distance if d else -distance)
                    term = prod[CONV - 1 - distance, b, at : at + CHUNK, :]
                    if masked:
                        term = jnp.where(sides[d] >= distance, term, 0.0)
                    half = half + term
                value = half * jnp.tanh(half) + half
                at = d * mixed + b * 128
                narrow = value.astype(bf16)
                conv_ref[q, 0, :, at : at + 128] = narrow
                if b == inner // 128:
                    write[d] = narrow
                elif b < inner // 128:
                    at = d * inner + b * 128
                    scaled = (value * tails[:, at : at + 128]).astype(bf16)
                    fresh = mm(write[d], scaled, TN)
                    fresh_ref[q, d, :, lanes] = fresh.astype(bf16)
                    if d == 0:
                        run[0, :, lanes] = run[0, :, lanes] * jnp.exp2(passing[:, lanes]) + fresh
                    else:
                        run[1, :, lanes] = run[1, :, lanes] + jnp.exp2(reach[0:1, lanes]) * fresh
        reach[...] = reach[...] + passing

    edges = near[g + 1]

    @pl.when(edges == 0)
    def _():
        group(False)

    @pl.when(edges != 0)
    def _():
        group(True)

    @pl.when(g == groups - 1)
    def _():
        end_ref[...] = run[...].astype(bf16)
        total_ref[...] = reach[...]


def states(axis, owners, mix, halo, gain, vw, sw, raw, lens, bias, rate, cv, cs):
    tokens, mixed = mix.shape
    chunks = tokens // CHUNK
    inner = vw.shape[1]
    rounds = chunks // owners
    rows = rounds * CHUNK
    per = rows // 16
    last = tokens // 16 - 1
    return pl.pallas_call(
        functools.partial(states_kernel, axis),
        grid=(owners,),
        in_specs=[
            pl.BlockSpec((rows, mixed), lambda c: (c, 0)),
            pl.BlockSpec((16, mixed), lambda c: (jnp.maximum(c * per - 1, 0), 0)),
            pl.BlockSpec((16, mixed), lambda c: (jnp.minimum(c * per + per, last), 0)),
            whole(halo.shape),
            whole(gain.shape),
            whole(vw.shape),
            whole(sw.shape),
            whole(raw.shape),
            SMEM_SPEC,
            SMEM_SPEC,
            SMEM_SPEC,
            whole(cv.shape),
            whole(cs.shape),
        ],
        out_specs=[
            pl.BlockSpec((rounds, 1, CHUNK, 2 * mixed), lambda c: (0, c, 0, 0)),
            pl.BlockSpec((rounds, 2, STATE, inner), lambda c: (c, 0, 0, 0)),
            whole((chunks, 32, CHUNK)),
            whole((chunks, 8, CHUNK)),
            whole((2, STATE, inner)),
            whole((8, inner)),
        ],
        out_shape=[
            jax.ShapeDtypeStruct((rounds, owners, CHUNK, 2 * mixed), bf16),
            jax.ShapeDtypeStruct((chunks, 2, STATE, inner), bf16),
            jax.ShapeDtypeStruct((chunks, 32, CHUNK), f32),
            jax.ShapeDtypeStruct((chunks, 8, CHUNK), f32),
            jax.ShapeDtypeStruct((2, STATE, inner), bf16),
            jax.ShapeDtypeStruct((8, inner), f32),
        ],
        scratch_shapes=[
            pltpu.VMEM((CONV - 1, mixed // 128, rows + 2 * REACH, 128), f32),
            pltpu.VMEM((2 * HALO, mixed), f32),
            pltpu.VMEM((2, STATE, inner), f32),
            pltpu.VMEM((8, inner), f32),
            pltpu.VMEM((64, 2 * inner), bf16),
            pltpu.SMEM((owners + 2,), jnp.int32),
        ],
        compiler_params=params(),
        name="states",
    )(mix, mix, mix, halo, gain, vw, sw, raw, lens, bias, rate, cv, cs)


def split(x, parts):
    pieces = []
    for _ in range(parts - 1):
        pieces.append(x.astype(bf16).astype(f32))
        x = x - pieces[-1]
    return pieces + [x]


def finish_kernel(
    seq_count,
    head_count,
    end_ref,
    total_ref,
    cols_ref,
    row_ref,
    skip_ref,
    gain_ref,
    gw_ref,
    norm_gain_ref,
    conv_hbm,
    fresh_hbm,
    hidden_hbm,
    w_hbm,
    hop_hbm,
    out_ref,
    conv,
    wide,
    gate,
    fresh,
    rest,
    weight,
    ends,
    totals,
    incoming,
    entry,
    pick,
    spread,
    inside,
    gated,
    squares,
    others,
    sending,
    arrived,
    load,
    seq_send,
    seq_recv,
    w_send,
    w_recv,
    ss_send,
    ss_recv,
    send,
    recv,
):
    me = lax.axis_index("seq")
    head = lax.axis_index("head")
    chips = head_count // 2
    rounds, owners = conv.shape[0], conv.shape[1]
    chunks = rounds * owners
    inner = gate.shape[3]
    mixed = conv.shape[3] // 2
    rows = rounds * CHUNK
    slots = [(dy, dc) for dy in range(chips) for dc in range(2)]
    peers = [head_peer(head, chips, dy, dc) for dy, dc in slots]
    up, down, partner = peers[2], peers[2 * chips - 2], peers[1]

    def fetch(src, dst, n):
        copy = pltpu.make_async_copy(src, dst, load.at[n])
        copy.start()
        return copy

    def part(k):
        return pl.ds(k * inner, inner)

    conv_in, wide_in = [], []
    for q in range(rounds):
        conv_in.append(fetch(conv_hbm.at[q], conv.at[q], q))
        wide_in.append(fetch(hidden_hbm.at[:, q], wide.at[q], rounds + 7 + q))
    fresh_in = fetch(fresh_hbm, fresh, rounds)
    half = inner // 2
    side = (2 * chips - 2) * inner
    far = 4 * inner
    top, bottom = pl.ds(0, half), pl.ds(half, half)
    late = [
        fetch(hidden_hbm.at[head], rest, rounds + 2),
        fetch(w_hbm, weight.at[part(0)], rounds + 3),
        fetch(hop_hbm.at[2], weight.at[part(1)], rounds + 4),
        fetch(hop_hbm.at[0, top], weight.at[pl.ds(2 * inner, half)], rounds + 5),
        fetch(hop_hbm.at[1, bottom], weight.at[pl.ds(side + half, half)], rounds + 6),
    ]

    greet(
        [{"seq": (me + k) % seq_count} for k in range(1, seq_count)]
        + [{"head": p} for p in peers[1:]]
    )
    started = []

    def start(copy):
        copy.start()
        started.append(copy)
        return copy

    travelling = []
    for k in range(1, seq_count):
        target = (me + k) % seq_count
        backward = (me + k) // seq_count
        travelling.append(
            start(
                remote(
                    end_ref.at[backward], ends.at[k], seq_send.at[0, k], seq_recv.at[0, k], seq=target
                )
            )
        )
        travelling.append(
            start(remote(total_ref, totals.at[k], seq_send.at[1, k], seq_recv.at[1, k], seq=target))
        )
    def weigh(n, src, row, where, count=half):
        at = weight.at[pl.ds(row, count)]
        return start(remote(src, at, w_send.at[n], w_recv.at[n], head=where))

    u1 = weigh(0, w_hbm.at[bottom], 2 * inner + half, up)
    u2 = weigh(1, w_hbm.at[top], side, down)
    t1 = weigh(2, hop_hbm.at[0, top], far, up)
    t3 = weigh(3, hop_hbm.at[1, bottom], far + half, down)
    beside = [
        weigh(4, hop_hbm.at[0, top], 3 * inner, partner),
        weigh(5, hop_hbm.at[1, bottom], side + inner + half, partner),
    ]

    def cross():
        for copy in (u1, u2, t1, t3):
            copy.wait_recv()
        return [
            weigh(6, weight.at[pl.ds(2 * inner + half, half)], 3 * inner + half, partner),
            weigh(7, weight.at[pl.ds(side, half)], side + inner, partner),
            weigh(8, weight.at[part(4)], 5 * inner, partner, inner),
        ]

    i = lax.broadcasted_iota(jnp.int32, (CHUNK, CHUNK), 0)
    j = lax.broadcasted_iota(jnp.int32, (CHUNK, CHUNK), 1)
    lower = i >= j
    upper = i <= j
    low = j < HEAD_DIM
    skip = head_lanes([jnp.full((1, 1), skip_ref[h], f32) for h in range(4)])
    sub = lax.broadcasted_iota(jnp.int32, (8, CHUNK), 0)
    line = lax.broadcasted_iota(jnp.int32, pick.shape[1:], 0)
    block = lax.broadcasted_iota(jnp.int32, pick.shape[1:], 1) // CHUNK
    sign = jnp.where(block < 4, 1.0, -1.0)
    chosen = jnp.where((line < 24) & (line % 8 == block), sign, 0.0).astype(bf16)
    for u in range(pick.shape[0]):
        pick[u] = chosen
    line = lax.broadcasted_iota(jnp.int32, spread.shape, 0)
    lane = lax.broadcasted_iota(jnp.int32, spread.shape, 1)
    wanted = (lane // inner) * 8 + (lane % inner) // HEAD_DIM
    spread[...] = (line % 16 == wanted).astype(f32).astype(bf16)

    def within(q, d, u):
        c = d * rounds + q
        row = row_ref[c]
        lines = jnp.concatenate(split(jnp.where(sub < 4, -row, row), 3), axis=0)
        for n in range(8):
            own = lax.broadcasted_iota(jnp.int32, lines.shape, 0) % 8 == n
            pick[u, 32:56, n * CHUNK : (n + 1) * CHUNK] = jnp.where(own, lines, 0.0).astype(bf16)
        left = jnp.concatenate(
            split(cols_ref[c, 0:8, :], 3)
            + [jnp.zeros((8, CHUNK), f32), jnp.ones((24, CHUNK), f32), jnp.zeros((8, CHUNK), f32)],
            axis=0,
        ).astype(bf16)
        made = mm(left, pick[u], TN)
        pair = []
        for e, keep in ((0, lower), (1, upper)):
            base = e * mixed + inner
            write = conv[q, d, :, base : base + STATE]
            read = conv[q, d, :, base + STATE : base + 2 * STATE]
            pair.append(jnp.where(keep, mm(read, write, NT), 0.0))
        for p in range(2):
            weights = ([], [])
            for h in (2 * p, 2 * p + 1):
                table = jnp.exp2(
                    jnp.where(
                        lower,
                        made[:, h * CHUNK : (h + 1) * CHUNK],
                        made[:, (4 + h) * CHUNK : (5 + h) * CHUNK],
                    )
                )
                for e in range(2):
                    weights[e].append((pair[e] * table).astype(bf16))
            for e in range(2):
                at = e * mixed + p * CHUNK
                x = conv[q, d, :, at : at + CHUNK]
                zero = jnp.zeros_like(x)
                stacked = jnp.concatenate([jnp.where(low, x, zero), jnp.where(low, zero, x)], axis=0)
                made_here = mm(jnp.concatenate(weights[e], axis=1), stacked)
                made_here = made_here + skip[:, p * CHUNK : (p + 1) * CHUNK] * x.astype(f32)
                inside[q, d, :, e * inner + p * CHUNK : e * inner + (p + 1) * CHUNK] = made_here

    def gates(q, n):
        two = wide[q, pl.ds(2 * n, 2)].reshape(2 * CHUNK, wide.shape[3])
        two = mm(normalized(two, norm_gain_ref[...].reshape(1, -1)), gw_ref[...]).astype(bf16)
        for u in range(2):
            gate[q, 2 * n + u] = two[u * CHUNK : (u + 1) * CHUNK]

    for q in range(rounds):
        conv_in[q].wait()
        wide_in[q].wait()

        def step(n, carry, q=q):
            if q < 2:
                gates(q, n)
            for u in range(2):
                within(q, 2 * n + u, u)
            return carry

        lax.fori_loop(0, owners // 2, step, 0)

    for copy in travelling:
        copy.wait_recv()
    incoming[...] = jnp.zeros_like(incoming)
    for k in range(seq_count - 1, 0, -1):

        @pl.when(k <= me)
        def _(k=k):
            incoming[0] = incoming[0] * jnp.exp2(totals[k, 0:1, :]) + ends[k].astype(f32)

    for k in range(1, seq_count):

        @pl.when(k > me)
        def _(k=k):
            incoming[1] = incoming[1] * jnp.exp2(totals[k, 0:1, :]) + ends[k].astype(f32)

    fresh_in.wait()

    def passing(c):
        return jnp.exp2(head_lanes([cols_ref[c, h : h + 1, CHUNK - 1 :] for h in range(4)]))

    def walk(n, carry):
        for e in range(2):
            at = [2 * n, 2 * n + 1] if e == 0 else [chunks - 1 - 2 * n, chunks - 2 - 2 * n]
            factors = [passing(c) for c in at]
            for lanes in (slice(0, inner // 2), slice(inner // 2, inner)):
                state = incoming[e, :, lanes]
                for c, factor in zip(at, factors):
                    entry[e, c, :, lanes] = state.astype(bf16)
                    state = state * factor[:, lanes] + fresh[c, e, :, lanes].astype(f32)
                incoming[e, :, lanes] = state
        return carry

    lax.fori_loop(0, chunks // 2, walk, 0)

    ones = jnp.ones((8, inner), bf16)
    gain = gain_ref[...].reshape(1, -1).astype(f32)
    sixteen = lax.broadcasted_iota(jnp.int32, (2 * owners, CHUNK), 0)

    def carried(q, d, sums):
        c = d * rounds + q
        left = jnp.concatenate(split(cols_ref[c, 8:24, :], 2), axis=0).astype(bf16)
        scale = mm(left, spread[...], TN)
        act = silu(gate[q, d].astype(f32))
        for e in range(2):
            at = e * mixed + inner + STATE
            lanes = slice(e * inner, (e + 1) * inner)
            part_in = mm(conv[q, d, :, at : at + STATE], entry[e, c])
            value = (inside[q, d, :, lanes] + part_in * scale[:, lanes]) * act
            gated[q, d, :, lanes] = value.astype(bf16)
            square = mm(ones, (value * value).astype(bf16), NT)
            square = jnp.concatenate([square] * (2 * owners // 8), axis=0)
            sums = jnp.where(sixteen == 2 * d + e, square, sums)
        return sums

    def combine(q):
        for k in range(1, head_count):
            ss[q][k - 1].wait_recv()
        total = squares[q]
        for k in range(1, head_count):
            total = total + others[q, k]
        total = lax.rsqrt(total * (1.0 / (inner * head_count)) + epsilon)
        scale = jnp.concatenate([total, jnp.zeros((CHUNK - 2 * owners, CHUNK), f32)], axis=0).T
        for d in range(owners):
            both = gated[q, d, :, :inner].astype(f32) * scale[:, 2 * d : 2 * d + 1]
            both = both + gated[q, d, :, inner:].astype(f32) * scale[:, 2 * d + 1 : 2 * d + 2]
            sending[q, d] = (both * gain).astype(bf16)
        arrived[q * CHUNK : (q + 1) * CHUNK, 0:inner] = sending[q, head]
        return [
            start(
                remote(
                    sending.at[q, peers[k]],
                    arrived.at[pl.ds(q * CHUNK, CHUNK), part(k)],
                    send.at[q, k],
                    recv.at[q, k],
                    head=peers[k],
                )
            )
            for k in sorted(range(1, head_count), key=lambda k: -min(slots[k][0], chips - slots[k][0]))
        ]

    ss, pieces = [], []
    for q in range(rounds):
        if q >= 2:

            def later(n, carry, q=q):
                gates(q, n)
                return carry

            lax.fori_loop(0, owners // 2, later, 0)

        def some(n, sums, q=q):
            for u in range(4):
                sums = carried(q, 4 * n + u, sums)
            return sums

        squares[q] = lax.fori_loop(0, owners // 4, some, jnp.zeros((2 * owners, CHUNK), f32))
        ss.append(
            [
                start(
                    remote(
                        squares.at[q], others.at[q, k], ss_send.at[q, k], ss_recv.at[q, k], head=peers[k]
                    )
                )
                for k in range(1, head_count)
            ]
        )
        if q:
            pieces.append(combine(q - 1))
        if q == 0:
            beside += cross()
    pieces.append(combine(rounds - 1))

    for copy in late:
        copy.wait()
    for copy in beside:
        copy.wait_recv()
    width = out_ref.shape[1]
    step_lanes = 256
    early = (rounds - 1) * CHUNK
    for first, count, done in ((0, early, pieces[:-1]), (early, CHUNK, pieces[-1:])):
        for batch in done:
            for copy in batch:
                copy.wait_recv()
        if count:

            def project_out(b, carry, first=first, count=count):
                lanes = pl.ds(pl.multiple_of(b * step_lanes, step_lanes), step_lanes)
                here = pl.ds(first, count)
                of = pl.ds(first // CHUNK, count // CHUNK)
                out_ref[here, lanes] = (
                    mm(arrived[here, :], weight[:, lanes]) + rest[of, :, lanes].reshape(count, step_lanes).astype(f32)
                ).astype(bf16)
                return carry

            lax.fori_loop(0, width // step_lanes, project_out, 0)
    for copy in started:
        copy.wait_send()


def finish(mesh_shape, end, total, cols, row, skip, gain, gw, norm_gain, conv, fresh, hidden, w, hop):
    seq_count, head_count = mesh_shape
    rounds, owners = conv.shape[:2]
    rows = rounds * CHUNK
    inner = gw.shape[1]
    width = hidden.shape[3]
    dma = pltpu.SemaphoreType.DMA
    return pl.pallas_call(
        functools.partial(finish_kernel, seq_count, head_count),
        in_specs=[
            whole(end.shape),
            whole(total.shape),
            whole(cols.shape),
            whole(row.shape),
            SMEM_SPEC,
            whole(gain.shape),
            whole(gw.shape),
            whole(norm_gain.shape),
        ]
        + [ANY_SPEC] * 5,
        out_specs=whole((rows, width)),
        out_shape=jax.ShapeDtypeStruct((rows, width), bf16),
        scratch_shapes=[
            pltpu.VMEM(conv.shape, bf16),
            pltpu.VMEM((rounds, owners, CHUNK, width), bf16),
            pltpu.VMEM((rounds, owners, CHUNK, inner), bf16),
            pltpu.VMEM(fresh.shape, bf16),
            pltpu.VMEM((rounds, CHUNK, width), bf16),
            pltpu.VMEM((head_count * inner, width), bf16),
            pltpu.VMEM((seq_count,) + end.shape[1:], bf16),
            pltpu.VMEM((seq_count,) + total.shape, f32),
            pltpu.VMEM(end.shape, f32),
            pltpu.VMEM((2, rounds * owners) + end.shape[1:], bf16),
            pltpu.VMEM((2, 64, 8 * CHUNK), bf16),
            pltpu.VMEM((32, 2 * inner), bf16),
            pltpu.VMEM((rounds, owners, CHUNK, 2 * inner), f32),
            pltpu.VMEM((rounds, owners, CHUNK, 2 * inner), bf16),
            pltpu.VMEM((rounds, 2 * owners, CHUNK), f32),
            pltpu.VMEM((rounds, head_count, 2 * owners, CHUNK), f32),
            pltpu.VMEM((rounds, head_count, CHUNK, inner), bf16),
            pltpu.VMEM((rows, head_count * inner), bf16),
            dma((2 * rounds + 7,)),
            dma((2, seq_count)),
            dma((2, seq_count)),
            dma((9,)),
            dma((9,)),
            dma((rounds, head_count)),
            dma((rounds, head_count)),
            dma((rounds, head_count)),
            dma((rounds, head_count)),
        ],
        compiler_params=params(collective_id=1, has_side_effects=True),
        name="finish",
    )(end, total, cols, row, skip, gain, gw, norm_gain, conv, fresh, hidden, w, hop)


def local(
    hidden_in,
    norm_gain,
    gate_weight,
    value_weight,
    state_weight,
    step_weight,
    step_bias,
    decay_log,
    skip_gain,
    conv_value,
    conv_state,
    output_gain,
    output_weight,
    piece_lengths,
):
    seq_count, head_count = lax.axis_size("seq"), lax.axis_size("head")
    shape = (seq_count, head_count)
    mix, raw, halo, hop = project(
        shape, hidden_in, norm_gain, value_weight, state_weight, step_weight.T, output_weight
    )
    conv, fresh, cols, row, end, total = states(
        "seq",
        head_count,
        mix,
        halo,
        norm_gain,
        value_weight,
        state_weight,
        raw,
        piece_lengths,
        step_bias,
        decay_log,
        conv_value,
        conv_state,
    )
    return finish(
        shape,
        end,
        total,
        cols,
        row,
        skip_gain,
        output_gain,
        gate_weight,
        norm_gain,
        conv,
        fresh,
        hidden_in.reshape(head_count, -1, CHUNK, hidden_in.shape[1]),
        output_weight,
        hop,
    )


def solution(mesh):
    in_specs = (
        P("seq", None),
        P(),
        P(None, "head"),
        P(None, "head"),
        P(),
        P(None, "head"),
        P("head"),
        P("head"),
        P("head"),
        P(None, "head"),
        P(),
        P("head"),
        P("head", None),
        P(),
    )
    out_specs = P(("seq", "head"), None)
    return jax.shard_map(local, mesh=mesh, in_specs=in_specs, out_specs=out_specs, check_vma=False)
```

```python
import functools
import math

import jax
import jax.numpy as jnp
from jax import lax
from jax.experimental import pallas as pl
from jax.experimental.pallas import tpu as pltpu
from jax.sharding import PartitionSpec as P

HEAD_DIM = 64
STATE = 128
CONV = 4
CHUNK = 128
PIECES = 16
HALO = 16
REACH = 8
RESET = 256.0
LOG2E = math.log2(math.e)

f32 = jnp.float32
bf16 = jnp.bfloat16
epsilon = 1e-05
MESH = pl.DeviceIdType.MESH
NN = (((1,), (0,)), ((), ()))
NT = (((1,), (1,)), ((), ()))
TN = (((0,), (0,)), ((), ()))


def mm(a, b, dims=NN, precision=None):
    return lax.dot_general(a, b, dims, precision=precision, preferred_element_type=f32)


def silu(x):
    half = 0.5 * x
    return half * jnp.tanh(half) + half


def normalized(h, gain):
    wide = h.astype(f32)
    scale = lax.rsqrt(jnp.mean(wide * wide, axis=1, keepdims=True) + epsilon)
    return (wide * scale * gain.astype(f32)).astype(bf16)


def whole(shape):
    zeros = (0,) * len(shape)
    return pl.BlockSpec(shape, lambda *_: zeros)


SMEM_SPEC = pl.BlockSpec(memory_space=pltpu.SMEM)
ANY_SPEC = pl.BlockSpec(memory_space=pl.ANY)


def params(**kw):
    return pltpu.CompilerParams(vmem_limit_bytes=60 * 1024 * 1024, **kw)


def remote(src, dst, send, recv, **where):
    return pltpu.make_async_remote_copy(
        src_ref=src,
        dst_ref=dst,
        send_sem=send,
        recv_sem=recv,
        device_id=where,
        device_id_type=MESH,
    )


def greet(axes_and_peers):
    barrier = pltpu.get_barrier_semaphore()
    for where in axes_and_peers:
        pl.semaphore_signal(barrier, inc=1, device_id=where, device_id_type=MESH)
    pl.semaphore_wait(barrier, len(axes_and_peers))


def head_peer(me, chips, dy, dc):
    y, core = me // 2, me % 2
    return ((y + dy) % chips) * 2 + (core + dc) % 2


def project_copies(seq_count, head_count, hidden, w, halo, hop, send, recv):
    me = lax.axis_index("seq")
    head = lax.axis_index("head")
    chips = head_count // 2
    tokens = hidden.shape[0]
    after = (me + 1) % seq_count
    before = (me + seq_count - 1) % seq_count
    first, last = pl.ds(0, HALO), pl.ds(tokens - HALO, HALO)
    low, high = pl.ds(0, HALO), pl.ds(HALO, HALO)
    half = w.shape[0] // 2
    top, bottom = pl.ds(0, half), pl.ds(half, half)
    up = head_peer(head, chips, 1, 0)
    down = head_peer(head, chips, chips - 1, 0)
    partner = head_peer(head, chips, 0, 1)
    return (
        remote(hidden.at[last], halo.at[low], send.at[0], recv.at[0], seq=after),
        remote(hidden.at[first], halo.at[high], send.at[1], recv.at[1], seq=before),
        remote(w.at[top], hop.at[0, top], send.at[2], recv.at[2], head=up),
        remote(w.at[bottom], hop.at[1, bottom], send.at[3], recv.at[3], head=down),
        remote(w, hop.at[2], send.at[4], recv.at[4], head=partner),
    ), [{"seq": after}, {"seq": before}, {"head": up}, {"head": down}, {"head": partner}]


def project_kernel(
    mesh_shape,
    h_ref,
    gain_ref,
    vw_ref,
    sw_ref,
    tw_ref,
    hidden,
    w,
    mix_ref,
    raw_ref,
    halo,
    hop,
    turned,
    rows,
    send,
    recv,
):
    i = pl.program_id(0)
    copies, peers = project_copies(*mesh_shape, hidden, w, halo, hop, send, recv)
    barrier = pltpu.get_barrier_semaphore()

    @pl.when(i == 0)
    def _():
        for where in peers:
            pl.semaphore_signal(barrier, inc=1, device_id=where, device_id_type=MESH)
        narrow = tw_ref[...].astype(f32)
        turned[...] = jnp.concatenate([narrow, narrow], axis=0).astype(bf16)

    @pl.when(i == 1)
    def _():
        pl.semaphore_wait(barrier, len(peers))
        for copy in copies:
            copy.start()

    inner = vw_ref.shape[1]
    gain = gain_ref[...].reshape(1, -1)
    deep = min(256, h_ref.shape[0])
    for first in range(0, h_ref.shape[0], deep):
        for r in range(first, first + deep, 32):
            rows[r : r + 32, :] = normalized(h_ref[r : r + 32, :], gain)
        at = slice(first, first + deep)
        n = rows[at, :]
        mix_ref[at, :inner] = mm(n, vw_ref[...]).astype(bf16)
        mix_ref[at, inner:] = mm(n, sw_ref[...]).astype(bf16)
        raw = mm(turned[...], n, NT)
        for q in range(deep // CHUNK):
            raw_ref[first // CHUNK + q] = raw[:, q * CHUNK : (q + 1) * CHUNK]

    @pl.when(i == pl.num_programs(0) - 1)
    def _():
        for copy in copies:
            copy.wait()


def project(mesh_shape, hidden, gain, vw, sw, tw, w):
    tokens, width = hidden.shape
    inner = vw.shape[1]
    mixed = inner + sw.shape[1]
    rows = tokens // mesh_shape[1]
    return pl.pallas_call(
        functools.partial(project_kernel, mesh_shape),
        grid=(tokens // rows,),
        in_specs=[
            pl.BlockSpec((rows, width), lambda i: (i, 0)),
            whole(gain.shape),
            whole(vw.shape),
            whole(sw.shape),
            whole(tw.shape),
            ANY_SPEC,
            ANY_SPEC,
        ],
        out_specs=[
            pl.BlockSpec((rows, mixed), lambda i: (i, 0)),
            pl.BlockSpec((rows // CHUNK, 8, CHUNK), lambda i: (i, 0, 0)),
            ANY_SPEC,
            ANY_SPEC,
        ],
        out_shape=[
            jax.ShapeDtypeStruct((tokens, mixed), bf16),
            jax.ShapeDtypeStruct((tokens // CHUNK, 8, CHUNK), f32),
            jax.ShapeDtypeStruct((2 * HALO, width), bf16),
            jax.ShapeDtypeStruct((3,) + w.shape, bf16),
        ],
        scratch_shapes=[
            pltpu.VMEM((8, width), bf16),
            pltpu.VMEM((rows, width), bf16),
            pltpu.SemaphoreType.DMA((5,)),
            pltpu.SemaphoreType.DMA((5,)),
        ],
        compiler_params=params(collective_id=2, has_side_effects=True),
        name="project",
    )(hidden, gain, vw, sw, tw, hidden, w)


def head_lanes(columns):
    low = lax.broadcasted_iota(jnp.int32, (columns[0].shape[0], 2 * HEAD_DIM), 1) < HEAD_DIM
    pairs = [
        jnp.where(low, columns[2 * p], columns[2 * p + 1]) for p in range(len(columns) // 2)
    ]
    return jnp.concatenate(pairs, axis=1)


def decays(first_row, raw, lens_ref, bias_ref, rate_ref):
    chunks = raw.shape[0]
    shape = (chunks, 8, CHUNK)
    sub = lax.broadcasted_iota(jnp.int32, shape, 1)
    upper = sub < 4
    head = jnp.where(upper, sub, sub - 4)
    pos = (
        first_row
        + lax.broadcasted_iota(jnp.int32, shape, 0) * CHUNK
        + lax.broadcasted_iota(jnp.int32, shape, 2)
    )
    start = jnp.zeros(shape, jnp.int32)
    stop = jnp.full(shape, 1 << 30, jnp.int32)
    edge = jnp.int32(0)
    for k in range(PIECES):
        start = jnp.where(pos >= edge, edge, start)
        edge = edge + lens_ref[k]
        stop = jnp.minimum(stop, jnp.where(edge > pos, edge, 1 << 30))
    since = pos - start
    until = stop - 1 - pos
    bias = jnp.zeros(shape, f32)
    rate = jnp.zeros(shape, f32)
    for h in range(4):
        bias = jnp.where(head == h, bias_ref[h], bias)
        rate = jnp.where(head == h, rate_ref[h], rate)
    rate = jnp.exp(rate) * (-LOG2E)
    z = raw + bias
    step = jnp.maximum(z, 0.0) + jnp.log1p(jnp.exp(-jnp.abs(z)))
    log = step * rate
    reset = jnp.where(since == 0, -RESET, 0.0)
    ones = (
        lax.broadcasted_iota(jnp.int32, (CHUNK, CHUNK), 0)
        <= lax.broadcasted_iota(jnp.int32, (CHUNK, CHUNK), 1)
    ).astype(f32)
    cum = mm(
        (log + reset).reshape(chunks * 8, CHUNK), ones, precision=lax.Precision.HIGHEST
    ).reshape(shape)
    excl = cum - log
    total = cum[:, :, CHUNK - 1 :]
    log_step = jnp.where(step > 0.0, jnp.log2(step), -RESET)
    row = jnp.where(upper, cum - log_step, excl + log_step)
    g1 = jnp.where(upper, cum, excl)
    g2 = jnp.where(upper, jnp.exp2(cum), jnp.exp2(total - cum) * step)
    g3 = jnp.where(upper, jnp.exp2(total - excl), jnp.exp2(excl) * step)
    g4 = jnp.where(upper, since, until).astype(f32)
    return row, g1, g2, g3, g4


def states_kernel(
    axis,
    mix_ref,
    before_ref,
    after_ref,
    halo_ref,
    gain_ref,
    vw_ref,
    sw_ref,
    raw_ref,
    lens_ref,
    bias_ref,
    rate_ref,
    cv_ref,
    cs_ref,
    conv_ref,
    fresh_ref,
    cols_ref,
    row_ref,
    end_ref,
    total_ref,
    prod,
    halo,
    run,
    reach,
    spread,
    near,
):
    g = pl.program_id(0)
    groups = pl.num_programs(0)
    inner = vw_ref.shape[1]
    rows, mixed = mix_ref.shape
    rounds = rows // CHUNK
    blocks = mixed // 128
    first_row = lax.axis_index(axis) * (groups * rows)

    @pl.when(g == 0)
    def _():
        n = normalized(halo_ref[...], gain_ref[...].reshape(1, -1))
        halo[:, :inner] = mm(n, vw_ref[...]).astype(bf16).astype(f32)
        halo[:, inner:] = mm(n, sw_ref[...]).astype(bf16).astype(f32)
        row, g1, g2, g3, g4 = decays(first_row, raw_ref[...], lens_ref, bias_ref, rate_ref)
        row_ref[...] = row
        cols_ref[:, 0:8, :] = g1
        cols_ref[:, 8:16, :] = g2
        cols_ref[:, 16:24, :] = g3
        cols_ref[:, 24:32, :] = g4
        run[...] = jnp.zeros_like(run)
        reach[...] = jnp.zeros_like(reach)
        line = lax.broadcasted_iota(jnp.int32, spread.shape, 0) % 32
        lane = lax.broadcasted_iota(jnp.int32, spread.shape, 1)
        wanted = 12 + (lane // inner) * 8 + (lane % inner) // HEAD_DIM
        spread[...] = (line == wanted).astype(f32).astype(bf16)

        def clear(k, carry):
            near[k] = 0
            return carry

        lax.fori_loop(0, near.shape[0], clear, 0)

        def mark(k, edge):
            for shift in (-(CONV - 1), CONV - 2):
                at = (edge + shift - first_row + rows) // rows
                near[jnp.clip(at, 0, near.shape[0] - 1)] = 1
            return edge + lens_ref[jnp.minimum(k, PIECES - 1)]

        lax.fori_loop(0, PIECES + 1, mark, jnp.int32(0))

    taps = jnp.concatenate([cv_ref[...], cs_ref[...]], axis=1).astype(f32) * 0.5

    def put(b, at, values):
        lanes = slice(b * 128, (b + 1) * 128)
        for k in range(CONV - 1):
            prod[k, b, at : at + values.shape[0], :] = values * taps[k : k + 1, lanes]

    def ready(q):
        for b in range(blocks):
            lanes = slice(b * 128, (b + 1) * 128)
            put(b, REACH + q * CHUNK, mix_ref[q * CHUNK : (q + 1) * CHUNK, lanes].astype(f32))

    def group(masked):
        for b in range(blocks):
            lanes = slice(b * 128, (b + 1) * 128)
            ahead = before_ref[:, lanes].astype(f32)[16 - REACH :, :]
            put(b, 0, jnp.where(g == 0, halo[HALO - REACH : HALO, lanes], ahead))
            behind = after_ref[:, lanes].astype(f32)[:REACH, :]
            put(b, REACH + rows, jnp.where(g == groups - 1, halo[HALO : HALO + REACH, lanes], behind))
        ready(0)
        for q in range(rounds):
            if q + 1 < rounds:
                ready(q + 1)
            chunk(q, masked)

    def chunk(q, masked):
        cols = cols_ref[g * rounds + q]
        high = cols.astype(bf16).astype(f32)
        both = jnp.concatenate([high, cols - high], axis=0).astype(bf16)
        tails = mm(both, spread[...], TN)
        passing = head_lanes([cols[h : h + 1, CHUNK - 1 :] for h in range(4)])
        if masked:
            turned = jnp.concatenate([cols, jnp.zeros((CHUNK - 32, CHUNK), f32)], axis=0).T
            sides = [jnp.broadcast_to(turned[:, r : r + 1], (CHUNK, 128)) for r in (24, 28)]
        write = [None, None]
        for b in [inner // 128] + list(range(inner // 128)) + list(range(inner // 128 + 1, blocks)):
            lanes = slice(b * 128, (b + 1) * 128)
            centre = mix_ref[q * CHUNK : (q + 1) * CHUNK, lanes].astype(f32) * taps[CONV - 1 : CONV, lanes]
            for d in range(2):
                half = centre
                for distance in range(1, CONV):
                    at = REACH + q * CHUNK + (distance if d else -distance)
                    term = prod[CONV - 1 - distance, b, at : at + CHUNK, :]
                    if masked:
                        term = jnp.where(sides[d] >= distance, term, 0.0)
                    half = half + term
                value = half * jnp.tanh(half) + half
                at = d * mixed + b * 128
                narrow = value.astype(bf16)
                conv_ref[q, 0, :, at : at + 128] = narrow
                if b == inner // 128:
                    write[d] = narrow
                elif b < inner // 128:
                    at = d * inner + b * 128
                    scaled = (value * tails[:, at : at + 128]).astype(bf16)
                    fresh = mm(write[d], scaled, TN)
                    fresh_ref[q, d, :, lanes] = fresh.astype(bf16)
                    if d == 0:
                        run[0, :, lanes] = run[0, :, lanes] * jnp.exp2(passing[:, lanes]) + fresh
                    else:
                        run[1, :, lanes] = run[1, :, lanes] + jnp.exp2(reach[0:1, lanes]) * fresh
        reach[...] = reach[...] + passing

    edges = near[g + 1]

    @pl.when(edges == 0)
    def _():
        group(False)

    @pl.when(edges != 0)
    def _():
        group(True)

    @pl.when(g == groups - 1)
    def _():
        end_ref[...] = run[...].astype(bf16)
        total_ref[...] = reach[...]


def states(axis, owners, mix, halo, gain, vw, sw, raw, lens, bias, rate, cv, cs):
    tokens, mixed = mix.shape
    chunks = tokens // CHUNK
    inner = vw.shape[1]
    rounds = chunks // owners
    rows = rounds * CHUNK
    per = rows // 16
    last = tokens // 16 - 1
    return pl.pallas_call(
        functools.partial(states_kernel, axis),
        grid=(owners,),
        in_specs=[
            pl.BlockSpec((rows, mixed), lambda c: (c, 0)),
            pl.BlockSpec((16, mixed), lambda c: (jnp.maximum(c * per - 1, 0), 0)),
            pl.BlockSpec((16, mixed), lambda c: (jnp.minimum(c * per + per, last), 0)),
            whole(halo.shape),
            whole(gain.shape),
            whole(vw.shape),
            whole(sw.shape),
            whole(raw.shape),
            SMEM_SPEC,
            SMEM_SPEC,
            SMEM_SPEC,
            whole(cv.shape),
            whole(cs.shape),
        ],
        out_specs=[
            pl.BlockSpec((rounds, 1, CHUNK, 2 * mixed), lambda c: (0, c, 0, 0)),
            pl.BlockSpec((rounds, 2, STATE, inner), lambda c: (c, 0, 0, 0)),
            whole((chunks, 32, CHUNK)),
            whole((chunks, 8, CHUNK)),
            whole((2, STATE, inner)),
            whole((8, inner)),
        ],
        out_shape=[
            jax.ShapeDtypeStruct((rounds, owners, CHUNK, 2 * mixed), bf16),
            jax.ShapeDtypeStruct((chunks, 2, STATE, inner), bf16),
            jax.ShapeDtypeStruct((chunks, 32, CHUNK), f32),
            jax.ShapeDtypeStruct((chunks, 8, CHUNK), f32),
            jax.ShapeDtypeStruct((2, STATE, inner), bf16),
            jax.ShapeDtypeStruct((8, inner), f32),
        ],
        scratch_shapes=[
            pltpu.VMEM((CONV - 1, mixed // 128, rows + 2 * REACH, 128), f32),
            pltpu.VMEM((2 * HALO, mixed), f32),
            pltpu.VMEM((2, STATE, inner), f32),
            pltpu.VMEM((8, inner), f32),
            pltpu.VMEM((64, 2 * inner), bf16),
            pltpu.SMEM((owners + 2,), jnp.int32),
        ],
        compiler_params=params(),
        name="states",
    )(mix, mix, mix, halo, gain, vw, sw, raw, lens, bias, rate, cv, cs)


def split(x, parts):
    pieces = []
    for _ in range(parts - 1):
        pieces.append(x.astype(bf16).astype(f32))
        x = x - pieces[-1]
    return pieces + [x]


def finish_kernel(
    seq_count,
    head_count,
    end_ref,
    total_ref,
    cols_ref,
    row_ref,
    skip_ref,
    gain_ref,
    gw_ref,
    norm_gain_ref,
    conv_hbm,
    fresh_hbm,
    hidden_hbm,
    w_hbm,
    hop_hbm,
    out_ref,
    conv,
    wide,
    gate,
    fresh,
    rest,
    weight,
    ends,
    totals,
    incoming,
    entry,
    pick,
    spread,
    inside,
    gated,
    squares,
    others,
    sending,
    arrived,
    load,
    seq_send,
    seq_recv,
    w_send,
    w_recv,
    ss_send,
    ss_recv,
    send,
    recv,
):
    me = lax.axis_index("seq")
    head = lax.axis_index("head")
    chips = head_count // 2
    rounds, owners = conv.shape[0], conv.shape[1]
    chunks = rounds * owners
    inner = gate.shape[3]
    mixed = conv.shape[3] // 2
    rows = rounds * CHUNK
    slots = [(dy, dc) for dy in range(chips) for dc in range(2)]
    peers = [head_peer(head, chips, dy, dc) for dy, dc in slots]
    up, down, partner = peers[2], peers[2 * chips - 2], peers[1]

    def fetch(src, dst, n):
        copy = pltpu.make_async_copy(src, dst, load.at[n])
        copy.start()
        return copy

    def part(k):
        return pl.ds(k * inner, inner)

    conv_in, wide_in = [], []
    for q in range(rounds):
        conv_in.append(fetch(conv_hbm.at[q], conv.at[q], q))
        wide_in.append(fetch(hidden_hbm.at[:, q], wide.at[q], rounds + 7 + q))
    fresh_in = fetch(fresh_hbm, fresh, rounds)
    half = inner // 2
    side = (2 * chips - 2) * inner
    far = 4 * inner
    top, bottom = pl.ds(0, half), pl.ds(half, half)
    late = [
        fetch(hidden_hbm.at[head], rest, rounds + 2),
        fetch(w_hbm, weight.at[part(0)], rounds + 3),
        fetch(hop_hbm.at[2], weight.at[part(1)], rounds + 4),
        fetch(hop_hbm.at[0, top], weight.at[pl.ds(2 * inner, half)], rounds + 5),
        fetch(hop_hbm.at[1, bottom], weight.at[pl.ds(side + half, half)], rounds + 6),
    ]

    greet(
        [{"seq": (me + k) % seq_count} for k in range(1, seq_count)]
        + [{"head": p} for p in peers[1:]]
    )
    started = []

    def start(copy):
        copy.start()
        started.append(copy)
        return copy

    travelling = []
    for k in range(1, seq_count):
        target = (me + k) % seq_count
        backward = (me + k) // seq_count
        travelling.append(
            start(
                remote(
                    end_ref.at[backward], ends.at[k], seq_send.at[0, k], seq_recv.at[0, k], seq=target
                )
            )
        )
        travelling.append(
            start(remote(total_ref, totals.at[k], seq_send.at[1, k], seq_recv.at[1, k], seq=target))
        )
    def weigh(n, src, row, where, count=half):
        at = weight.at[pl.ds(row, count)]
        return start(remote(src, at, w_send.at[n], w_recv.at[n], head=where))

    u1 = weigh(0, w_hbm.at[bottom], 2 * inner + half, up)
    u2 = weigh(1, w_hbm.at[top], side, down)
    t1 = weigh(2, hop_hbm.at[0, top], far, up)
    t3 = weigh(3, hop_hbm.at[1, bottom], far + half, down)
    beside = [
        weigh(4, hop_hbm.at[0, top], 3 * inner, partner),
        weigh(5, hop_hbm.at[1, bottom], side + inner + half, partner),
    ]

    def cross():
        for copy in (u1, u2, t1, t3):
            copy.wait_recv()
        return [
            weigh(6, weight.at[pl.ds(2 * inner + half, half)], 3 * inner + half, partner),
            weigh(7, weight.at[pl.ds(side, half)], side + inner, partner),
            weigh(8, weight.at[part(4)], 5 * inner, partner, inner),
        ]

    i = lax.broadcasted_iota(jnp.int32, (CHUNK, CHUNK), 0)
    j = lax.broadcasted_iota(jnp.int32, (CHUNK, CHUNK), 1)
    lower = i >= j
    upper = i <= j
    low = j < HEAD_DIM
    skip = head_lanes([jnp.full((1, 1), skip_ref[h], f32) for h in range(4)])
    sub = lax.broadcasted_iota(jnp.int32, (8, CHUNK), 0)
    line = lax.broadcasted_iota(jnp.int32, pick.shape[1:], 0)
    block = lax.broadcasted_iota(jnp.int32, pick.shape[1:], 1) // CHUNK
    sign = jnp.where(block < 4, 1.0, -1.0)
    chosen = jnp.where((line < 24) & (line % 8 == block), sign, 0.0).astype(bf16)
    for u in range(pick.shape[0]):
        pick[u] = chosen
    line = lax.broadcasted_iota(jnp.int32, spread.shape, 0)
    lane = lax.broadcasted_iota(jnp.int32, spread.shape, 1)
    wanted = (lane // inner) * 8 + (lane % inner) // HEAD_DIM
    spread[...] = (line % 16 == wanted).astype(f32).astype(bf16)

    def within(q, d, u):
        c = d * rounds + q
        row = row_ref[c]
        lines = jnp.concatenate(split(jnp.where(sub < 4, -row, row), 3), axis=0)
        for n in range(8):
            own = lax.broadcasted_iota(jnp.int32, lines.shape, 0) % 8 == n
            pick[u, 32:56, n * CHUNK : (n + 1) * CHUNK] = jnp.where(own, lines, 0.0).astype(bf16)
        left = jnp.concatenate(
            split(cols_ref[c, 0:8, :], 3)
            + [jnp.zeros((8, CHUNK), f32), jnp.ones((24, CHUNK), f32), jnp.zeros((8, CHUNK), f32)],
            axis=0,
        ).astype(bf16)
        made = mm(left, pick[u], TN)
        pair = []
        for e, keep in ((0, lower), (1, upper)):
            base = e * mixed + inner
            write = conv[q, d, :, base : base + STATE]
            read = conv[q, d, :, base + STATE : base + 2 * STATE]
            pair.append(jnp.where(keep, mm(read, write, NT), 0.0))
        for p in range(2):
            weights = ([], [])
            for h in (2 * p, 2 * p + 1):
                table = jnp.exp2(
                    jnp.where(
                        lower,
                        made[:, h * CHUNK : (h + 1) * CHUNK],
                        made[:, (4 + h) * CHUNK : (5 + h) * CHUNK],
                    )
                )
                for e in range(2):
                    weights[e].append((pair[e] * table).astype(bf16))
            for e in range(2):
                at = e * mixed + p * CHUNK
                x = conv[q, d, :, at : at + CHUNK]
                zero = jnp.zeros_like(x)
                stacked = jnp.concatenate([jnp.where(low, x, zero), jnp.where(low, zero, x)], axis=0)
                made_here = mm(jnp.concatenate(weights[e], axis=1), stacked)
                made_here = made_here + skip[:, p * CHUNK : (p + 1) * CHUNK] * x.astype(f32)
                inside[q, d, :, e * inner + p * CHUNK : e * inner + (p + 1) * CHUNK] = made_here

    def gates(q, n):
        two = wide[q, pl.ds(2 * n, 2)].reshape(2 * CHUNK, wide.shape[3])
        two = mm(normalized(two, norm_gain_ref[...].reshape(1, -1)), gw_ref[...]).astype(bf16)
        for u in range(2):
            gate[q, 2 * n + u] = two[u * CHUNK : (u + 1) * CHUNK]

    for q in range(rounds):
        conv_in[q].wait()
        wide_in[q].wait()

        def step(n, carry, q=q):
            if q == 0:
                gates(q, n)
            for u in range(2):
                within(q, 2 * n + u, u)
            return carry

        lax.fori_loop(0, owners // 2, step, 0)

    for copy in travelling:
        copy.wait_recv()
    incoming[...] = jnp.zeros_like(incoming)
    for k in range(seq_count - 1, 0, -1):

        @pl.when(k <= me)
        def _(k=k):
            incoming[0] = incoming[0] * jnp.exp2(totals[k, 0:1, :]) + ends[k].astype(f32)

    for k in range(1, seq_count):

        @pl.when(k > me)
        def _(k=k):
            incoming[1] = incoming[1] * jnp.exp2(totals[k, 0:1, :]) + ends[k].astype(f32)

    fresh_in.wait()

    def passing(c):
        return jnp.exp2(head_lanes([cols_ref[c, h : h + 1, CHUNK - 1 :] for h in range(4)]))

    def walk(n, carry):
        for e in range(2):
            at = [2 * n, 2 * n + 1] if e == 0 else [chunks - 1 - 2 * n, chunks - 2 - 2 * n]
            factors = [passing(c) for c in at]
            for lanes in (slice(0, inner // 2), slice(inner // 2, inner)):
                state = incoming[e, :, lanes]
                for c, factor in zip(at, factors):
                    entry[e, c, :, lanes] = state.astype(bf16)
                    state = state * factor[:, lanes] + fresh[c, e, :, lanes].astype(f32)
                incoming[e, :, lanes] = state
        return carry

    lax.fori_loop(0, chunks // 2, walk, 0)

    ones = jnp.ones((8, inner), bf16)
    gain = gain_ref[...].reshape(1, -1).astype(f32)
    sixteen = lax.broadcasted_iota(jnp.int32, (2 * owners, CHUNK), 0)

    def carried(q, d, sums):
        c = d * rounds + q
        left = jnp.concatenate(split(cols_ref[c, 8:24, :], 2), axis=0).astype(bf16)
        scale = mm(left, spread[...], TN)
        act = silu(gate[q, d].astype(f32))
        for e in range(2):
            at = e * mixed + inner + STATE
            lanes = slice(e * inner, (e + 1) * inner)
            part_in = mm(conv[q, d, :, at : at + STATE], entry[e, c])
            value = (inside[q, d, :, lanes] + part_in * scale[:, lanes]) * act
            gated[q, d, :, lanes] = value.astype(bf16)
            square = mm(ones, (value * value).astype(bf16), NT)
            square = jnp.concatenate([square] * (2 * owners // 8), axis=0)
            sums = jnp.where(sixteen == 2 * d + e, square, sums)
        return sums

    def combine(q):
        for k in range(1, head_count):
            ss[q][k - 1].wait_recv()
        total = squares[q]
        for k in range(1, head_count):
            total = total + others[q, k]
        total = lax.rsqrt(total * (1.0 / (inner * head_count)) + epsilon)
        scale = jnp.concatenate([total, jnp.zeros((CHUNK - 2 * owners, CHUNK), f32)], axis=0).T
        for d in range(owners):
            both = gated[q, d, :, :inner].astype(f32) * scale[:, 2 * d : 2 * d + 1]
            both = both + gated[q, d, :, inner:].astype(f32) * scale[:, 2 * d + 1 : 2 * d + 2]
            sending[q, d] = (both * gain).astype(bf16)
        arrived[q * CHUNK : (q + 1) * CHUNK, 0:inner] = sending[q, head]
        return [
            start(
                remote(
                    sending.at[q, peers[k]],
                    arrived.at[pl.ds(q * CHUNK, CHUNK), part(k)],
                    send.at[q, k],
                    recv.at[q, k],
                    head=peers[k],
                )
            )
            for k in sorted(range(1, head_count), key=lambda k: -min(slots[k][0], chips - slots[k][0]))
        ]

    ss, pieces = [], []
    for q in range(rounds):
        def some(n, sums, q=q):
            for u in range(4):
                sums = carried(q, 4 * n + u, sums)
            return sums

        squares[q] = lax.fori_loop(0, owners // 4, some, jnp.zeros((2 * owners, CHUNK), f32))
        ss.append(
            [
                start(
                    remote(
                        squares.at[q], others.at[q, k], ss_send.at[q, k], ss_recv.at[q, k], head=peers[k]
                    )
                )
                for k in range(1, head_count)
            ]
        )
        if q + 1 < rounds:

            def later(n, carry, q=q):
                gates(q + 1, n)
                return carry

            lax.fori_loop(0, owners // 2, later, 0)
        pieces.append(combine(q))
        if q == 0:
            beside += cross()

    for copy in late:
        copy.wait()
    for copy in beside:
        copy.wait_recv()
    width = out_ref.shape[1]
    step_lanes = 256
    early = (rounds - 1) * CHUNK
    for first, count, done in ((0, early, pieces[:-1]), (early, CHUNK, pieces[-1:])):
        for batch in done:
            for copy in batch:
                copy.wait_recv()
        if count:

            def project_out(b, carry, first=first, count=count):
                lanes = pl.ds(pl.multiple_of(b * step_lanes, step_lanes), step_lanes)
                here = pl.ds(first, count)
                of = pl.ds(first // CHUNK, count // CHUNK)
                out_ref[here, lanes] = (
                    mm(arrived[here, :], weight[:, lanes]) + rest[of, :, lanes].reshape(count, step_lanes).astype(f32)
                ).astype(bf16)
                return carry

            lax.fori_loop(0, width // step_lanes, project_out, 0)
    for copy in started:
        copy.wait_send()


def finish(mesh_shape, end, total, cols, row, skip, gain, gw, norm_gain, conv, fresh, hidden, w, hop):
    seq_count, head_count = mesh_shape
    rounds, owners = conv.shape[:2]
    rows = rounds * CHUNK
    inner = gw.shape[1]
    width = hidden.shape[3]
    dma = pltpu.SemaphoreType.DMA
    return pl.pallas_call(
        functools.partial(finish_kernel, seq_count, head_count),
        in_specs=[
            whole(end.shape),
            whole(total.shape),
            whole(cols.shape),
            whole(row.shape),
            SMEM_SPEC,
            whole(gain.shape),
            whole(gw.shape),
            whole(norm_gain.shape),
        ]
        + [ANY_SPEC] * 5,
        out_specs=whole((rows, width)),
        out_shape=jax.ShapeDtypeStruct((rows, width), bf16),
        scratch_shapes=[
            pltpu.VMEM(conv.shape, bf16),
            pltpu.VMEM((rounds, owners, CHUNK, width), bf16),
            pltpu.VMEM((rounds, owners, CHUNK, inner), bf16),
            pltpu.VMEM(fresh.shape, bf16),
            pltpu.VMEM((rounds, CHUNK, width), bf16),
            pltpu.VMEM((head_count * inner, width), bf16),
            pltpu.VMEM((seq_count,) + end.shape[1:], bf16),
            pltpu.VMEM((seq_count,) + total.shape, f32),
            pltpu.VMEM(end.shape, f32),
            pltpu.VMEM((2, rounds * owners) + end.shape[1:], bf16),
            pltpu.VMEM((2, 64, 8 * CHUNK), bf16),
            pltpu.VMEM((32, 2 * inner), bf16),
            pltpu.VMEM((rounds, owners, CHUNK, 2 * inner), f32),
            pltpu.VMEM((rounds, owners, CHUNK, 2 * inner), bf16),
            pltpu.VMEM((rounds, 2 * owners, CHUNK), f32),
            pltpu.VMEM((rounds, head_count, 2 * owners, CHUNK), f32),
            pltpu.VMEM((rounds, head_count, CHUNK, inner), bf16),
            pltpu.VMEM((rows, head_count * inner), bf16),
            dma((2 * rounds + 7,)),
            dma((2, seq_count)),
            dma((2, seq_count)),
            dma((9,)),
            dma((9,)),
            dma((rounds, head_count)),
            dma((rounds, head_count)),
            dma((rounds, head_count)),
            dma((rounds, head_count)),
        ],
        compiler_params=params(collective_id=1, has_side_effects=True),
        name="finish",
    )(end, total, cols, row, skip, gain, gw, norm_gain, conv, fresh, hidden, w, hop)


def local(
    hidden_in,
    norm_gain,
    gate_weight,
    value_weight,
    state_weight,
    step_weight,
    step_bias,
    decay_log,
    skip_gain,
    conv_value,
    conv_state,
    output_gain,
    output_weight,
    piece_lengths,
):
    seq_count, head_count = lax.axis_size("seq"), lax.axis_size("head")
    shape = (seq_count, head_count)
    mix, raw, halo, hop = project(
        shape, hidden_in, norm_gain, value_weight, state_weight, step_weight.T, output_weight
    )
    conv, fresh, cols, row, end, total = states(
        "seq",
        head_count,
        mix,
        halo,
        norm_gain,
        value_weight,
        state_weight,
        raw,
        piece_lengths,
        step_bias,
        decay_log,
        conv_value,
        conv_state,
    )
    return finish(
        shape,
        end,
        total,
        cols,
        row,
        skip_gain,
        output_gain,
        gate_weight,
        norm_gain,
        conv,
        fresh,
        hidden_in.reshape(head_count, -1, CHUNK, hidden_in.shape[1]),
        output_weight,
        hop,
    )


def solution(mesh):
    in_specs = (
        P("seq", None),
        P(),
        P(None, "head"),
        P(None, "head"),
        P(),
        P(None, "head"),
        P("head"),
        P("head"),
        P("head"),
        P(None, "head"),
        P(),
        P("head"),
        P("head", None),
        P(),
    )
    out_specs = P(("seq", "head"), None)
    return jax.shard_map(local, mesh=mesh, in_specs=in_specs, out_specs=out_specs, check_vma=False)
```

```python
import functools
import math

import jax
import jax.numpy as jnp
from jax import lax
from jax.experimental import pallas as pl
from jax.experimental.pallas import tpu as pltpu
from jax.sharding import PartitionSpec as P

HEAD_DIM = 64
STATE = 128
CONV = 4
CHUNK = 128
PIECES = 16
HALO = 16
REACH = 8
RESET = 256.0
LOG2E = math.log2(math.e)

f32 = jnp.float32
bf16 = jnp.bfloat16
epsilon = 1e-05
MESH = pl.DeviceIdType.MESH
NN = (((1,), (0,)), ((), ()))
NT = (((1,), (1,)), ((), ()))
TN = (((0,), (0,)), ((), ()))


def mm(a, b, dims=NN, precision=None):
    return lax.dot_general(a, b, dims, precision=precision, preferred_element_type=f32)


def silu(x):
    half = 0.5 * x
    return half * jnp.tanh(half) + half


def normalized(h, gain):
    wide = h.astype(f32)
    scale = lax.rsqrt(jnp.mean(wide * wide, axis=1, keepdims=True) + epsilon)
    return (wide * scale * gain.astype(f32)).astype(bf16)


def whole(shape):
    zeros = (0,) * len(shape)
    return pl.BlockSpec(shape, lambda *_: zeros)


SMEM_SPEC = pl.BlockSpec(memory_space=pltpu.SMEM)
ANY_SPEC = pl.BlockSpec(memory_space=pl.ANY)


def params(**kw):
    return pltpu.CompilerParams(vmem_limit_bytes=60 * 1024 * 1024, **kw)


def remote(src, dst, send, recv, **where):
    return pltpu.make_async_remote_copy(
        src_ref=src,
        dst_ref=dst,
        send_sem=send,
        recv_sem=recv,
        device_id=where,
        device_id_type=MESH,
    )


def greet(axes_and_peers):
    barrier = pltpu.get_barrier_semaphore()
    for where in axes_and_peers:
        pl.semaphore_signal(barrier, inc=1, device_id=where, device_id_type=MESH)
    pl.semaphore_wait(barrier, len(axes_and_peers))


def head_peer(me, chips, dy, dc):
    y, core = me // 2, me % 2
    return ((y + dy) % chips) * 2 + (core + dc) % 2


def project_copies(seq_count, head_count, hidden, w, halo, hop, send, recv):
    me = lax.axis_index("seq")
    head = lax.axis_index("head")
    chips = head_count // 2
    tokens = hidden.shape[0]
    after = (me + 1) % seq_count
    before = (me + seq_count - 1) % seq_count
    first, last = pl.ds(0, HALO), pl.ds(tokens - HALO, HALO)
    low, high = pl.ds(0, HALO), pl.ds(HALO, HALO)
    half = w.shape[0] // 2
    top, bottom = pl.ds(0, half), pl.ds(half, half)
    up = head_peer(head, chips, 1, 0)
    down = head_peer(head, chips, chips - 1, 0)
    partner = head_peer(head, chips, 0, 1)
    return (
        remote(hidden.at[last], halo.at[low], send.at[0], recv.at[0], seq=after),
        remote(hidden.at[first], halo.at[high], send.at[1], recv.at[1], seq=before),
        remote(w.at[top], hop.at[0, top], send.at[2], recv.at[2], head=up),
        remote(w.at[bottom], hop.at[1, bottom], send.at[3], recv.at[3], head=down),
        remote(w, hop.at[2], send.at[4], recv.at[4], head=partner),
    ), [{"seq": after}, {"seq": before}, {"head": up}, {"head": down}, {"head": partner}]


def project_kernel(
    mesh_shape,
    h_ref,
    gain_ref,
    vw_ref,
    sw_ref,
    tw_ref,
    hidden,
    w,
    mix_ref,
    raw_ref,
    halo,
    hop,
    turned,
    rows,
    send,
    recv,
):
    i = pl.program_id(0)
    copies, peers = project_copies(*mesh_shape, hidden, w, halo, hop, send, recv)
    barrier = pltpu.get_barrier_semaphore()

    @pl.when(i == 0)
    def _():
        for where in peers:
            pl.semaphore_signal(barrier, inc=1, device_id=where, device_id_type=MESH)
        narrow = tw_ref[...].astype(f32)
        turned[...] = jnp.concatenate([narrow, narrow], axis=0).astype(bf16)

    @pl.when(i == 1)
    def _():
        pl.semaphore_wait(barrier, len(peers))
        for copy in copies:
            copy.start()

    inner = vw_ref.shape[1]
    gain = gain_ref[...].reshape(1, -1)
    deep = min(256, h_ref.shape[0])
    for first in range(0, h_ref.shape[0], deep):
        for r in range(first, first + deep, 32):
            rows[r : r + 32, :] = normalized(h_ref[r : r + 32, :], gain)
        at = slice(first, first + deep)
        n = rows[at, :]
        mix_ref[at, :inner] = mm(n, vw_ref[...]).astype(bf16)
        mix_ref[at, inner:] = mm(n, sw_ref[...]).astype(bf16)
        raw = mm(turned[...], n, NT)
        for q in range(deep // CHUNK):
            raw_ref[first // CHUNK + q] = raw[:, q * CHUNK : (q + 1) * CHUNK]

    @pl.when(i == pl.num_programs(0) - 1)
    def _():
        for copy in copies:
            copy.wait()


def project(mesh_shape, hidden, gain, vw, sw, tw, w):
    tokens, width = hidden.shape
    inner = vw.shape[1]
    mixed = inner + sw.shape[1]
    rows = tokens // mesh_shape[1]
    return pl.pallas_call(
        functools.partial(project_kernel, mesh_shape),
        grid=(tokens // rows,),
        in_specs=[
            pl.BlockSpec((rows, width), lambda i: (i, 0)),
            whole(gain.shape),
            whole(vw.shape),
            whole(sw.shape),
            whole(tw.shape),
            ANY_SPEC,
            ANY_SPEC,
        ],
        out_specs=[
            pl.BlockSpec((rows, mixed), lambda i: (i, 0)),
            pl.BlockSpec((rows // CHUNK, 8, CHUNK), lambda i: (i, 0, 0)),
            ANY_SPEC,
            ANY_SPEC,
        ],
        out_shape=[
            jax.ShapeDtypeStruct((tokens, mixed), bf16),
            jax.ShapeDtypeStruct((tokens // CHUNK, 8, CHUNK), f32),
            jax.ShapeDtypeStruct((2 * HALO, width), bf16),
            jax.ShapeDtypeStruct((3,) + w.shape, bf16),
        ],
        scratch_shapes=[
            pltpu.VMEM((8, width), bf16),
            pltpu.VMEM((rows, width), bf16),
            pltpu.SemaphoreType.DMA((5,)),
            pltpu.SemaphoreType.DMA((5,)),
        ],
        compiler_params=params(collective_id=2, has_side_effects=True),
        name="project",
    )(hidden, gain, vw, sw, tw, hidden, w)


def head_lanes(columns):
    low = lax.broadcasted_iota(jnp.int32, (columns[0].shape[0], 2 * HEAD_DIM), 1) < HEAD_DIM
    pairs = [
        jnp.where(low, columns[2 * p], columns[2 * p + 1]) for p in range(len(columns) // 2)
    ]
    return jnp.concatenate(pairs, axis=1)


def decays(first_row, raw, lens_ref, bias_ref, rate_ref):
    chunks = raw.shape[0]
    shape = (chunks, 8, CHUNK)
    sub = lax.broadcasted_iota(jnp.int32, shape, 1)
    upper = sub < 4
    head = jnp.where(upper, sub, sub - 4)
    pos = (
        first_row
        + lax.broadcasted_iota(jnp.int32, shape, 0) * CHUNK
        + lax.broadcasted_iota(jnp.int32, shape, 2)
    )
    start = jnp.zeros(shape, jnp.int32)
    stop = jnp.full(shape, 1 << 30, jnp.int32)
    edge = jnp.int32(0)
    for k in range(PIECES):
        start = jnp.where(pos >= edge, edge, start)
        edge = edge + lens_ref[k]
        stop = jnp.minimum(stop, jnp.where(edge > pos, edge, 1 << 30))
    since = pos - start
    until = stop - 1 - pos
    bias = jnp.zeros(shape, f32)
    rate = jnp.zeros(shape, f32)
    for h in range(4):
        bias = jnp.where(head == h, bias_ref[h], bias)
        rate = jnp.where(head == h, rate_ref[h], rate)
    rate = jnp.exp(rate) * (-LOG2E)
    z = raw + bias
    step = jnp.maximum(z, 0.0) + jnp.log1p(jnp.exp(-jnp.abs(z)))
    log = step * rate
    reset = jnp.where(since == 0, -RESET, 0.0)
    ones = (
        lax.broadcasted_iota(jnp.int32, (CHUNK, CHUNK), 0)
        <= lax.broadcasted_iota(jnp.int32, (CHUNK, CHUNK), 1)
    ).astype(f32)
    cum = mm(
        (log + reset).reshape(chunks * 8, CHUNK), ones, precision=lax.Precision.HIGHEST
    ).reshape(shape)
    excl = cum - log
    total = cum[:, :, CHUNK - 1 :]
    log_step = jnp.where(step > 0.0, jnp.log2(step), -RESET)
    row = jnp.where(upper, cum - log_step, excl + log_step)
    g1 = jnp.where(upper, cum, excl)
    g2 = jnp.where(upper, jnp.exp2(cum), jnp.exp2(total - cum) * step)
    g3 = jnp.where(upper, jnp.exp2(total - excl), jnp.exp2(excl) * step)
    g4 = jnp.where(upper, since, until).astype(f32)
    return row, g1, g2, g3, g4


def states_kernel(
    axis,
    mix_ref,
    before_ref,
    after_ref,
    halo_ref,
    gain_ref,
    vw_ref,
    sw_ref,
    raw_ref,
    lens_ref,
    bias_ref,
    rate_ref,
    cv_ref,
    cs_ref,
    conv_ref,
    fresh_ref,
    cols_ref,
    row_ref,
    end_ref,
    total_ref,
    prod,
    halo,
    run,
    reach,
    spread,
    near,
):
    g = pl.program_id(0)
    groups = pl.num_programs(0)
    inner = vw_ref.shape[1]
    rows, mixed = mix_ref.shape
    rounds = rows // CHUNK
    blocks = mixed // 128
    first_row = lax.axis_index(axis) * (groups * rows)

    @pl.when(g == 0)
    def _():
        n = normalized(halo_ref[...], gain_ref[...].reshape(1, -1))
        halo[:, :inner] = mm(n, vw_ref[...]).astype(bf16).astype(f32)
        halo[:, inner:] = mm(n, sw_ref[...]).astype(bf16).astype(f32)
        row, g1, g2, g3, g4 = decays(first_row, raw_ref[...], lens_ref, bias_ref, rate_ref)
        row_ref[...] = row
        cols_ref[:, 0:8, :] = g1
        cols_ref[:, 8:16, :] = g2
        cols_ref[:, 16:24, :] = g3
        cols_ref[:, 24:32, :] = g4
        run[...] = jnp.zeros_like(run)
        reach[...] = jnp.zeros_like(reach)
        line = lax.broadcasted_iota(jnp.int32, spread.shape, 0) % 32
        lane = lax.broadcasted_iota(jnp.int32, spread.shape, 1)
        wanted = 12 + (lane // inner) * 8 + (lane % inner) // HEAD_DIM
        spread[...] = (line == wanted).astype(f32).astype(bf16)

        def clear(k, carry):
            near[k] = 0
            return carry

        lax.fori_loop(0, near.shape[0], clear, 0)

        def mark(k, edge):
            for shift in (-(CONV - 1), CONV - 2):
                at = (edge + shift - first_row + rows) // rows
                near[jnp.clip(at, 0, near.shape[0] - 1)] = 1
            return edge + lens_ref[jnp.minimum(k, PIECES - 1)]

        lax.fori_loop(0, PIECES + 1, mark, jnp.int32(0))

    taps = jnp.concatenate([cv_ref[...], cs_ref[...]], axis=1).astype(f32) * 0.5

    def put(b, at, values):
        lanes = slice(b * 128, (b + 1) * 128)
        for k in range(CONV - 1):
            prod[k, b, at : at + values.shape[0], :] = values * taps[k : k + 1, lanes]

    def ready(q):
        for b in range(blocks):
            lanes = slice(b * 128, (b + 1) * 128)
            put(b, REACH + q * CHUNK, mix_ref[q * CHUNK : (q + 1) * CHUNK, lanes].astype(f32))

    def group(masked):
        for b in range(blocks):
            lanes = slice(b * 128, (b + 1) * 128)
            ahead = before_ref[:, lanes].astype(f32)[16 - REACH :, :]
            put(b, 0, jnp.where(g == 0, halo[HALO - REACH : HALO, lanes], ahead))
            behind = after_ref[:, lanes].astype(f32)[:REACH, :]
            put(b, REACH + rows, jnp.where(g == groups - 1, halo[HALO : HALO + REACH, lanes], behind))
        ready(0)
        for q in range(rounds):
            if q + 1 < rounds:
                ready(q + 1)
            chunk(q, masked)

    def chunk(q, masked):
        cols = cols_ref[g * rounds + q]
        high = cols.astype(bf16).astype(f32)
        both = jnp.concatenate([high, cols - high], axis=0).astype(bf16)
        tails = mm(both, spread[...], TN)
        passing = head_lanes([cols[h : h + 1, CHUNK - 1 :] for h in range(4)])
        if masked:
            turned = jnp.concatenate([cols, jnp.zeros((CHUNK - 32, CHUNK), f32)], axis=0).T
            sides = [jnp.broadcast_to(turned[:, r : r + 1], (CHUNK, 128)) for r in (24, 28)]
        write = [None, None]
        for b in [inner // 128] + list(range(inner // 128)) + list(range(inner // 128 + 1, blocks)):
            lanes = slice(b * 128, (b + 1) * 128)
            centre = mix_ref[q * CHUNK : (q + 1) * CHUNK, lanes].astype(f32) * taps[CONV - 1 : CONV, lanes]
            for d in range(2):
                half = centre
                for distance in range(1, CONV):
                    at = REACH + q * CHUNK + (distance if d else -distance)
                    term = prod[CONV - 1 - distance, b, at : at + CHUNK, :]
                    if masked:
                        term = jnp.where(sides[d] >= distance, term, 0.0)
                    half = half + term
                value = half * jnp.tanh(half) + half
                at = d * mixed + b * 128
                narrow = value.astype(bf16)
                conv_ref[q, 0, :, at : at + 128] = narrow
                if b == inner // 128:
                    write[d] = narrow
                elif b < inner // 128:
                    at = d * inner + b * 128
                    scaled = (value * tails[:, at : at + 128]).astype(bf16)
                    fresh = mm(write[d], scaled, TN)
                    fresh_ref[q, d, :, lanes] = fresh.astype(bf16)
                    if d == 0:
                        run[0, :, lanes] = run[0, :, lanes] * jnp.exp2(passing[:, lanes]) + fresh
                    else:
                        run[1, :, lanes] = run[1, :, lanes] + jnp.exp2(reach[0:1, lanes]) * fresh
        reach[...] = reach[...] + passing

    edges = near[g + 1]

    @pl.when(edges == 0)
    def _():
        group(False)

    @pl.when(edges != 0)
    def _():
        group(True)

    @pl.when(g == groups - 1)
    def _():
        end_ref[...] = run[...].astype(bf16)
        total_ref[...] = reach[...]


def states(axis, owners, mix, halo, gain, vw, sw, raw, lens, bias, rate, cv, cs):
    tokens, mixed = mix.shape
    chunks = tokens // CHUNK
    inner = vw.shape[1]
    rounds = chunks // owners
    rows = rounds * CHUNK
    per = rows // 16
    last = tokens // 16 - 1
    return pl.pallas_call(
        functools.partial(states_kernel, axis),
        grid=(owners,),
        in_specs=[
            pl.BlockSpec((rows, mixed), lambda c: (c, 0)),
            pl.BlockSpec((16, mixed), lambda c: (jnp.maximum(c * per - 1, 0), 0)),
            pl.BlockSpec((16, mixed), lambda c: (jnp.minimum(c * per + per, last), 0)),
            whole(halo.shape),
            whole(gain.shape),
            whole(vw.shape),
            whole(sw.shape),
            whole(raw.shape),
            SMEM_SPEC,
            SMEM_SPEC,
            SMEM_SPEC,
            whole(cv.shape),
            whole(cs.shape),
        ],
        out_specs=[
            pl.BlockSpec((rounds, 1, CHUNK, 2 * mixed), lambda c: (0, c, 0, 0)),
            pl.BlockSpec((rounds, 2, STATE, inner), lambda c: (c, 0, 0, 0)),
            whole((chunks, 32, CHUNK)),
            whole((chunks, 8, CHUNK)),
            whole((2, STATE, inner)),
            whole((8, inner)),
        ],
        out_shape=[
            jax.ShapeDtypeStruct((rounds, owners, CHUNK, 2 * mixed), bf16),
            jax.ShapeDtypeStruct((chunks, 2, STATE, inner), bf16),
            jax.ShapeDtypeStruct((chunks, 32, CHUNK), f32),
            jax.ShapeDtypeStruct((chunks, 8, CHUNK), f32),
            jax.ShapeDtypeStruct((2, STATE, inner), bf16),
            jax.ShapeDtypeStruct((8, inner), f32),
        ],
        scratch_shapes=[
            pltpu.VMEM((CONV - 1, mixed // 128, rows + 2 * REACH, 128), f32),
            pltpu.VMEM((2 * HALO, mixed), f32),
            pltpu.VMEM((2, STATE, inner), f32),
            pltpu.VMEM((8, inner), f32),
            pltpu.VMEM((64, 2 * inner), bf16),
            pltpu.SMEM((owners + 2,), jnp.int32),
        ],
        compiler_params=params(),
        name="states",
    )(mix, mix, mix, halo, gain, vw, sw, raw, lens, bias, rate, cv, cs)


def split(x, parts):
    pieces = []
    for _ in range(parts - 1):
        pieces.append(x.astype(bf16).astype(f32))
        x = x - pieces[-1]
    return pieces + [x]


def finish_kernel(
    seq_count,
    head_count,
    end_ref,
    total_ref,
    cols_ref,
    row_ref,
    skip_ref,
    gain_ref,
    gw_ref,
    norm_gain_ref,
    conv_hbm,
    fresh_hbm,
    hidden_hbm,
    w_hbm,
    hop_hbm,
    out_ref,
    conv,
    wide,
    gate,
    fresh,
    rest,
    weight,
    ends,
    totals,
    incoming,
    entry,
    pick,
    spread,
    inside,
    gated,
    squares,
    others,
    sending,
    arrived,
    load,
    seq_send,
    seq_recv,
    w_send,
    w_recv,
    ss_send,
    ss_recv,
    send,
    recv,
):
    me = lax.axis_index("seq")
    head = lax.axis_index("head")
    chips = head_count // 2
    rounds, owners = conv.shape[0], conv.shape[1]
    chunks = rounds * owners
    inner = gate.shape[3]
    mixed = conv.shape[3] // 2
    rows = rounds * CHUNK
    slots = [(dy, dc) for dy in range(chips) for dc in range(2)]
    peers = [head_peer(head, chips, dy, dc) for dy, dc in slots]
    up, down, partner = peers[2], peers[2 * chips - 2], peers[1]

    def fetch(src, dst, n):
        copy = pltpu.make_async_copy(src, dst, load.at[n])
        copy.start()
        return copy

    def part(k):
        return pl.ds(k * inner, inner)

    conv_in, wide_in = [], []
    for q in range(rounds):
        conv_in.append(fetch(conv_hbm.at[q], conv.at[q], q))
        wide_in.append(fetch(hidden_hbm.at[:, q], wide.at[q], rounds + 7 + q))
    fresh_in = fetch(fresh_hbm, fresh, rounds)
    half = inner // 2
    side = (2 * chips - 2) * inner
    far = 4 * inner
    top, bottom = pl.ds(0, half), pl.ds(half, half)
    late = [
        fetch(hidden_hbm.at[head], rest, rounds + 2),
        fetch(w_hbm, weight.at[part(0)], rounds + 3),
        fetch(hop_hbm.at[2], weight.at[part(1)], rounds + 4),
        fetch(hop_hbm.at[0, top], weight.at[pl.ds(2 * inner, half)], rounds + 5),
        fetch(hop_hbm.at[1, bottom], weight.at[pl.ds(side + half, half)], rounds + 6),
    ]

    greet(
        [{"seq": (me + k) % seq_count} for k in range(1, seq_count)]
        + [{"head": p} for p in peers[1:]]
    )
    started = []

    def start(copy):
        copy.start()
        started.append(copy)
        return copy

    travelling = []
    row = math.isqrt(seq_count)

    def reach(k):
        return sum(min(n, row - n) for n in (k % row, k // row))

    for k in sorted(range(1, seq_count), key=reach, reverse=True):
        target = (me + k) % seq_count
        backward = (me + k) // seq_count
        travelling.append(
            start(
                remote(
                    end_ref.at[backward], ends.at[k], seq_send.at[0, k], seq_recv.at[0, k], seq=target
                )
            )
        )
        travelling.append(
            start(remote(total_ref, totals.at[k], seq_send.at[1, k], seq_recv.at[1, k], seq=target))
        )
    def weigh(n, src, row, where, count=half):
        at = weight.at[pl.ds(row, count)]
        return start(remote(src, at, w_send.at[n], w_recv.at[n], head=where))

    u1 = weigh(0, w_hbm.at[bottom], 2 * inner + half, up)
    u2 = weigh(1, w_hbm.at[top], side, down)
    t1 = weigh(2, hop_hbm.at[0, top], far, up)
    t3 = weigh(3, hop_hbm.at[1, bottom], far + half, down)
    beside = [
        weigh(4, hop_hbm.at[0, top], 3 * inner, partner),
        weigh(5, hop_hbm.at[1, bottom], side + inner + half, partner),
    ]

    def cross():
        for copy in (u1, u2, t1, t3):
            copy.wait_recv()
        return [
            weigh(6, weight.at[pl.ds(2 * inner + half, half)], 3 * inner + half, partner),
            weigh(7, weight.at[pl.ds(side, half)], side + inner, partner),
            weigh(8, weight.at[part(4)], 5 * inner, partner, inner),
        ]

    i = lax.broadcasted_iota(jnp.int32, (CHUNK, CHUNK), 0)
    j = lax.broadcasted_iota(jnp.int32, (CHUNK, CHUNK), 1)
    lower = i >= j
    upper = i <= j
    low = j < HEAD_DIM
    skip = head_lanes([jnp.full((1, 1), skip_ref[h], f32) for h in range(4)])
    sub = lax.broadcasted_iota(jnp.int32, (8, CHUNK), 0)
    line = lax.broadcasted_iota(jnp.int32, pick.shape[1:], 0)
    block = lax.broadcasted_iota(jnp.int32, pick.shape[1:], 1) // CHUNK
    sign = jnp.where(block < 4, 1.0, -1.0)
    chosen = jnp.where((line < 24) & (line % 8 == block), sign, 0.0).astype(bf16)
    for u in range(pick.shape[0]):
        pick[u] = chosen
    line = lax.broadcasted_iota(jnp.int32, spread.shape, 0)
    lane = lax.broadcasted_iota(jnp.int32, spread.shape, 1)
    wanted = (lane // inner) * 8 + (lane % inner) // HEAD_DIM
    spread[...] = (line % 16 == wanted).astype(f32).astype(bf16)

    def within(q, d, u):
        c = d * rounds + q
        row = row_ref[c]
        lines = jnp.concatenate(split(jnp.where(sub < 4, -row, row), 3), axis=0)
        for n in range(8):
            own = lax.broadcasted_iota(jnp.int32, lines.shape, 0) % 8 == n
            pick[u, 32:56, n * CHUNK : (n + 1) * CHUNK] = jnp.where(own, lines, 0.0).astype(bf16)
        left = jnp.concatenate(
            split(cols_ref[c, 0:8, :], 3)
            + [jnp.zeros((8, CHUNK), f32), jnp.ones((24, CHUNK), f32), jnp.zeros((8, CHUNK), f32)],
            axis=0,
        ).astype(bf16)
        made = mm(left, pick[u], TN)
        pair = []
        for e, keep in ((0, lower), (1, upper)):
            base = e * mixed + inner
            write = conv[q, d, :, base : base + STATE]
            read = conv[q, d, :, base + STATE : base + 2 * STATE]
            pair.append(jnp.where(keep, mm(read, write, NT), 0.0))
        for p in range(2):
            weights = ([], [])
            for h in (2 * p, 2 * p + 1):
                table = jnp.exp2(
                    jnp.where(
                        lower,
                        made[:, h * CHUNK : (h + 1) * CHUNK],
                        made[:, (4 + h) * CHUNK : (5 + h) * CHUNK],
                    )
                )
                for e in range(2):
                    weights[e].append((pair[e] * table).astype(bf16))
            for e in range(2):
                at = e * mixed + p * CHUNK
                x = conv[q, d, :, at : at + CHUNK]
                zero = jnp.zeros_like(x)
                stacked = jnp.concatenate([jnp.where(low, x, zero), jnp.where(low, zero, x)], axis=0)
                made_here = mm(jnp.concatenate(weights[e], axis=1), stacked)
                made_here = made_here + skip[:, p * CHUNK : (p + 1) * CHUNK] * x.astype(f32)
                inside[q, d, :, e * inner + p * CHUNK : e * inner + (p + 1) * CHUNK] = made_here

    def gates(q, n):
        two = wide[q, pl.ds(2 * n, 2)].reshape(2 * CHUNK, wide.shape[3])
        two = mm(normalized(two, norm_gain_ref[...].reshape(1, -1)), gw_ref[...]).astype(bf16)
        for u in range(2):
            gate[q, 2 * n + u] = two[u * CHUNK : (u + 1) * CHUNK]

    for q in range(rounds):
        conv_in[q].wait()
        wide_in[q].wait()

        def step(n, carry, q=q):
            if q < 2:
                gates(q, n)
            for u in range(2):
                within(q, 2 * n + u, u)
            return carry

        lax.fori_loop(0, owners // 2, step, 0)

    for copy in travelling:
        copy.wait_recv()
    incoming[...] = jnp.zeros_like(incoming)
    for k in range(seq_count - 1, 0, -1):

        @pl.when(k <= me)
        def _(k=k):
            incoming[0] = incoming[0] * jnp.exp2(totals[k, 0:1, :]) + ends[k].astype(f32)

    for k in range(1, seq_count):

        @pl.when(k > me)
        def _(k=k):
            incoming[1] = incoming[1] * jnp.exp2(totals[k, 0:1, :]) + ends[k].astype(f32)

    fresh_in.wait()

    def passing(c):
        return jnp.exp2(head_lanes([cols_ref[c, h : h + 1, CHUNK - 1 :] for h in range(4)]))

    def walk(n, carry):
        for e in range(2):
            at = [2 * n, 2 * n + 1] if e == 0 else [chunks - 1 - 2 * n, chunks - 2 - 2 * n]
            factors = [passing(c) for c in at]
            for lanes in (slice(0, inner // 2), slice(inner // 2, inner)):
                state = incoming[e, :, lanes]
                for c, factor in zip(at, factors):
                    entry[e, c, :, lanes] = state.astype(bf16)
                    state = state * factor[:, lanes] + fresh[c, e, :, lanes].astype(f32)
                incoming[e, :, lanes] = state
        return carry

    lax.fori_loop(0, chunks // 2, walk, 0)

    ones = jnp.ones((8, inner), bf16)
    gain = gain_ref[...].reshape(1, -1).astype(f32)
    sixteen = lax.broadcasted_iota(jnp.int32, (2 * owners, CHUNK), 0)

    def carried(q, d, sums):
        c = d * rounds + q
        left = jnp.concatenate(split(cols_ref[c, 8:24, :], 2), axis=0).astype(bf16)
        scale = mm(left, spread[...], TN)
        act = silu(gate[q, d].astype(f32))
        for e in range(2):
            at = e * mixed + inner + STATE
            lanes = slice(e * inner, (e + 1) * inner)
            part_in = mm(conv[q, d, :, at : at + STATE], entry[e, c])
            value = (inside[q, d, :, lanes] + part_in * scale[:, lanes]) * act
            gated[q, d, :, lanes] = value.astype(bf16)
            square = mm(ones, (value * value).astype(bf16), NT)
            square = jnp.concatenate([square] * (2 * owners // 8), axis=0)
            sums = jnp.where(sixteen == 2 * d + e, square, sums)
        return sums

    def combine(q):
        for k in range(1, head_count):
            ss[q][k - 1].wait_recv()
        total = squares[q]
        for k in range(1, head_count):
            total = total + others[q, k]
        total = lax.rsqrt(total * (1.0 / (inner * head_count)) + epsilon)
        scale = jnp.concatenate([total, jnp.zeros((CHUNK - 2 * owners, CHUNK), f32)], axis=0).T
        for d in range(owners):
            both = gated[q, d, :, :inner].astype(f32) * scale[:, 2 * d : 2 * d + 1]
            both = both + gated[q, d, :, inner:].astype(f32) * scale[:, 2 * d + 1 : 2 * d + 2]
            sending[q, d] = (both * gain).astype(bf16)
        arrived[q * CHUNK : (q + 1) * CHUNK, 0:inner] = sending[q, head]
        return [
            start(
                remote(
                    sending.at[q, peers[k]],
                    arrived.at[pl.ds(q * CHUNK, CHUNK), part(k)],
                    send.at[q, k],
                    recv.at[q, k],
                    head=peers[k],
                )
            )
            for k in sorted(range(1, head_count), key=lambda k: -min(slots[k][0], chips - slots[k][0]))
        ]

    ss, pieces = [], []
    for q in range(rounds):
        if q >= 2:

            def later(n, carry, q=q):
                gates(q, n)
                return carry

            lax.fori_loop(0, owners // 2, later, 0)

        def some(n, sums, q=q):
            for u in range(4):
                sums = carried(q, 4 * n + u, sums)
            return sums

        squares[q] = lax.fori_loop(0, owners // 4, some, jnp.zeros((2 * owners, CHUNK), f32))
        ss.append(
            [
                start(
                    remote(
                        squares.at[q], others.at[q, k], ss_send.at[q, k], ss_recv.at[q, k], head=peers[k]
                    )
                )
                for k in range(1, head_count)
            ]
        )
        if q:
            pieces.append(combine(q - 1))
        if q == 0:
            beside += cross()
    pieces.append(combine(rounds - 1))

    for copy in late:
        copy.wait()
    for copy in beside:
        copy.wait_recv()
    width = out_ref.shape[1]
    step_lanes = 256
    early = (rounds - 1) * CHUNK
    for first, count, done in ((0, early, pieces[:-1]), (early, CHUNK, pieces[-1:])):
        for batch in done:
            for copy in batch:
                copy.wait_recv()
        if count:

            def project_out(b, carry, first=first, count=count):
                lanes = pl.ds(pl.multiple_of(b * step_lanes, step_lanes), step_lanes)
                here = pl.ds(first, count)
                of = pl.ds(first // CHUNK, count // CHUNK)
                out_ref[here, lanes] = (
                    mm(arrived[here, :], weight[:, lanes]) + rest[of, :, lanes].reshape(count, step_lanes).astype(f32)
                ).astype(bf16)
                return carry

            lax.fori_loop(0, width // step_lanes, project_out, 0)
    for copy in started:
        copy.wait_send()


def finish(mesh_shape, end, total, cols, row, skip, gain, gw, norm_gain, conv, fresh, hidden, w, hop):
    seq_count, head_count = mesh_shape
    rounds, owners = conv.shape[:2]
    rows = rounds * CHUNK
    inner = gw.shape[1]
    width = hidden.shape[3]
    dma = pltpu.SemaphoreType.DMA
    return pl.pallas_call(
        functools.partial(finish_kernel, seq_count, head_count),
        in_specs=[
            whole(end.shape),
            whole(total.shape),
            whole(cols.shape),
            whole(row.shape),
            SMEM_SPEC,
            whole(gain.shape),
            whole(gw.shape),
            whole(norm_gain.shape),
        ]
        + [ANY_SPEC] * 5,
        out_specs=whole((rows, width)),
        out_shape=jax.ShapeDtypeStruct((rows, width), bf16),
        scratch_shapes=[
            pltpu.VMEM(conv.shape, bf16),
            pltpu.VMEM((rounds, owners, CHUNK, width), bf16),
            pltpu.VMEM((rounds, owners, CHUNK, inner), bf16),
            pltpu.VMEM(fresh.shape, bf16),
            pltpu.VMEM((rounds, CHUNK, width), bf16),
            pltpu.VMEM((head_count * inner, width), bf16),
            pltpu.VMEM((seq_count,) + end.shape[1:], bf16),
            pltpu.VMEM((seq_count,) + total.shape, f32),
            pltpu.VMEM(end.shape, f32),
            pltpu.VMEM((2, rounds * owners) + end.shape[1:], bf16),
            pltpu.VMEM((2, 64, 8 * CHUNK), bf16),
            pltpu.VMEM((32, 2 * inner), bf16),
            pltpu.VMEM((rounds, owners, CHUNK, 2 * inner), f32),
            pltpu.VMEM((rounds, owners, CHUNK, 2 * inner), bf16),
            pltpu.VMEM((rounds, 2 * owners, CHUNK), f32),
            pltpu.VMEM((rounds, head_count, 2 * owners, CHUNK), f32),
            pltpu.VMEM((rounds, head_count, CHUNK, inner), bf16),
            pltpu.VMEM((rows, head_count * inner), bf16),
            dma((2 * rounds + 7,)),
            dma((2, seq_count)),
            dma((2, seq_count)),
            dma((9,)),
            dma((9,)),
            dma((rounds, head_count)),
            dma((rounds, head_count)),
            dma((rounds, head_count)),
            dma((rounds, head_count)),
        ],
        compiler_params=params(collective_id=1, has_side_effects=True),
        name="finish",
    )(end, total, cols, row, skip, gain, gw, norm_gain, conv, fresh, hidden, w, hop)


def local(
    hidden_in,
    norm_gain,
    gate_weight,
    value_weight,
    state_weight,
    step_weight,
    step_bias,
    decay_log,
    skip_gain,
    conv_value,
    conv_state,
    output_gain,
    output_weight,
    piece_lengths,
):
    seq_count, head_count = lax.axis_size("seq"), lax.axis_size("head")
    shape = (seq_count, head_count)
    mix, raw, halo, hop = project(
        shape, hidden_in, norm_gain, value_weight, state_weight, step_weight.T, output_weight
    )
    conv, fresh, cols, row, end, total = states(
        "seq",
        head_count,
        mix,
        halo,
        norm_gain,
        value_weight,
        state_weight,
        raw,
        piece_lengths,
        step_bias,
        decay_log,
        conv_value,
        conv_state,
    )
    return finish(
        shape,
        end,
        total,
        cols,
        row,
        skip_gain,
        output_gain,
        gate_weight,
        norm_gain,
        conv,
        fresh,
        hidden_in.reshape(head_count, -1, CHUNK, hidden_in.shape[1]),
        output_weight,
        hop,
    )


def solution(mesh):
    in_specs = (
        P("seq", None),
        P(),
        P(None, "head"),
        P(None, "head"),
        P(),
        P(None, "head"),
        P("head"),
        P("head"),
        P("head"),
        P(None, "head"),
        P(),
        P("head"),
        P("head", None),
        P(),
    )
    out_specs = P(("seq", "head"), None)
    return jax.shard_map(local, mesh=mesh, in_specs=in_specs, out_specs=out_specs, check_vma=False)
```

```python
import functools
import math

import jax
import jax.numpy as jnp
from jax import lax
from jax.experimental import pallas as pl
from jax.experimental.pallas import tpu as pltpu
from jax.sharding import PartitionSpec as P

HEAD_DIM = 64
STATE = 128
CONV = 4
CHUNK = 128
PIECES = 16
HALO = 16
REACH = 8
RESET = 256.0
LOG2E = math.log2(math.e)

f32 = jnp.float32
bf16 = jnp.bfloat16
epsilon = 1e-05
MESH = pl.DeviceIdType.MESH
NN = (((1,), (0,)), ((), ()))
NT = (((1,), (1,)), ((), ()))
TN = (((0,), (0,)), ((), ()))


def mm(a, b, dims=NN, precision=None):
    return lax.dot_general(a, b, dims, precision=precision, preferred_element_type=f32)


def silu(x):
    half = 0.5 * x
    return half * jnp.tanh(half) + half


def normalized(h, gain):
    wide = h.astype(f32)
    scale = lax.rsqrt(jnp.mean(wide * wide, axis=1, keepdims=True) + epsilon)
    return (wide * scale * gain.astype(f32)).astype(bf16)


def whole(shape):
    zeros = (0,) * len(shape)
    return pl.BlockSpec(shape, lambda *_: zeros)


SMEM_SPEC = pl.BlockSpec(memory_space=pltpu.SMEM)
ANY_SPEC = pl.BlockSpec(memory_space=pl.ANY)


def params(**kw):
    return pltpu.CompilerParams(vmem_limit_bytes=60 * 1024 * 1024, **kw)


def remote(src, dst, send, recv, **where):
    return pltpu.make_async_remote_copy(
        src_ref=src,
        dst_ref=dst,
        send_sem=send,
        recv_sem=recv,
        device_id=where,
        device_id_type=MESH,
    )


def greet(axes_and_peers):
    barrier = pltpu.get_barrier_semaphore()
    for where in axes_and_peers:
        pl.semaphore_signal(barrier, inc=1, device_id=where, device_id_type=MESH)
    pl.semaphore_wait(barrier, len(axes_and_peers))


def head_peer(me, chips, dy, dc):
    y, core = me // 2, me % 2
    return ((y + dy) % chips) * 2 + (core + dc) % 2


def project_copies(seq_count, head_count, hidden, w, halo, hop, send, recv):
    me = lax.axis_index("seq")
    head = lax.axis_index("head")
    chips = head_count // 2
    tokens = hidden.shape[0]
    after = (me + 1) % seq_count
    before = (me + seq_count - 1) % seq_count
    first, last = pl.ds(0, HALO), pl.ds(tokens - HALO, HALO)
    low, high = pl.ds(0, HALO), pl.ds(HALO, HALO)
    half = w.shape[0] // 2
    top, bottom = pl.ds(0, half), pl.ds(half, half)
    up = head_peer(head, chips, 1, 0)
    down = head_peer(head, chips, chips - 1, 0)
    partner = head_peer(head, chips, 0, 1)
    return (
        remote(hidden.at[last], halo.at[low], send.at[0], recv.at[0], seq=after),
        remote(hidden.at[first], halo.at[high], send.at[1], recv.at[1], seq=before),
        remote(w.at[top], hop.at[0, top], send.at[2], recv.at[2], head=up),
        remote(w.at[bottom], hop.at[1, bottom], send.at[3], recv.at[3], head=down),
        remote(w, hop.at[2], send.at[4], recv.at[4], head=partner),
    ), [{"seq": after}, {"seq": before}, {"head": up}, {"head": down}, {"head": partner}]


def project_kernel(
    mesh_shape,
    h_ref,
    gain_ref,
    vw_ref,
    sw_ref,
    tw_ref,
    hidden,
    w,
    mix_ref,
    raw_ref,
    halo,
    hop,
    turned,
    rows,
    send,
    recv,
):
    i = pl.program_id(0)
    copies, peers = project_copies(*mesh_shape, hidden, w, halo, hop, send, recv)
    barrier = pltpu.get_barrier_semaphore()

    @pl.when(i == 0)
    def _():
        for where in peers:
            pl.semaphore_signal(barrier, inc=1, device_id=where, device_id_type=MESH)
        narrow = tw_ref[...].astype(f32)
        turned[...] = jnp.concatenate([narrow, narrow], axis=0).astype(bf16)

    @pl.when(i == 1)
    def _():
        pl.semaphore_wait(barrier, len(peers))
        for copy in copies:
            copy.start()

    inner = vw_ref.shape[1]
    gain = gain_ref[...].reshape(1, -1)
    deep = min(256, h_ref.shape[0])
    for first in range(0, h_ref.shape[0], deep):
        for r in range(first, first + deep, 32):
            rows[r : r + 32, :] = normalized(h_ref[r : r + 32, :], gain)
        at = slice(first, first + deep)
        n = rows[at, :]
        mix_ref[at, :inner] = mm(n, vw_ref[...]).astype(bf16)
        mix_ref[at, inner:] = mm(n, sw_ref[...]).astype(bf16)
        raw = mm(turned[...], n, NT)
        for q in range(deep // CHUNK):
            raw_ref[first // CHUNK + q] = raw[:, q * CHUNK : (q + 1) * CHUNK]

    @pl.when(i == pl.num_programs(0) - 1)
    def _():
        for copy in copies:
            copy.wait()


def project(mesh_shape, hidden, gain, vw, sw, tw, w):
    tokens, width = hidden.shape
    inner = vw.shape[1]
    mixed = inner + sw.shape[1]
    rows = tokens // mesh_shape[1]
    return pl.pallas_call(
        functools.partial(project_kernel, mesh_shape),
        grid=(tokens // rows,),
        in_specs=[
            pl.BlockSpec((rows, width), lambda i: (i, 0)),
            whole(gain.shape),
            whole(vw.shape),
            whole(sw.shape),
            whole(tw.shape),
            ANY_SPEC,
            ANY_SPEC,
        ],
        out_specs=[
            pl.BlockSpec((rows, mixed), lambda i: (i, 0)),
            pl.BlockSpec((rows // CHUNK, 8, CHUNK), lambda i: (i, 0, 0)),
            ANY_SPEC,
            ANY_SPEC,
        ],
        out_shape=[
            jax.ShapeDtypeStruct((tokens, mixed), bf16),
            jax.ShapeDtypeStruct((tokens // CHUNK, 8, CHUNK), f32),
            jax.ShapeDtypeStruct((2 * HALO, width), bf16),
            jax.ShapeDtypeStruct((3,) + w.shape, bf16),
        ],
        scratch_shapes=[
            pltpu.VMEM((8, width), bf16),
            pltpu.VMEM((rows, width), bf16),
            pltpu.SemaphoreType.DMA((5,)),
            pltpu.SemaphoreType.DMA((5,)),
        ],
        compiler_params=params(collective_id=2, has_side_effects=True),
        name="project",
    )(hidden, gain, vw, sw, tw, hidden, w)


def head_lanes(columns):
    low = lax.broadcasted_iota(jnp.int32, (columns[0].shape[0], 2 * HEAD_DIM), 1) < HEAD_DIM
    pairs = [
        jnp.where(low, columns[2 * p], columns[2 * p + 1]) for p in range(len(columns) // 2)
    ]
    return jnp.concatenate(pairs, axis=1)


def decays(first_row, raw, lens_ref, bias_ref, rate_ref):
    chunks = raw.shape[0]
    shape = (chunks, 8, CHUNK)
    sub = lax.broadcasted_iota(jnp.int32, shape, 1)
    upper = sub < 4
    head = jnp.where(upper, sub, sub - 4)
    pos = (
        first_row
        + lax.broadcasted_iota(jnp.int32, shape, 0) * CHUNK
        + lax.broadcasted_iota(jnp.int32, shape, 2)
    )
    start = jnp.zeros(shape, jnp.int32)
    stop = jnp.full(shape, 1 << 30, jnp.int32)
    edge = jnp.int32(0)
    for k in range(PIECES):
        start = jnp.where(pos >= edge, edge, start)
        edge = edge + lens_ref[k]
        stop = jnp.minimum(stop, jnp.where(edge > pos, edge, 1 << 30))
    since = pos - start
    until = stop - 1 - pos
    bias = jnp.zeros(shape, f32)
    rate = jnp.zeros(shape, f32)
    for h in range(4):
        bias = jnp.where(head == h, bias_ref[h], bias)
        rate = jnp.where(head == h, rate_ref[h], rate)
    rate = jnp.exp(rate) * (-LOG2E)
    z = raw + bias
    step = jnp.maximum(z, 0.0) + jnp.log1p(jnp.exp(-jnp.abs(z)))
    log = step * rate
    reset = jnp.where(since == 0, -RESET, 0.0)
    ones = (
        lax.broadcasted_iota(jnp.int32, (CHUNK, CHUNK), 0)
        <= lax.broadcasted_iota(jnp.int32, (CHUNK, CHUNK), 1)
    ).astype(f32)
    cum = mm(
        (log + reset).reshape(chunks * 8, CHUNK), ones, precision=lax.Precision.HIGHEST
    ).reshape(shape)
    excl = cum - log
    total = cum[:, :, CHUNK - 1 :]
    log_step = jnp.where(step > 0.0, jnp.log2(step), -RESET)
    row = jnp.where(upper, cum - log_step, excl + log_step)
    g1 = jnp.where(upper, cum, excl)
    g2 = jnp.where(upper, jnp.exp2(cum), jnp.exp2(total - cum) * step)
    g3 = jnp.where(upper, jnp.exp2(total - excl), jnp.exp2(excl) * step)
    g4 = jnp.where(upper, since, until).astype(f32)
    return row, g1, g2, g3, g4


def states_kernel(
    axis,
    mix_ref,
    before_ref,
    after_ref,
    halo_ref,
    gain_ref,
    vw_ref,
    sw_ref,
    raw_ref,
    lens_ref,
    bias_ref,
    rate_ref,
    cv_ref,
    cs_ref,
    conv_ref,
    fresh_ref,
    cols_ref,
    row_ref,
    end_ref,
    total_ref,
    prod,
    halo,
    run,
    reach,
    spread,
    near,
):
    g = pl.program_id(0)
    groups = pl.num_programs(0)
    inner = vw_ref.shape[1]
    rows, mixed = mix_ref.shape
    rounds = rows // CHUNK
    blocks = mixed // 128
    first_row = lax.axis_index(axis) * (groups * rows)

    @pl.when(g == 0)
    def _():
        n = normalized(halo_ref[...], gain_ref[...].reshape(1, -1))
        halo[:, :inner] = mm(n, vw_ref[...]).astype(bf16).astype(f32)
        halo[:, inner:] = mm(n, sw_ref[...]).astype(bf16).astype(f32)
        row, g1, g2, g3, g4 = decays(first_row, raw_ref[...], lens_ref, bias_ref, rate_ref)
        row_ref[...] = row
        cols_ref[:, 0:8, :] = g1
        cols_ref[:, 8:16, :] = g2
        cols_ref[:, 16:24, :] = g3
        cols_ref[:, 24:32, :] = g4
        run[...] = jnp.zeros_like(run)
        reach[...] = jnp.zeros_like(reach)
        line = lax.broadcasted_iota(jnp.int32, spread.shape, 0) % 32
        lane = lax.broadcasted_iota(jnp.int32, spread.shape, 1)
        wanted = 12 + (lane // inner) * 8 + (lane % inner) // HEAD_DIM
        spread[...] = (line == wanted).astype(f32).astype(bf16)

        def clear(k, carry):
            near[k] = 0
            return carry

        lax.fori_loop(0, near.shape[0], clear, 0)

        def mark(k, edge):
            for shift in (-(CONV - 1), CONV - 2):
                at = (edge + shift - first_row + rows) // rows
                near[jnp.clip(at, 0, near.shape[0] - 1)] = 1
            return edge + lens_ref[jnp.minimum(k, PIECES - 1)]

        lax.fori_loop(0, PIECES + 1, mark, jnp.int32(0))

    taps = jnp.concatenate([cv_ref[...], cs_ref[...]], axis=1).astype(f32) * 0.5

    def put(b, at, values):
        lanes = slice(b * 128, (b + 1) * 128)
        for k in range(CONV - 1):
            prod[k, b, at : at + values.shape[0], :] = values * taps[k : k + 1, lanes]

    def ready(q):
        for b in range(blocks):
            lanes = slice(b * 128, (b + 1) * 128)
            put(b, REACH + q * CHUNK, mix_ref[q * CHUNK : (q + 1) * CHUNK, lanes].astype(f32))

    def group(masked):
        for b in range(blocks):
            lanes = slice(b * 128, (b + 1) * 128)
            ahead = before_ref[:, lanes].astype(f32)[16 - REACH :, :]
            put(b, 0, jnp.where(g == 0, halo[HALO - REACH : HALO, lanes], ahead))
            behind = after_ref[:, lanes].astype(f32)[:REACH, :]
            put(b, REACH + rows, jnp.where(g == groups - 1, halo[HALO : HALO + REACH, lanes], behind))
        ready(0)
        for q in range(rounds):
            if q + 1 < rounds:
                ready(q + 1)
            chunk(q, masked)

    def chunk(q, masked):
        cols = cols_ref[g * rounds + q]
        high = cols.astype(bf16).astype(f32)
        both = jnp.concatenate([high, cols - high], axis=0).astype(bf16)
        tails = mm(both, spread[...], TN)
        passing = head_lanes([cols[h : h + 1, CHUNK - 1 :] for h in range(4)])
        if masked:
            turned = jnp.concatenate([cols, jnp.zeros((CHUNK - 32, CHUNK), f32)], axis=0).T
            sides = [jnp.broadcast_to(turned[:, r : r + 1], (CHUNK, 128)) for r in (24, 28)]
        write = [None, None]
        for b in [inner // 128] + list(range(inner // 128)) + list(range(inner // 128 + 1, blocks)):
            lanes = slice(b * 128, (b + 1) * 128)
            centre = mix_ref[q * CHUNK : (q + 1) * CHUNK, lanes].astype(f32) * taps[CONV - 1 : CONV, lanes]
            for d in range(2):
                half = centre
                for distance in range(1, CONV):
                    at = REACH + q * CHUNK + (distance if d else -distance)
                    term = prod[CONV - 1 - distance, b, at : at + CHUNK, :]
                    if masked:
                        term = jnp.where(sides[d] >= distance, term, 0.0)
                    half = half + term
                value = half * jnp.tanh(half) + half
                at = d * mixed + b * 128
                narrow = value.astype(bf16)
                conv_ref[q, 0, :, at : at + 128] = narrow
                if b == inner // 128:
                    write[d] = narrow
                elif b < inner // 128:
                    at = d * inner + b * 128
                    scaled = (value * tails[:, at : at + 128]).astype(bf16)
                    fresh = mm(write[d], scaled, TN)
                    fresh_ref[q, d, :, lanes] = fresh.astype(bf16)
                    if d == 0:
                        run[0, :, lanes] = run[0, :, lanes] * jnp.exp2(passing[:, lanes]) + fresh
                    else:
                        run[1, :, lanes] = run[1, :, lanes] + jnp.exp2(reach[0:1, lanes]) * fresh
        reach[...] = reach[...] + passing

    edges = near[g + 1]

    @pl.when(edges == 0)
    def _():
        group(False)

    @pl.when(edges != 0)
    def _():
        group(True)

    @pl.when(g == groups - 1)
    def _():
        end_ref[...] = run[...].astype(bf16)
        total_ref[...] = reach[...]


def states(axis, owners, mix, halo, gain, vw, sw, raw, lens, bias, rate, cv, cs):
    tokens, mixed = mix.shape
    chunks = tokens // CHUNK
    inner = vw.shape[1]
    rounds = chunks // owners
    rows = rounds * CHUNK
    per = rows // 16
    last = tokens // 16 - 1
    return pl.pallas_call(
        functools.partial(states_kernel, axis),
        grid=(owners,),
        in_specs=[
            pl.BlockSpec((rows, mixed), lambda c: (c, 0)),
            pl.BlockSpec((16, mixed), lambda c: (jnp.maximum(c * per - 1, 0), 0)),
            pl.BlockSpec((16, mixed), lambda c: (jnp.minimum(c * per + per, last), 0)),
            whole(halo.shape),
            whole(gain.shape),
            whole(vw.shape),
            whole(sw.shape),
            whole(raw.shape),
            SMEM_SPEC,
            SMEM_SPEC,
            SMEM_SPEC,
            whole(cv.shape),
            whole(cs.shape),
        ],
        out_specs=[
            pl.BlockSpec((rounds, 1, CHUNK, 2 * mixed), lambda c: (0, c, 0, 0)),
            pl.BlockSpec((rounds, 2, STATE, inner), lambda c: (c, 0, 0, 0)),
            whole((chunks, 32, CHUNK)),
            whole((chunks, 8, CHUNK)),
            whole((2, STATE, inner)),
            whole((8, inner)),
        ],
        out_shape=[
            jax.ShapeDtypeStruct((rounds, owners, CHUNK, 2 * mixed), bf16),
            jax.ShapeDtypeStruct((chunks, 2, STATE, inner), bf16),
            jax.ShapeDtypeStruct((chunks, 32, CHUNK), f32),
            jax.ShapeDtypeStruct((chunks, 8, CHUNK), f32),
            jax.ShapeDtypeStruct((2, STATE, inner), bf16),
            jax.ShapeDtypeStruct((8, inner), f32),
        ],
        scratch_shapes=[
            pltpu.VMEM((CONV - 1, mixed // 128, rows + 2 * REACH, 128), f32),
            pltpu.VMEM((2 * HALO, mixed), f32),
            pltpu.VMEM((2, STATE, inner), f32),
            pltpu.VMEM((8, inner), f32),
            pltpu.VMEM((64, 2 * inner), bf16),
            pltpu.SMEM((owners + 2,), jnp.int32),
        ],
        compiler_params=params(),
        name="states",
    )(mix, mix, mix, halo, gain, vw, sw, raw, lens, bias, rate, cv, cs)


def split(x, parts):
    pieces = []
    for _ in range(parts - 1):
        pieces.append(x.astype(bf16).astype(f32))
        x = x - pieces[-1]
    return pieces + [x]


def finish_kernel(
    seq_count,
    head_count,
    end_ref,
    total_ref,
    cols_ref,
    row_ref,
    skip_ref,
    gain_ref,
    gw_ref,
    norm_gain_ref,
    conv_hbm,
    fresh_hbm,
    hidden_hbm,
    w_hbm,
    hop_hbm,
    out_ref,
    conv,
    wide,
    gate,
    fresh,
    rest,
    weight,
    ends,
    totals,
    incoming,
    entry,
    pick,
    spread,
    inside,
    gated,
    squares,
    others,
    sending,
    arrived,
    load,
    seq_send,
    seq_recv,
    w_send,
    w_recv,
    ss_send,
    ss_recv,
    send,
    recv,
):
    me = lax.axis_index("seq")
    head = lax.axis_index("head")
    chips = head_count // 2
    rounds, owners = conv.shape[0], conv.shape[1]
    chunks = rounds * owners
    inner = gate.shape[3]
    mixed = conv.shape[3] // 2
    rows = rounds * CHUNK
    slots = [(dy, dc) for dy in range(chips) for dc in range(2)]
    peers = [head_peer(head, chips, dy, dc) for dy, dc in slots]
    up, down, partner = peers[2], peers[2 * chips - 2], peers[1]

    def fetch(src, dst, n):
        copy = pltpu.make_async_copy(src, dst, load.at[n])
        copy.start()
        return copy

    def part(k):
        return pl.ds(k * inner, inner)

    conv_in, wide_in = [], []
    for q in range(rounds):
        conv_in.append(fetch(conv_hbm.at[q], conv.at[q], q))
        wide_in.append(fetch(hidden_hbm.at[:, q], wide.at[q], rounds + 7 + q))
    fresh_in = fetch(fresh_hbm, fresh, rounds)
    half = inner // 2
    side = (2 * chips - 2) * inner
    far = 4 * inner
    top, bottom = pl.ds(0, half), pl.ds(half, half)
    late = [
        fetch(hidden_hbm.at[head], rest, rounds + 2),
        fetch(w_hbm, weight.at[part(0)], rounds + 3),
        fetch(hop_hbm.at[2], weight.at[part(1)], rounds + 4),
        fetch(hop_hbm.at[0, top], weight.at[pl.ds(2 * inner, half)], rounds + 5),
        fetch(hop_hbm.at[1, bottom], weight.at[pl.ds(side + half, half)], rounds + 6),
    ]

    greet(
        [{"seq": (me + k) % seq_count} for k in range(1, seq_count)]
        + [{"head": p} for p in peers[1:]]
    )
    started = []

    def start(copy):
        copy.start()
        started.append(copy)
        return copy

    travelling = []
    for k in range(1, seq_count):
        target = (me + k) % seq_count
        backward = (me + k) // seq_count
        travelling.append(
            start(
                remote(
                    end_ref.at[backward], ends.at[k], seq_send.at[0, k], seq_recv.at[0, k], seq=target
                )
            )
        )
        travelling.append(
            start(remote(total_ref, totals.at[k], seq_send.at[1, k], seq_recv.at[1, k], seq=target))
        )
    def weigh(n, src, row, where, count=half):
        at = weight.at[pl.ds(row, count)]
        return start(remote(src, at, w_send.at[n], w_recv.at[n], head=where))

    u1 = weigh(0, w_hbm.at[bottom], 2 * inner + half, up)
    u2 = weigh(1, w_hbm.at[top], side, down)
    t1 = weigh(2, hop_hbm.at[0, top], far, up)
    t3 = weigh(3, hop_hbm.at[1, bottom], far + half, down)
    beside = [
        weigh(4, hop_hbm.at[0, top], 3 * inner, partner),
        weigh(5, hop_hbm.at[1, bottom], side + inner + half, partner),
    ]

    def cross():
        for copy in (u1, u2, t1, t3):
            copy.wait_recv()
        return [
            weigh(6, weight.at[pl.ds(2 * inner + half, half)], 3 * inner + half, partner),
            weigh(7, weight.at[pl.ds(side, half)], side + inner, partner),
            weigh(8, weight.at[part(4)], 5 * inner, partner, inner),
        ]

    i = lax.broadcasted_iota(jnp.int32, (CHUNK, CHUNK), 0)
    j = lax.broadcasted_iota(jnp.int32, (CHUNK, CHUNK), 1)
    lower = i >= j
    upper = i <= j
    low = j < HEAD_DIM
    skip = head_lanes([jnp.full((1, 1), skip_ref[h], f32) for h in range(4)])
    sub = lax.broadcasted_iota(jnp.int32, (8, CHUNK), 0)
    line = lax.broadcasted_iota(jnp.int32, pick.shape[1:], 0)
    block = lax.broadcasted_iota(jnp.int32, pick.shape[1:], 1) // CHUNK
    sign = jnp.where(block < 4, 1.0, -1.0)
    chosen = jnp.where((line < 24) & (line % 8 == block), sign, 0.0).astype(bf16)
    for u in range(pick.shape[0]):
        pick[u] = chosen
    line = lax.broadcasted_iota(jnp.int32, spread.shape, 0)
    lane = lax.broadcasted_iota(jnp.int32, spread.shape, 1)
    wanted = (lane // inner) * 8 + (lane % inner) // HEAD_DIM
    spread[...] = (line % 16 == wanted).astype(f32).astype(bf16)

    def within(q, d, u):
        c = d * rounds + q
        row = row_ref[c]
        lines = jnp.concatenate(split(jnp.where(sub < 4, -row, row), 3), axis=0)
        for n in range(8):
            own = lax.broadcasted_iota(jnp.int32, lines.shape, 0) % 8 == n
            pick[u, 32:56, n * CHUNK : (n + 1) * CHUNK] = jnp.where(own, lines, 0.0).astype(bf16)
        left = jnp.concatenate(
            split(cols_ref[c, 0:8, :], 3)
            + [jnp.zeros((8, CHUNK), f32), jnp.ones((24, CHUNK), f32), jnp.zeros((8, CHUNK), f32)],
            axis=0,
        ).astype(bf16)
        made = mm(left, pick[u], TN)
        pair = []
        for e, keep in ((0, lower), (1, upper)):
            base = e * mixed + inner
            write = conv[q, d, :, base : base + STATE]
            read = conv[q, d, :, base + STATE : base + 2 * STATE]
            pair.append(jnp.where(keep, mm(read, write, NT), 0.0))
        for p in range(2):
            weights = ([], [])
            for h in (2 * p, 2 * p + 1):
                table = jnp.exp2(
                    jnp.where(
                        lower,
                        made[:, h * CHUNK : (h + 1) * CHUNK],
                        made[:, (4 + h) * CHUNK : (5 + h) * CHUNK],
                    )
                )
                for e in range(2):
                    weights[e].append((pair[e] * table).astype(bf16))
            for e in range(2):
                at = e * mixed + p * CHUNK
                x = conv[q, d, :, at : at + CHUNK]
                zero = jnp.zeros_like(x)
                stacked = jnp.concatenate([jnp.where(low, x, zero), jnp.where(low, zero, x)], axis=0)
                made_here = mm(jnp.concatenate(weights[e], axis=1), stacked)
                made_here = made_here + skip[:, p * CHUNK : (p + 1) * CHUNK] * x.astype(f32)
                inside[q, d, :, e * inner + p * CHUNK : e * inner + (p + 1) * CHUNK] = made_here

    def gates(q, n):
        two = wide[q, pl.ds(2 * n, 2)].reshape(2 * CHUNK, wide.shape[3])
        two = mm(normalized(two, norm_gain_ref[...].reshape(1, -1)), gw_ref[...]).astype(bf16)
        for u in range(2):
            gate[q, 2 * n + u] = two[u * CHUNK : (u + 1) * CHUNK]

    for q in range(rounds):
        conv_in[q].wait()
        wide_in[q].wait()

        def step(n, carry, q=q):
            if q < 1:
                gates(q, n)
            for u in range(2):
                within(q, 2 * n + u, u)
            return carry

        lax.fori_loop(0, owners // 2, step, 0)

    for copy in travelling:
        copy.wait_recv()
    incoming[...] = jnp.zeros_like(incoming)
    for k in range(seq_count - 1, 0, -1):

        @pl.when(k <= me)
        def _(k=k):
            incoming[0] = incoming[0] * jnp.exp2(totals[k, 0:1, :]) + ends[k].astype(f32)

    for k in range(1, seq_count):

        @pl.when(k > me)
        def _(k=k):
            incoming[1] = incoming[1] * jnp.exp2(totals[k, 0:1, :]) + ends[k].astype(f32)

    fresh_in.wait()

    def passing(c):
        return jnp.exp2(head_lanes([cols_ref[c, h : h + 1, CHUNK - 1 :] for h in range(4)]))

    def walk(n, carry):
        for e in range(2):
            at = [2 * n, 2 * n + 1] if e == 0 else [chunks - 1 - 2 * n, chunks - 2 - 2 * n]
            factors = [passing(c) for c in at]
            for lanes in (slice(0, inner // 2), slice(inner // 2, inner)):
                state = incoming[e, :, lanes]
                for c, factor in zip(at, factors):
                    entry[e, c, :, lanes] = state.astype(bf16)
                    state = state * factor[:, lanes] + fresh[c, e, :, lanes].astype(f32)
                incoming[e, :, lanes] = state
        return carry

    lax.fori_loop(0, chunks // 2, walk, 0)

    ones = jnp.ones((8, inner), bf16)
    gain = gain_ref[...].reshape(1, -1).astype(f32)
    sixteen = lax.broadcasted_iota(jnp.int32, (2 * owners, CHUNK), 0)

    def carried(q, d, sums):
        c = d * rounds + q
        left = jnp.concatenate(split(cols_ref[c, 8:24, :], 2), axis=0).astype(bf16)
        scale = mm(left, spread[...], TN)
        act = silu(gate[q, d].astype(f32))
        for e in range(2):
            at = e * mixed + inner + STATE
            lanes = slice(e * inner, (e + 1) * inner)
            part_in = mm(conv[q, d, :, at : at + STATE], entry[e, c])
            value = (inside[q, d, :, lanes] + part_in * scale[:, lanes]) * act
            gated[q, d, :, lanes] = value.astype(bf16)
            square = mm(ones, (value * value).astype(bf16), NT)
            square = jnp.concatenate([square] * (2 * owners // 8), axis=0)
            sums = jnp.where(sixteen == 2 * d + e, square, sums)
        return sums

    def combine(q):
        for k in range(1, head_count):
            ss[q][k - 1].wait_recv()
        total = squares[q]
        for k in range(1, head_count):
            total = total + others[q, k]
        total = lax.rsqrt(total * (1.0 / (inner * head_count)) + epsilon)
        scale = jnp.concatenate([total, jnp.zeros((CHUNK - 2 * owners, CHUNK), f32)], axis=0).T
        for d in range(owners):
            both = gated[q, d, :, :inner].astype(f32) * scale[:, 2 * d : 2 * d + 1]
            both = both + gated[q, d, :, inner:].astype(f32) * scale[:, 2 * d + 1 : 2 * d + 2]
            sending[q, d] = (both * gain).astype(bf16)
        arrived[q * CHUNK : (q + 1) * CHUNK, 0:inner] = sending[q, head]
        return [
            start(
                remote(
                    sending.at[q, peers[k]],
                    arrived.at[pl.ds(q * CHUNK, CHUNK), part(k)],
                    send.at[q, k],
                    recv.at[q, k],
                    head=peers[k],
                )
            )
            for k in sorted(range(1, head_count), key=lambda k: -min(slots[k][0], chips - slots[k][0]))
        ]

    ss, pieces = [], []
    for q in range(rounds):
        if q >= 1:

            def later(n, carry, q=q):
                gates(q, n)
                return carry

            lax.fori_loop(0, owners // 2, later, 0)

        def some(n, sums, q=q):
            for u in range(4):
                sums = carried(q, 4 * n + u, sums)
            return sums

        squares[q] = lax.fori_loop(0, owners // 4, some, jnp.zeros((2 * owners, CHUNK), f32))
        ss.append(
            [
                start(
                    remote(
                        squares.at[q], others.at[q, k], ss_send.at[q, k], ss_recv.at[q, k], head=peers[k]
                    )
                )
                for k in range(1, head_count)
            ]
        )
        if q:
            pieces.append(combine(q - 1))
        if q == 0:
            beside += cross()
    pieces.append(combine(rounds - 1))

    for copy in late:
        copy.wait()
    for copy in beside:
        copy.wait_recv()
    width = out_ref.shape[1]
    step_lanes = 256
    early = (rounds - 1) * CHUNK
    for first, count, done in ((0, early, pieces[:-1]), (early, CHUNK, pieces[-1:])):
        for batch in done:
            for copy in batch:
                copy.wait_recv()
        if count:

            def project_out(b, carry, first=first, count=count):
                lanes = pl.ds(pl.multiple_of(b * step_lanes, step_lanes), step_lanes)
                here = pl.ds(first, count)
                of = pl.ds(first // CHUNK, count // CHUNK)
                out_ref[here, lanes] = (
                    mm(arrived[here, :], weight[:, lanes]) + rest[of, :, lanes].reshape(count, step_lanes).astype(f32)
                ).astype(bf16)
                return carry

            lax.fori_loop(0, width // step_lanes, project_out, 0)
    for copy in started:
        copy.wait_send()


def finish(mesh_shape, end, total, cols, row, skip, gain, gw, norm_gain, conv, fresh, hidden, w, hop):
    seq_count, head_count = mesh_shape
    rounds, owners = conv.shape[:2]
    rows = rounds * CHUNK
    inner = gw.shape[1]
    width = hidden.shape[3]
    dma = pltpu.SemaphoreType.DMA
    return pl.pallas_call(
        functools.partial(finish_kernel, seq_count, head_count),
        in_specs=[
            whole(end.shape),
            whole(total.shape),
            whole(cols.shape),
            whole(row.shape),
            SMEM_SPEC,
            whole(gain.shape),
            whole(gw.shape),
            whole(norm_gain.shape),
        ]
        + [ANY_SPEC] * 5,
        out_specs=whole((rows, width)),
        out_shape=jax.ShapeDtypeStruct((rows, width), bf16),
        scratch_shapes=[
            pltpu.VMEM(conv.shape, bf16),
            pltpu.VMEM((rounds, owners, CHUNK, width), bf16),
            pltpu.VMEM((rounds, owners, CHUNK, inner), bf16),
            pltpu.VMEM(fresh.shape, bf16),
            pltpu.VMEM((rounds, CHUNK, width), bf16),
            pltpu.VMEM((head_count * inner, width), bf16),
            pltpu.VMEM((seq_count,) + end.shape[1:], bf16),
            pltpu.VMEM((seq_count,) + total.shape, f32),
            pltpu.VMEM(end.shape, f32),
            pltpu.VMEM((2, rounds * owners) + end.shape[1:], bf16),
            pltpu.VMEM((2, 64, 8 * CHUNK), bf16),
            pltpu.VMEM((32, 2 * inner), bf16),
            pltpu.VMEM((rounds, owners, CHUNK, 2 * inner), f32),
            pltpu.VMEM((rounds, owners, CHUNK, 2 * inner), bf16),
            pltpu.VMEM((rounds, 2 * owners, CHUNK), f32),
            pltpu.VMEM((rounds, head_count, 2 * owners, CHUNK), f32),
            pltpu.VMEM((rounds, head_count, CHUNK, inner), bf16),
            pltpu.VMEM((rows, head_count * inner), bf16),
            dma((2 * rounds + 7,)),
            dma((2, seq_count)),
            dma((2, seq_count)),
            dma((9,)),
            dma((9,)),
            dma((rounds, head_count)),
            dma((rounds, head_count)),
            dma((rounds, head_count)),
            dma((rounds, head_count)),
        ],
        compiler_params=params(collective_id=1, has_side_effects=True),
        name="finish",
    )(end, total, cols, row, skip, gain, gw, norm_gain, conv, fresh, hidden, w, hop)


def local(
    hidden_in,
    norm_gain,
    gate_weight,
    value_weight,
    state_weight,
    step_weight,
    step_bias,
    decay_log,
    skip_gain,
    conv_value,
    conv_state,
    output_gain,
    output_weight,
    piece_lengths,
):
    seq_count, head_count = lax.axis_size("seq"), lax.axis_size("head")
    shape = (seq_count, head_count)
    mix, raw, halo, hop = project(
        shape, hidden_in, norm_gain, value_weight, state_weight, step_weight.T, output_weight
    )
    conv, fresh, cols, row, end, total = states(
        "seq",
        head_count,
        mix,
        halo,
        norm_gain,
        value_weight,
        state_weight,
        raw,
        piece_lengths,
        step_bias,
        decay_log,
        conv_value,
        conv_state,
    )
    return finish(
        shape,
        end,
        total,
        cols,
        row,
        skip_gain,
        output_gain,
        gate_weight,
        norm_gain,
        conv,
        fresh,
        hidden_in.reshape(head_count, -1, CHUNK, hidden_in.shape[1]),
        output_weight,
        hop,
    )


def solution(mesh):
    in_specs = (
        P("seq", None),
        P(),
        P(None, "head"),
        P(None, "head"),
        P(),
        P(None, "head"),
        P("head"),
        P("head"),
        P("head"),
        P(None, "head"),
        P(),
        P("head"),
        P("head", None),
        P(),
    )
    out_specs = P(("seq", "head"), None)
    return jax.shard_map(local, mesh=mesh, in_specs=in_specs, out_specs=out_specs, check_vma=False)
```
